256 devices in a mesh: segment: 2 (over core), rows: 32 (over z, x), dp: 4 (over y).
Axes of the slice: x: 4, y: 4, z: 8, core: 2. Of those that a mesh axis runs over, the one named last changes fastest.
Arguments:
- coarse: bfloat16 [8, 100, 384, 256], P(('segment', 'dp'), None, 'rows'), may hold values from -6 to 6
- target: bfloat16 [8, 64, 384, 256], P(('segment', 'dp'), None, 'rows'), may hold values from -6 to 6
- noise: bfloat16 [8, 32, 64, 64, 144], P(('segment', 'dp'), 'rows'), may hold values from -6 to 6
- regions: int32 [8, 32, 32, 4], P(('segment', 'dp')), may hold values from 0 to 244, as said below
- reg_conv: bfloat16 [128, 900], replicated, may hold values from -0.1875 to 0.1875
- reg_out: bfloat16 [64, 128], replicated, may hold values from -0.5 to 0.5
- conv_one: bfloat16 [128, 1152], replicated, may hold values from -0.1875 to 0.1875
- conv_two: bfloat16 [128, 1152], replicated, may hold values from -0.1875 to 0.1875
- out_proj: bfloat16 [64, 128], replicated, may hold values from -0.5 to 0.5
- step_embed: float32 [32, 128], replicated, may hold values from -3 to 3
Outputs:
- mean_field: bfloat16 [8, 64, 384, 256], P(('segment', 'dp'), None, 'rows')
- owner_loss: float32 [8, 32], P(('segment', 'dp'), 'rows')
- grad_conv_one: float32 [128, 1152], replicated
- grad_conv_two: float32 [128, 1152], replicated
- grad_out_proj: float32 [64, 128], replicated
- grad_embed: float32 [32, 128], replicated
The draws below stay inside these ranges and needn't reach their ends.
Inputs may be any that keep to these rules, and one draw needn't show every extreme that they name: `regions`: for sample s, strip i and entry k: entry 0 is the patch's row offset within strip i (0 on the last strip), entry 1 its first column, at most 244, entry 2 its owner, entry 3 its noise level below 32. Every owner receives 2 * 32, 32 or 16 patches of a sample; for each owner with 64 there is one with 32 and two with 16. No strip lists more than 2 patches for one owner, and some strip lists exactly 2 for one owner.
All inputs are finite; a program needn't handle non-finite values.
Results may differ from the reference program's by a relative error of at most 0.0048.
Values may be sent and summed in bfloat16 or wider, within the bound.
A program may use at most 192 MiB of HBM per device.

```python
import math
import jax
import jax.numpy as jnp
from jax import lax

CIN = 100
CT = 64
REG = 128
DC = 128
NT = 32
PATCH = 12
KS = 32
W = 256
NS = 8
H = 384
CAP = 2
MOST = 64
N_ROWS = 32


def draw_sample_regions(key):
    subkeys = jax.random.split(key, 4)
    pattern = jnp.array([2 * KS, KS, KS // 2, KS // 2], dtype=jnp.int32)
    owner_loads = jnp.tile(pattern, N_ROWS // 4)
    ranking = jax.random.permutation(subkeys[0], N_ROWS).astype(jnp.int32)
    bounds = jnp.cumsum(owner_loads)
    tokens = jnp.arange(N_ROWS * KS, dtype=jnp.int32)
    rank_ids = jnp.sum((tokens[:, None] >= bounds[None, :]).astype(jnp.int32), axis=1)
    owner_of = ranking[rank_ids]
    run_ids = tokens // CAP
    source_row = run_ids % N_ROWS
    slot_index = run_ids // N_ROWS * CAP + tokens % CAP
    owner_table = jnp.zeros((N_ROWS, KS), jnp.int32).at[source_row, slot_index].set(owner_of)
    offsets = jax.random.randint(subkeys[1], (N_ROWS, KS), 0, PATCH, dtype=jnp.int32)
    last_strip = jnp.arange(N_ROWS, dtype=jnp.int32)[:, None] == N_ROWS - 1
    offsets = jnp.where(last_strip, 0, offsets)
    first_cols = jax.random.randint(subkeys[2], (N_ROWS, KS), 0, W - PATCH + 1, dtype=jnp.int32)
    step_ids = jax.random.randint(subkeys[3], (N_ROWS, KS), 0, NT, dtype=jnp.int32)
    return jnp.stack([offsets, first_cols, owner_table, step_ids], axis=-1).astype(jnp.int32)


def draw_regions(key, part):
    sample_keys = jax.random.split(jax.random.fold_in(key, 17), NS)
    return jax.vmap(draw_sample_regions)(sample_keys)


def shard_levels(own_key, extent, pieces, least, largest):
    def one(dim, parts):
        draws = jax.random.uniform(jax.random.fold_in(jax.random.fold_in(own_key, 6), dim), (parts,), jnp.float32, least / len(pieces), largest / len(pieces))
        return jnp.repeat(jnp.exp(draws), extent[dim] // parts).reshape((-1,) + (1,) * (len(extent) - dim - 1))

    factor_of = one(*pieces[0])
    for cut in pieces[1:]:
        factor_of = factor_of * one(*cut)
    return factor_of


def centred(key, extent, deviation, bound, pieces=(), kind=jnp.bfloat16):
    drawn = jax.random.normal(key, extent, jnp.float32) * deviation
    if len(pieces) > 0:
        drawn = shard_levels(key, extent, pieces, -0.22, 0.18) * drawn
    return jnp.clip(drawn, min=-bound, max=bound).astype(kind)


def setup_inputs(seed: int = 0) -> dict:
    arg_keys = jax.random.split(jax.random.key(seed), 11)
    return {
        "coarse": centred(arg_keys[0], (NS, CIN, H, W), 1.0, 6.0, ((0, 8), (2, 32))),
        "target": centred(arg_keys[1], (NS, CT, H, W), 1.0, 6.0, ((0, 8), (2, 32))),
        "noise": centred(arg_keys[2], (NS, N_ROWS, MOST, CT, PATCH * PATCH), 1.0, 6.0, ((0, 8), (1, 32))),
        "regions": draw_regions(jax.random.fold_in(arg_keys[10], 71), 0),
        "reg_conv": centred(arg_keys[4], (REG, 9 * CIN), (9 * CIN) ** -0.5, 0.1875),
        "reg_out": centred(arg_keys[5], (CT, REG), REG ** -0.5, 0.5),
        "conv_one": centred(arg_keys[6], (DC, 18 * CT), (18 * CT) ** -0.5, 0.1875),
        "conv_two": centred(arg_keys[7], (DC, 9 * DC), (9 * DC) ** -0.5, 0.1875),
        "out_proj": centred(arg_keys[8], (CT, DC), DC ** -0.5, 0.5),
        "step_embed": centred(arg_keys[9], (NT, DC), 0.5, 3.0, (), jnp.float32),
    }


TAPS = ((-1, -1), (-1, 0), (-1, 1), (0, -1), (0, 0), (0, 1), (1, -1), (1, 0), (1, 1))

def shifted(values, row_step, col_step, stride):
    length = values.shape[-1]
    margin = stride + 1
    widths = [(0, 0)] * (values.ndim - 1) + [(margin, margin)]
    padded = jnp.pad(values, widths)
    offset = margin + row_step * stride + col_step
    moved = lax.slice_in_dim(padded, offset, offset + length, axis=values.ndim - 1)
    column = jnp.arange(length, dtype=jnp.int32) % stride + col_step
    inside = (column >= 0) & (column < stride)
    return jnp.where(inside, moved, jnp.zeros((), moved.dtype))

def columns(values, stride):
    return jnp.concatenate([shifted(values, row_step, col_step, stride) for row_step, col_step in TAPS], axis=-2)

def fold(gradients, stride):
    width = gradients.shape[-2] // 9
    result = jnp.zeros(gradients.shape[:-2] + (width, gradients.shape[-1]), jnp.float32)
    for position, (row_step, col_step) in enumerate(TAPS):
        piece = gradients[..., position * width:(position + 1) * width, :]
        result = result + shifted(piece, -row_step, -col_step, stride)
    return result

def noise_levels(level_count):
    steps_f = jnp.arange(level_count, dtype=jnp.float32)
    return 0.1 * jnp.exp(steps_f * (math.log(100.0) / (level_count - 1)))

def silu_slope(values):
    gate = jax.nn.sigmoid(values)
    return gate * (1.0 + values * (1.0 - gate))

def product(form, left, right):
    return jnp.einsum(form, left.astype(jnp.float32), right.astype(jnp.float32), precision=lax.Precision.HIGHEST)

def regress(grid_rows, reg_conv, reg_out):
    channels, height, width = grid_rows.shape
    flat = grid_rows.reshape(channels, height * width)
    hidden = product('ok,kp->op', reg_conv, columns(flat, width))
    activated = jax.nn.silu(hidden).astype(jnp.bfloat16)
    mean_flat = product('co,op->cp', reg_out, activated).astype(jnp.bfloat16)
    return mean_flat.reshape(reg_out.shape[0], height, width)

def patch_block(mean_part, target_part, noise_part, step_ids, in_use, weights):
    conv_one, conv_two, out_proj, step_embed = weights
    stride = PATCH
    level_count = step_embed.shape[0]
    sigma_table = noise_levels(level_count)
    step_hot = (step_ids[:, None] == jnp.arange(level_count, dtype=jnp.int32)[None, :]).astype(jnp.float32)
    sigma = lax.optimization_barrier(jnp.sum(step_hot * sigma_table[None, :], axis=1))
    sigma_sq = sigma * sigma + 1.0
    scale_in = (1.0 / jnp.sqrt(sigma_sq))[:, None, None]
    scale_skip = (1.0 / sigma_sq)[:, None, None]
    scale_out = (sigma / jnp.sqrt(sigma_sq))[:, None, None]
    weight_loss = sigma_sq / (sigma * sigma)
    mean_float = mean_part.astype(jnp.float32)
    residual = target_part.astype(jnp.float32) - mean_float
    noisy = residual + sigma[:, None, None] * noise_part.astype(jnp.float32)
    inputs = jnp.concatenate([scale_in * noisy, mean_float], axis=1).astype(jnp.bfloat16)
    cols_in = columns(inputs, stride)
    embedded = lax.optimization_barrier(jnp.sum(step_hot[:, :, None] * step_embed[None, :, :], axis=1))
    pre_one = product('ok,bkp->bop', conv_one, cols_in) + embedded[:, :, None]
    act_one = jax.nn.silu(pre_one).astype(jnp.bfloat16)
    cols_one = columns(act_one, stride)
    pre_two = product('ok,bkp->bop', conv_two, cols_one)
    act_two = jax.nn.silu(pre_two).astype(jnp.bfloat16)
    output = product('co,bop->bcp', out_proj, act_two)
    error = scale_skip * noisy + scale_out * output - residual
    losses = weight_loss * lax.optimization_barrier(jnp.mean(error * error, axis=(1, 2))) * in_use
    factor = 2.0 * weight_loss * in_use / (error.shape[1] * error.shape[2])
    grad_output = (factor[:, None, None] * scale_out * error).astype(jnp.bfloat16)
    grad_proj = product('bcp,bop->co', grad_output, act_two)
    grad_act_two = product('co,bcp->bop', out_proj, grad_output)
    grad_pre_two = (grad_act_two * silu_slope(pre_two)).astype(jnp.bfloat16)
    grad_two = product('bop,bkp->ok', grad_pre_two, cols_one)
    grad_cols = product('ok,bop->bkp', conv_two, grad_pre_two)
    grad_act_one = fold(grad_cols, stride)
    grad_pre_one = (grad_act_one * silu_slope(pre_one)).astype(jnp.bfloat16)
    grad_one = product('bop,bkp->ok', grad_pre_one, cols_in)
    pixel_sums = lax.optimization_barrier(jnp.sum(grad_pre_one.astype(jnp.float32), axis=2))
    grad_table = lax.optimization_barrier(jnp.sum(step_hot[:, :, None] * pixel_sums[:, None, :], axis=0))
    return (losses, (grad_one, grad_two, grad_proj, grad_table))

def run_blocks(mean_part, target_part, noise_part, step_ids, in_use, weights):
    patch_count = mean_part.shape[0]
    blocks = patch_count // 4

    def regroup(values):
        return values.reshape((blocks, 4) + values.shape[1:])

    def advance(running, group_block):
        losses, gradients = patch_block(group_block[0], group_block[1], group_block[2], group_block[3], group_block[4], weights)
        summed = (running[0] + gradients[0], running[1] + gradients[1], running[2] + gradients[2], running[3] + gradients[3])
        return (summed, losses)
    initial = (jnp.zeros(weights[0].shape, jnp.float32), jnp.zeros(weights[1].shape, jnp.float32), jnp.zeros(weights[2].shape, jnp.float32), jnp.zeros(weights[3].shape, jnp.float32))
    stacked = (regroup(mean_part), regroup(target_part), regroup(noise_part), regroup(step_ids), regroup(in_use))
    gradients, losses = lax.scan(advance, initial, stacked)
    return (losses.reshape(patch_count), gradients)

def owner_tables(region_rows, strips):
    owners = region_rows[:, :, 2]
    owner_hot = (owners[:, :, None] == jnp.arange(strips, dtype=jnp.int32)[None, None, :]).astype(jnp.int32)
    pair_rank = lax.optimization_barrier(jnp.sum((jnp.cumsum(owner_hot, axis=1) - owner_hot) * owner_hot, axis=2))
    flat_hot = owner_hot.reshape(-1, strips)
    owner_slot = lax.optimization_barrier(jnp.sum((jnp.cumsum(flat_hot, axis=0) - flat_hot) * flat_hot, axis=1)).reshape(owners.shape)
    return (owners, pair_rank, owner_slot)

def reference(coarse, target, noise, regions, reg_conv, reg_out, conv_one, conv_two, out_proj, step_embed):
    weights = (conv_one, conv_two, out_proj, step_embed)
    strips = regions.shape[1]
    per_strip = regions.shape[2]
    means = []
    owner_rows = []
    totals = None
    zero_index = jnp.zeros((), jnp.int32)
    for sample in range(coarse.shape[0]):
        mean_grid = regress(coarse[sample], reg_conv, reg_out)
        pair_grid = jnp.stack([mean_grid, target[sample]])
        region_rows = regions[sample]
        owners, pair_rank, owner_slot = owner_tables(region_rows, strips)
        flat_regions = region_rows.reshape(strips * per_strip, 4)
        top_rows = jnp.arange(strips * per_strip, dtype=jnp.int32) // per_strip * PATCH + flat_regions[:, 0]

        def cut(row_at, col_at):
            piece = lax.dynamic_slice(pair_grid, (zero_index, zero_index, row_at.astype(jnp.int32), col_at.astype(jnp.int32)), (2, pair_grid.shape[1], PATCH, PATCH))
            return piece.reshape(2, pair_grid.shape[1], PATCH * PATCH)
        patches = jax.vmap(cut)(top_rows, flat_regions[:, 1])
        patch_noise = noise[sample][owners.reshape(-1), owner_slot.reshape(-1)]
        in_use = jnp.ones((strips * per_strip,), jnp.float32)
        losses, gradients = run_blocks(patches[:, 0], patches[:, 1], patch_noise, flat_regions[:, 3], in_use, weights)
        owner_hot = (owners.reshape(-1)[:, None] == jnp.arange(strips, dtype=jnp.int32)[None, :]).astype(jnp.float32)
        owner_rows.append(lax.optimization_barrier(jnp.sum(owner_hot * losses[:, None], axis=0)))
        means.append(mean_grid)
        if totals is None:
            totals = gradients
        else:
            totals = (totals[0] + gradients[0], totals[1] + gradients[1], totals[2] + gradients[2], totals[3] + gradients[3])
    return (jnp.stack(means), jnp.stack(owner_rows), totals[0], totals[1], totals[2], totals[3])
```

```python
import math

import jax
import jax.numpy as jnp
from jax import lax
from jax.sharding import PartitionSpec as P

PATCH = 12


TAPS = ((-1, -1), (-1, 0), (-1, 1), (0, -1), (0, 0), (0, 1), (1, -1), (1, 0), (1, 1))


def padded_2(cells, sides, width):
    for axis, dim in sides:
        count = lax.axis_size(axis)
        ends = count - 1
        head = lax.slice_in_dim(cells, 0, width, axis=dim)
        tail = lax.slice_in_dim(cells, cells.shape[dim] - width, cells.shape[dim], axis=dim)
        cells = jnp.concatenate(
            [
                lax.ppermute(tail, axis, [(i, (i + 1) % count) for i in range(ends)]),
                cells,
                lax.ppermute(head, axis, [((i + 1) % count, i) for i in range(ends)]),
            ],
            axis=dim,
        )
    return cells


def shifted_2(block, axis, distance):
    devices = range(lax.axis_size(axis))
    route = [(i - distance, i) for i in devices if i - distance in devices]
    return lax.ppermute(block, axis, route)


def shifted(values, row_step, col_step, stride):
    length = values.shape[-1]
    margin = stride + 1
    widths = [(0, 0)] * (values.ndim - 1) + [(margin, margin)]
    padded = jnp.pad(values, widths)
    offset = margin + row_step * stride + col_step
    moved = lax.slice_in_dim(padded, offset, offset + length, axis=values.ndim - 1)
    column = jnp.arange(length, dtype=jnp.int32) % stride + col_step
    inside = (column >= 0) & (column < stride)
    return jnp.where(inside, moved, jnp.zeros((), moved.dtype))


def columns(values, stride):
    return jnp.concatenate(
        [shifted(values, row_step, col_step, stride) for row_step, col_step in TAPS], axis=-2
    )


def fold(gradients, stride):
    width = gradients.shape[-2] // 9
    result = jnp.zeros(gradients.shape[:-2] + (width, gradients.shape[-1]), jnp.float32)
    for position, (row_step, col_step) in enumerate(TAPS):
        piece = gradients[..., position * width : (position + 1) * width, :]
        result = result + shifted(piece, -row_step, -col_step, stride)
    return result


def noise_levels(level_count):
    steps_f = jnp.arange(level_count, dtype=jnp.float32)
    return 0.1 * jnp.exp(steps_f * (math.log(100.0) / (level_count - 1)))


def silu_slope(values):
    gate = jax.nn.sigmoid(values)
    return gate * (1.0 + values * (1.0 - gate))


def product(form, left, right):
    return jnp.einsum(form, left, right, preferred_element_type=jnp.float32)


def regress(grid_rows, reg_conv, reg_out):
    channels, height, width = grid_rows.shape
    flat = grid_rows.reshape(channels, height * width)
    hidden = product("ok,kp->op", reg_conv, columns(flat, width))
    activated = jax.nn.silu(hidden).astype(jnp.bfloat16)
    mean_flat = product("co,op->cp", reg_out, activated).astype(jnp.bfloat16)
    return mean_flat.reshape(reg_out.shape[0], height, width)


def patch_block(mean_part, target_part, noise_part, step_ids, in_use, weights):
    conv_one, conv_two, out_proj, step_embed = weights
    stride = PATCH
    level_count = step_embed.shape[0]
    sigma_table = noise_levels(level_count)
    step_hot = (step_ids[:, None] == jnp.arange(level_count, dtype=jnp.int32)[None, :]).astype(
        jnp.float32
    )
    sigma = jnp.sum(step_hot * sigma_table[None, :], axis=1)
    sigma_sq = sigma * sigma + 1.0
    scale_in = (1.0 / jnp.sqrt(sigma_sq))[:, None, None]
    scale_skip = (1.0 / sigma_sq)[:, None, None]
    scale_out = (sigma / jnp.sqrt(sigma_sq))[:, None, None]
    weight_loss = sigma_sq / (sigma * sigma)
    mean_float = mean_part.astype(jnp.float32)
    residual = target_part.astype(jnp.float32) - mean_float
    noisy = residual + sigma[:, None, None] * noise_part.astype(jnp.float32)
    inputs = jnp.concatenate([scale_in * noisy, mean_float], axis=1).astype(jnp.bfloat16)
    cols_in = columns(inputs, stride)
    embedded = jnp.sum(step_hot[:, :, None] * step_embed[None, :, :], axis=1)
    pre_one = product("ok,bkp->bop", conv_one, cols_in) + embedded[:, :, None]
    act_one = jax.nn.silu(pre_one).astype(jnp.bfloat16)
    cols_one = columns(act_one, stride)
    pre_two = product("ok,bkp->bop", conv_two, cols_one)
    act_two = jax.nn.silu(pre_two).astype(jnp.bfloat16)
    output = product("co,bop->bcp", out_proj, act_two)
    error = scale_skip * noisy + scale_out * output - residual
    losses = weight_loss * jnp.mean(error * error, axis=(1, 2)) * in_use
    factor = 2.0 * weight_loss * in_use / (error.shape[1] * error.shape[2])
    grad_output = (factor[:, None, None] * scale_out * error).astype(jnp.bfloat16)
    grad_proj = product("bcp,bop->co", grad_output, act_two)
    grad_act_two = product("co,bcp->bop", out_proj, grad_output)
    grad_pre_two = (grad_act_two * silu_slope(pre_two)).astype(jnp.bfloat16)
    grad_two = product("bop,bkp->ok", grad_pre_two, cols_one)
    grad_cols = product("ok,bop->bkp", conv_two, grad_pre_two)
    grad_act_one = fold(grad_cols, stride)
    grad_pre_one = (grad_act_one * silu_slope(pre_one)).astype(jnp.bfloat16)
    grad_one = product("bop,bkp->ok", grad_pre_one, cols_in)
    pixel_sums = jnp.sum(grad_pre_one, axis=2, dtype=jnp.float32)
    grad_table = jnp.sum(step_hot[:, :, None] * pixel_sums[:, None, :], axis=0)
    return (losses, (grad_one, grad_two, grad_proj, grad_table))


def run_blocks(mean_part, target_part, noise_part, step_ids, in_use, weights):
    patch_count = mean_part.shape[0]
    blocks = patch_count // 4

    def regroup(values):
        return values.reshape((blocks, 4) + values.shape[1:])

    def advance(running, group_block):
        losses, gradients = patch_block(
            group_block[0], group_block[1], group_block[2], group_block[3], group_block[4], weights
        )
        summed = (
            running[0] + gradients[0],
            running[1] + gradients[1],
            running[2] + gradients[2],
            running[3] + gradients[3],
        )
        return (summed, losses)

    initial = (
        jnp.zeros(weights[0].shape, jnp.float32),
        jnp.zeros(weights[1].shape, jnp.float32),
        jnp.zeros(weights[2].shape, jnp.float32),
        jnp.zeros(weights[3].shape, jnp.float32),
    )
    stacked = (
        regroup(mean_part),
        regroup(target_part),
        regroup(noise_part),
        regroup(step_ids),
        regroup(in_use),
    )
    gradients, losses = lax.scan(advance, initial, stacked)
    return (losses.reshape(patch_count), gradients)


def owner_tables(region_rows, strips):
    owners = region_rows[:, :, 2]
    owner_hot = (owners[:, :, None] == jnp.arange(strips, dtype=jnp.int32)[None, None, :]).astype(
        jnp.int32
    )
    pair_rank = jnp.sum((jnp.cumsum(owner_hot, axis=1) - owner_hot) * owner_hot, axis=2)
    flat_hot = owner_hot.reshape(-1, strips)
    owner_slot = jnp.sum((jnp.cumsum(flat_hot, axis=0) - flat_hot) * flat_hot, axis=1).reshape(
        owners.shape
    )
    return (owners, pair_rank, owner_slot)


def noise_routes(region_rows, owners, pair_rank, owner_slot, strip_index, capacity):
    hits = (
        (owners == strip_index)[:, :, None]
        & (pair_rank[:, :, None] == jnp.arange(capacity, dtype=jnp.int32)[None, None, :])
    ).astype(jnp.int32)
    return jnp.sum(hits * owner_slot[:, :, None], axis=1)


def cut_patches(source_grid, row_at, col_at, height):
    zero_index = jnp.zeros((), jnp.int32)

    def cut(row_start, col_start):
        piece = lax.dynamic_slice(
            source_grid,
            (zero_index, zero_index, row_start, col_start),
            (2, source_grid.shape[1], height, height),
        )
        return piece.reshape(2, source_grid.shape[1], height * height)

    return jax.vmap(cut)(row_at, col_at)


def per_device(
    coarse, target, noise, regions, reg_conv, reg_out, conv_one, conv_two, out_proj, step_embed
):
    strips = lax.axis_size("rows")
    strip_index = lax.axis_index("rows")
    sample_count = lax.axis_size("segment") * lax.axis_size("dp")
    sample_index = lax.axis_index("segment") * lax.axis_size("dp") + lax.axis_index("dp")
    region_rows = regions[0]
    per_strip = region_rows.shape[1]
    capacity = max(2, (2 * per_strip + strips - 1) // strips)
    weights = (conv_one, conv_two, out_proj, step_embed)
    owners, pair_rank, owner_slot = owner_tables(region_rows, strips)
    send_slot = noise_routes(region_rows, owners, pair_rank, owner_slot, strip_index, capacity)
    outgoing = jnp.take(noise[0, 0], send_slot.reshape(-1), axis=0)
    outgoing = outgoing.reshape((strips, capacity) + outgoing.shape[1:])
    received = lax.all_to_all(outgoing, "rows", split_axis=0, concat_axis=0, tiled=True)
    rimmed = padded_2(coarse, (("rows", 2),), 1)
    mean_strip = regress(rimmed[0], reg_conv, reg_out)[:, 1:-1]
    height = mean_strip.shape[1]
    pair_strip = jnp.stack([mean_strip, target[0]])
    own_regions = lax.dynamic_index_in_dim(region_rows, strip_index, 0, keepdims=False)
    own_pairs = lax.dynamic_index_in_dim(pair_rank, strip_index, 0, keepdims=False)
    below = shifted_2(pair_strip[:, :, : height - 1], "rows", -1)
    extended = jnp.concatenate([pair_strip, below], axis=2)
    patches = cut_patches(extended, own_regions[:, 0], own_regions[:, 1], height)
    flat_recv = received.reshape((strips * capacity,) + received.shape[2:])
    patch_noise = jnp.take(flat_recv, own_regions[:, 2] * capacity + own_pairs, axis=0)
    in_use = jnp.ones((per_strip,), jnp.float32)
    losses, gradients = run_blocks(
        patches[:, 0], patches[:, 1], patch_noise, own_regions[:, 3], in_use, weights
    )
    owner_hot = (own_regions[:, 2][:, None] == jnp.arange(strips, dtype=jnp.int32)[None, :])
    owner_part = jnp.sum(owner_hot.astype(jnp.float32) * losses[:, None], axis=0)
    sample_hot = (jnp.arange(sample_count, dtype=jnp.int32) == sample_index).astype(jnp.float32)
    owner_table = sample_hot[:, None] * owner_part[None, :]
    pieces = (gradients[0], gradients[1], gradients[2], gradients[3], owner_table)
    flat = jnp.concatenate([piece.reshape(-1) for piece in pieces])
    summed = lax.psum(flat, ("segment", "rows", "dp"))
    results = []
    offset = 0
    for piece in pieces:
        results.append(summed[offset : offset + piece.size].reshape(piece.shape))
        offset += piece.size
    table = results[4]
    owner_total = lax.dynamic_slice(table, (sample_index, strip_index), (1, 1))
    return (mean_strip[None], owner_total, results[0], results[1], results[2], results[3])


def solution(mesh):
    placed = (
        P(("segment", "dp"), None, "rows", None),
        P(("segment", "dp"), None, "rows", None),
        P(("segment", "dp"), "rows", None, None, None),
        P(("segment", "dp"), None, None, None),
        P(),
        P(),
        P(),
        P(),
        P(),
        P(),
    )
    return jax.shard_map(
        per_device,
        mesh=mesh,
        in_specs=placed,
        out_specs=(
            P(("segment", "dp"), None, "rows", None),
            P(("segment", "dp"), "rows"),
            P(),
            P(),
            P(),
            P(),
        ),
        check_vma=False,
    )
```

```python
import math

import jax
import jax.numpy as jnp
from jax import lax
from jax.sharding import PartitionSpec as P

PATCH = 12


TAPS = ((-1, -1), (-1, 0), (-1, 1), (0, -1), (0, 0), (0, 1), (1, -1), (1, 0), (1, 1))


def padded_2(cells, sides, width):
    for axis, dim in sides:
        count = lax.axis_size(axis)
        ends = count - 1
        head = lax.slice_in_dim(cells, 0, width, axis=dim)
        tail = lax.slice_in_dim(cells, cells.shape[dim] - width, cells.shape[dim], axis=dim)
        cells = jnp.concatenate(
            [
                lax.ppermute(tail, axis, [(i, (i + 1) % count) for i in range(ends)]),
                cells,
                lax.ppermute(head, axis, [((i + 1) % count, i) for i in range(ends)]),
            ],
            axis=dim,
        )
    return cells


def shifted_2(block, axis, distance):
    devices = range(lax.axis_size(axis))
    route = [(i - distance, i) for i in devices if i - distance in devices]
    return lax.ppermute(block, axis, route)


def shifted(values, row_step, col_step, stride):
    length = values.shape[-1]
    margin = stride + 1
    widths = [(0, 0)] * (values.ndim - 1) + [(margin, margin)]
    padded = jnp.pad(values, widths)
    offset = margin + row_step * stride + col_step
    moved = lax.slice_in_dim(padded, offset, offset + length, axis=values.ndim - 1)
    column = jnp.arange(length, dtype=jnp.int32) % stride + col_step
    inside = (column >= 0) & (column < stride)
    return jnp.where(inside, moved, jnp.zeros((), moved.dtype))


def columns(values, stride):
    return jnp.concatenate(
        [shifted(values, row_step, col_step, stride) for row_step, col_step in TAPS], axis=-2
    )


def fold(gradients, stride):
    width = gradients.shape[-2] // 9
    result = jnp.zeros(gradients.shape[:-2] + (width, gradients.shape[-1]), jnp.float32)
    for position, (row_step, col_step) in enumerate(TAPS):
        piece = gradients[..., position * width : (position + 1) * width, :]
        result = result + shifted(piece, -row_step, -col_step, stride)
    return result


def noise_levels(level_count):
    steps_f = jnp.arange(level_count, dtype=jnp.float32)
    return 0.1 * jnp.exp(steps_f * (math.log(100.0) / (level_count - 1)))


def silu_slope(values):
    gate = jax.nn.sigmoid(values)
    return gate * (1.0 + values * (1.0 - gate))


def product(form, left, right):
    return jnp.einsum(form, left, right, preferred_element_type=jnp.float32)


def regress(grid_rows, reg_conv, reg_out):
    channels, height, width = grid_rows.shape
    flat = grid_rows.reshape(channels, height * width)
    hidden = product("ok,kp->op", reg_conv, columns(flat, width))
    activated = jax.nn.silu(hidden).astype(jnp.bfloat16)
    mean_flat = product("co,op->cp", reg_out, activated).astype(jnp.bfloat16)
    return mean_flat.reshape(reg_out.shape[0], height, width)


def patch_block(mean_part, target_part, noise_part, step_ids, in_use, weights):
    conv_one, conv_two, out_proj, step_embed = weights
    stride = PATCH
    level_count = step_embed.shape[0]
    sigma_table = noise_levels(level_count)
    step_hot = (step_ids[:, None] == jnp.arange(level_count, dtype=jnp.int32)[None, :]).astype(
        jnp.float32
    )
    sigma = jnp.sum(step_hot * sigma_table[None, :], axis=1)
    sigma_sq = sigma * sigma + 1.0
    scale_in = (1.0 / jnp.sqrt(sigma_sq))[:, None, None]
    scale_skip = (1.0 / sigma_sq)[:, None, None]
    scale_out = (sigma / jnp.sqrt(sigma_sq))[:, None, None]
    weight_loss = sigma_sq / (sigma * sigma)
    mean_float = mean_part.astype(jnp.float32)
    residual = target_part.astype(jnp.float32) - mean_float
    noisy = residual + sigma[:, None, None] * noise_part.astype(jnp.float32)
    inputs = jnp.concatenate([scale_in * noisy, mean_float], axis=1).astype(jnp.bfloat16)
    cols_in = columns(inputs, stride)
    embedded = jnp.sum(step_hot[:, :, None] * step_embed[None, :, :], axis=1)
    pre_one = product("ok,bkp->bop", conv_one, cols_in) + embedded[:, :, None]
    act_one = jax.nn.silu(pre_one).astype(jnp.bfloat16)
    cols_one = columns(act_one, stride)
    pre_two = product("ok,bkp->bop", conv_two, cols_one)
    act_two = jax.nn.silu(pre_two).astype(jnp.bfloat16)
    output = product("co,bop->bcp", out_proj, act_two)
    error = scale_skip * noisy + scale_out * output - residual
    losses = weight_loss * jnp.mean(error * error, axis=(1, 2)) * in_use
    factor = 2.0 * weight_loss * in_use / (error.shape[1] * error.shape[2])
    grad_output = (factor[:, None, None] * scale_out * error).astype(jnp.bfloat16)
    grad_proj = product("bcp,bop->co", grad_output, act_two)
    grad_act_two = product("co,bcp->bop", out_proj, grad_output)
    grad_pre_two = (grad_act_two * silu_slope(pre_two)).astype(jnp.bfloat16)
    grad_two = product("bop,bkp->ok", grad_pre_two, cols_one)
    grad_cols = product("ok,bop->bkp", conv_two, grad_pre_two)
    grad_act_one = fold(grad_cols, stride)
    grad_pre_one = (grad_act_one * silu_slope(pre_one)).astype(jnp.bfloat16)
    grad_one = product("bop,bkp->ok", grad_pre_one, cols_in)
    pixel_sums = jnp.sum(grad_pre_one, axis=2, dtype=jnp.float32)
    grad_table = jnp.sum(step_hot[:, :, None] * pixel_sums[:, None, :], axis=0)
    return (losses, (grad_one, grad_two, grad_proj, grad_table))


def run_blocks(mean_part, target_part, noise_part, step_ids, in_use, weights):
    patch_count = mean_part.shape[0]
    blocks = patch_count // 4

    def regroup(values):
        return values.reshape((blocks, 4) + values.shape[1:])

    def advance(running, group_block):
        losses, gradients = patch_block(
            group_block[0], group_block[1], group_block[2], group_block[3], group_block[4], weights
        )
        summed = (
            running[0] + gradients[0],
            running[1] + gradients[1],
            running[2] + gradients[2],
            running[3] + gradients[3],
        )
        return (summed, losses)

    initial = (
        jnp.zeros(weights[0].shape, jnp.float32),
        jnp.zeros(weights[1].shape, jnp.float32),
        jnp.zeros(weights[2].shape, jnp.float32),
        jnp.zeros(weights[3].shape, jnp.float32),
    )
    stacked = (
        regroup(mean_part),
        regroup(target_part),
        regroup(noise_part),
        regroup(step_ids),
        regroup(in_use),
    )
    gradients, losses = lax.scan(advance, initial, stacked)
    return (losses.reshape(patch_count), gradients)


def owner_tables(region_rows, strips):
    owners = region_rows[:, :, 2]
    owner_hot = (owners[:, :, None] == jnp.arange(strips, dtype=jnp.int32)[None, None, :]).astype(
        jnp.int32
    )
    pair_rank = jnp.sum((jnp.cumsum(owner_hot, axis=1) - owner_hot) * owner_hot, axis=2)
    flat_hot = owner_hot.reshape(-1, strips)
    owner_slot = jnp.sum((jnp.cumsum(flat_hot, axis=0) - flat_hot) * flat_hot, axis=1).reshape(
        owners.shape
    )
    return (owners, pair_rank, owner_slot)


def noise_routes(region_rows, owners, pair_rank, owner_slot, strip_index, capacity):
    hits = (
        (owners == strip_index)[:, :, None]
        & (pair_rank[:, :, None] == jnp.arange(capacity, dtype=jnp.int32)[None, None, :])
    ).astype(jnp.int32)
    return jnp.sum(hits * owner_slot[:, :, None], axis=1)


def exchange_sum(flat, steps):
    spread = 1
    for _, distance in steps:
        spread *= 2
    size = flat.shape[0]
    unit = spread * 8
    padded = (size + unit - 1) // unit * unit
    values = jnp.pad(flat, (0, padded - size))
    places = {axis: lax.axis_index(axis) for axis, _ in steps}
    for axis, distance in steps:
        count = lax.axis_size(axis)
        half = values.shape[0] // 2
        low, high = values[:half], values[half:]
        upper = (places[axis] // distance) % 2 == 1
        route = [(i, i ^ distance) for i in range(count)]
        kept = jnp.where(upper, high, low)
        sent = jnp.where(upper, low, high)
        values = kept + lax.ppermute(sent, axis, route)
    for axis, distance in reversed(steps):
        count = lax.axis_size(axis)
        upper = (places[axis] // distance) % 2 == 1
        route = [(i, i ^ distance) for i in range(count)]
        other = lax.ppermute(values, axis, route)
        values = jnp.where(
            upper, jnp.concatenate([other, values]), jnp.concatenate([values, other])
        )
    return values[:size]


def reduce_steps():
    sizes = {axis: lax.axis_size(axis) for axis in ("segment", "rows", "dp")}
    steps = []
    distance = 1
    while distance < max(sizes.values()):
        for axis in ("segment", "rows", "dp"):
            if distance < sizes[axis]:
                steps.append((axis, distance))
        distance *= 2
    return steps


def cut_patches(source_grid, row_at, col_at, height):
    zero_index = jnp.zeros((), jnp.int32)

    def cut(row_start, col_start):
        piece = lax.dynamic_slice(
            source_grid,
            (zero_index, zero_index, row_start, col_start),
            (2, source_grid.shape[1], height, height),
        )
        return piece.reshape(2, source_grid.shape[1], height * height)

    return jax.vmap(cut)(row_at, col_at)


def per_device(
    coarse, target, noise, regions, reg_conv, reg_out, conv_one, conv_two, out_proj, step_embed
):
    strips = lax.axis_size("rows")
    strip_index = lax.axis_index("rows")
    sample_count = lax.axis_size("segment") * lax.axis_size("dp")
    sample_index = lax.axis_index("segment") * lax.axis_size("dp") + lax.axis_index("dp")
    region_rows = regions[0]
    per_strip = region_rows.shape[1]
    capacity = max(2, (2 * per_strip + strips - 1) // strips)
    weights = (conv_one, conv_two, out_proj, step_embed)
    owners, pair_rank, owner_slot = owner_tables(region_rows, strips)
    send_slot = noise_routes(region_rows, owners, pair_rank, owner_slot, strip_index, capacity)
    outgoing = jnp.take(noise[0, 0], send_slot.reshape(-1), axis=0)
    outgoing = outgoing.reshape((strips, capacity) + outgoing.shape[1:])
    received = lax.all_to_all(outgoing, "rows", split_axis=0, concat_axis=0, tiled=True)
    rimmed = padded_2(coarse, (("rows", 2),), 1)
    mean_strip = regress(rimmed[0], reg_conv, reg_out)[:, 1:-1]
    height = mean_strip.shape[1]
    pair_strip = jnp.stack([mean_strip, target[0]])
    own_regions = lax.dynamic_index_in_dim(region_rows, strip_index, 0, keepdims=False)
    own_pairs = lax.dynamic_index_in_dim(pair_rank, strip_index, 0, keepdims=False)
    below = shifted_2(pair_strip[:, :, : height - 1], "rows", -1)
    extended = jnp.concatenate([pair_strip, below], axis=2)
    patches = cut_patches(extended, own_regions[:, 0], own_regions[:, 1], height)
    flat_recv = received.reshape((strips * capacity,) + received.shape[2:])
    patch_noise = jnp.take(flat_recv, own_regions[:, 2] * capacity + own_pairs, axis=0)
    in_use = jnp.ones((per_strip,), jnp.float32)
    losses, gradients = run_blocks(
        patches[:, 0], patches[:, 1], patch_noise, own_regions[:, 3], in_use, weights
    )
    owner_hot = (own_regions[:, 2][:, None] == jnp.arange(strips, dtype=jnp.int32)[None, :])
    owner_part = jnp.sum(owner_hot.astype(jnp.float32) * losses[:, None], axis=0)
    sample_hot = (jnp.arange(sample_count, dtype=jnp.int32) == sample_index).astype(jnp.float32)
    owner_table = sample_hot[:, None] * owner_part[None, :]
    pieces = (gradients[0], gradients[1], gradients[2], gradients[3], owner_table)
    flat = jnp.concatenate([piece.reshape(-1) for piece in pieces])
    summed = exchange_sum(flat, reduce_steps())
    results = []
    offset = 0
    for piece in pieces:
        results.append(summed[offset : offset + piece.size].reshape(piece.shape))
        offset += piece.size
    table = results[4]
    owner_total = lax.dynamic_slice(table, (sample_index, strip_index), (1, 1))
    return (mean_strip[None], owner_total, results[0], results[1], results[2], results[3])


def solution(mesh):
    placed = (
        P(("segment", "dp"), None, "rows", None),
        P(("segment", "dp"), None, "rows", None),
        P(("segment", "dp"), "rows", None, None, None),
        P(("segment", "dp"), None, None, None),
        P(),
        P(),
        P(),
        P(),
        P(),
        P(),
    )
    return jax.shard_map(
        per_device,
        mesh=mesh,
        in_specs=placed,
        out_specs=(
            P(("segment", "dp"), None, "rows", None),
            P(("segment", "dp"), "rows"),
            P(),
            P(),
            P(),
            P(),
        ),
        check_vma=False,
    )
```

```python
import math

import jax
import jax.numpy as jnp
from jax import lax
from jax.experimental import pallas as pl
from jax.experimental.pallas import tpu as pltpu
from jax.sharding import PartitionSpec as P

PATCH = 12


TAPS = ((-1, -1), (-1, 0), (-1, 1), (0, -1), (0, 0), (0, 1), (1, -1), (1, 0), (1, 1))


def padded_2(cells, sides, width):
    for axis, dim in sides:
        count = lax.axis_size(axis)
        ends = count - 1
        head = lax.slice_in_dim(cells, 0, width, axis=dim)
        tail = lax.slice_in_dim(cells, cells.shape[dim] - width, cells.shape[dim], axis=dim)
        cells = jnp.concatenate(
            [
                lax.ppermute(tail, axis, [(i, (i + 1) % count) for i in range(ends)]),
                cells,
                lax.ppermute(head, axis, [((i + 1) % count, i) for i in range(ends)]),
            ],
            axis=dim,
        )
    return cells


def shifted_2(block, axis, distance):
    devices = range(lax.axis_size(axis))
    route = [(i - distance, i) for i in devices if i - distance in devices]
    return lax.ppermute(block, axis, route)


def shifted(values, row_step, col_step, stride):
    length = values.shape[-1]
    margin = stride + 1
    widths = [(0, 0)] * (values.ndim - 1) + [(margin, margin)]
    padded = jnp.pad(values, widths)
    offset = margin + row_step * stride + col_step
    moved = lax.slice_in_dim(padded, offset, offset + length, axis=values.ndim - 1)
    column = jnp.arange(length, dtype=jnp.int32) % stride + col_step
    inside = (column >= 0) & (column < stride)
    return jnp.where(inside, moved, jnp.zeros((), moved.dtype))


def columns(values, stride):
    return jnp.concatenate(
        [shifted(values, row_step, col_step, stride) for row_step, col_step in TAPS], axis=-2
    )


def fold(gradients, stride):
    width = gradients.shape[-2] // 9
    result = jnp.zeros(gradients.shape[:-2] + (width, gradients.shape[-1]), jnp.float32)
    for position, (row_step, col_step) in enumerate(TAPS):
        piece = gradients[..., position * width : (position + 1) * width, :]
        result = result + shifted(piece, -row_step, -col_step, stride)
    return result


def noise_levels(level_count):
    steps_f = jnp.arange(level_count, dtype=jnp.float32)
    return 0.1 * jnp.exp(steps_f * (math.log(100.0) / (level_count - 1)))


def silu_slope(values):
    gate = jax.nn.sigmoid(values)
    return gate * (1.0 + values * (1.0 - gate))


def product(form, left, right):
    return jnp.einsum(form, left, right, preferred_element_type=jnp.float32)


def regress(grid_rows, reg_conv, reg_out):
    channels, height, width = grid_rows.shape
    flat = grid_rows.reshape(channels, height * width)
    hidden = product("ok,kp->op", reg_conv, columns(flat, width))
    activated = jax.nn.silu(hidden).astype(jnp.bfloat16)
    mean_flat = product("co,op->cp", reg_out, activated).astype(jnp.bfloat16)
    return mean_flat.reshape(reg_out.shape[0], height, width)


def patch_block(mean_part, target_part, noise_part, step_ids, in_use, weights):
    conv_one, conv_two, out_proj, step_embed = weights
    stride = PATCH
    level_count = step_embed.shape[0]
    sigma_table = noise_levels(level_count)
    step_hot = (step_ids[:, None] == jnp.arange(level_count, dtype=jnp.int32)[None, :]).astype(
        jnp.float32
    )
    sigma = jnp.sum(step_hot * sigma_table[None, :], axis=1)
    sigma_sq = sigma * sigma + 1.0
    scale_in = (1.0 / jnp.sqrt(sigma_sq))[:, None, None]
    scale_skip = (1.0 / sigma_sq)[:, None, None]
    scale_out = (sigma / jnp.sqrt(sigma_sq))[:, None, None]
    weight_loss = sigma_sq / (sigma * sigma)
    mean_float = mean_part.astype(jnp.float32)
    residual = target_part.astype(jnp.float32) - mean_float
    noisy = residual + sigma[:, None, None] * noise_part.astype(jnp.float32)
    inputs = jnp.concatenate([scale_in * noisy, mean_float], axis=1).astype(jnp.bfloat16)
    cols_in = columns(inputs, stride)
    embedded = jnp.sum(step_hot[:, :, None] * step_embed[None, :, :], axis=1)
    pre_one = product("ok,bkp->bop", conv_one, cols_in) + embedded[:, :, None]
    act_one = jax.nn.silu(pre_one).astype(jnp.bfloat16)
    cols_one = columns(act_one, stride)
    pre_two = product("ok,bkp->bop", conv_two, cols_one)
    act_two = jax.nn.silu(pre_two).astype(jnp.bfloat16)
    output = product("co,bop->bcp", out_proj, act_two)
    error = scale_skip * noisy + scale_out * output - residual
    losses = weight_loss * jnp.mean(error * error, axis=(1, 2)) * in_use
    factor = 2.0 * weight_loss * in_use / (error.shape[1] * error.shape[2])
    grad_output = (factor[:, None, None] * scale_out * error).astype(jnp.bfloat16)
    grad_proj = product("bcp,bop->co", grad_output, act_two)
    grad_act_two = product("co,bcp->bop", out_proj, grad_output)
    grad_pre_two = (grad_act_two * silu_slope(pre_two)).astype(jnp.bfloat16)
    grad_two = product("bop,bkp->ok", grad_pre_two, cols_one)
    grad_cols = product("ok,bop->bkp", conv_two, grad_pre_two)
    grad_act_one = fold(grad_cols, stride)
    grad_pre_one = (grad_act_one * silu_slope(pre_one)).astype(jnp.bfloat16)
    grad_one = product("bop,bkp->ok", grad_pre_one, cols_in)
    pixel_sums = jnp.sum(grad_pre_one, axis=2, dtype=jnp.float32)
    grad_table = jnp.sum(step_hot[:, :, None] * pixel_sums[:, None, :], axis=0)
    return (losses, (grad_one, grad_two, grad_proj, grad_table))


def run_blocks(mean_part, target_part, noise_part, step_ids, in_use, weights):
    patch_count = mean_part.shape[0]
    blocks = patch_count // 4

    def regroup(values):
        return values.reshape((blocks, 4) + values.shape[1:])

    def advance(running, group_block):
        losses, gradients = patch_block(
            group_block[0], group_block[1], group_block[2], group_block[3], group_block[4], weights
        )
        summed = (
            running[0] + gradients[0],
            running[1] + gradients[1],
            running[2] + gradients[2],
            running[3] + gradients[3],
        )
        return (summed, losses)

    initial = (
        jnp.zeros(weights[0].shape, jnp.float32),
        jnp.zeros(weights[1].shape, jnp.float32),
        jnp.zeros(weights[2].shape, jnp.float32),
        jnp.zeros(weights[3].shape, jnp.float32),
    )
    stacked = (
        regroup(mean_part),
        regroup(target_part),
        regroup(noise_part),
        regroup(step_ids),
        regroup(in_use),
    )
    gradients, losses = lax.scan(advance, initial, stacked)
    return (losses.reshape(patch_count), gradients)


def tap_masks(rows):
    cell = jnp.arange(rows, dtype=jnp.int32) % (PATCH * PATCH)
    line = cell // PATCH
    place = cell % PATCH
    cols = []
    for row_step, col_step in TAPS:
        inside = (line + row_step >= 0) & (line + row_step < PATCH)
        inside = inside & (place + col_step >= 0) & (place + col_step < PATCH)
        cols.append(inside.astype(jnp.float32))
    cols += [jnp.zeros((rows,), jnp.float32)] * (16 - len(cols))
    return jnp.stack(cols, axis=1)


def sig(values):
    return 1.0 / (1.0 + jnp.exp(-values))


def patch_kernel(xin_ref, skip_ref, scale_ref, emb_ref, mask_ref, w1t_ref, w2t_ref, w2_ref,
                 pt_ref, pm_ref, err_ref, sums_ref, g1_ref, g2_ref, gp_ref, cin_ref, cone_ref):
    rows = xin_ref.shape[0]
    groups = sums_ref.shape[0]
    cells = rows // groups
    channels = xin_ref.shape[1]

    @pl.when(pl.program_id(0) == 0)
    def _():
        g1_ref[...] = jnp.zeros_like(g1_ref)
        g2_ref[...] = jnp.zeros_like(g2_ref)
        gp_ref[...] = jnp.zeros_like(gp_ref)

    def stack(values, target):
        for tap, (row_step, col_step) in enumerate(TAPS):
            shift = row_step * PATCH + col_step
            moved = values if shift == 0 else pltpu.roll(values, (-shift) % rows, 0)
            moved = moved * mask_ref[:, tap : tap + 1]
            target[:, tap * channels : (tap + 1) * channels] = moved.astype(target.dtype)

    stack(xin_ref[...].astype(jnp.float32), cin_ref)
    pre_one = jnp.dot(cin_ref[...], w1t_ref[...], preferred_element_type=jnp.float32)
    pre_one = pre_one + emb_ref[...]
    gate_one = sig(pre_one)
    act_one = (pre_one * gate_one).astype(jnp.bfloat16)
    stack(act_one.astype(jnp.float32), cone_ref)
    pre_two = jnp.dot(cone_ref[...], w2t_ref[...], preferred_element_type=jnp.float32)
    gate_two = sig(pre_two)
    act_two = (pre_two * gate_two).astype(jnp.bfloat16)
    output = jnp.dot(act_two, pt_ref[...], preferred_element_type=jnp.float32)
    error = skip_ref[...] + scale_ref[:, 0:1] * output
    err_ref[...] = error
    grad_output = (scale_ref[:, 1:2] * error).astype(jnp.bfloat16)
    contract = (((0,), (0,)), ((), ()))
    gp_ref[...] += lax.dot_general(grad_output, act_two, contract, preferred_element_type=jnp.float32)
    grad_act_two = jnp.dot(grad_output, pm_ref[...], preferred_element_type=jnp.float32)
    slope_two = gate_two * (1.0 + pre_two * (1.0 - gate_two))
    grad_pre_two = (grad_act_two * slope_two).astype(jnp.bfloat16)
    g2_ref[...] += lax.dot_general(grad_pre_two, cone_ref[...], contract, preferred_element_type=jnp.float32)
    grad_act_one = jnp.zeros((rows, channels), jnp.float32)
    for tap, (row_step, col_step) in enumerate(TAPS):
        shift = row_step * PATCH + col_step
        piece = jnp.dot(grad_pre_two, w2_ref[:, tap * channels : (tap + 1) * channels],
                        preferred_element_type=jnp.float32)
        moved = piece if shift == 0 else pltpu.roll(piece, shift % rows, 0)
        grad_act_one = grad_act_one + moved * mask_ref[:, 8 - tap : 9 - tap]
    slope_one = gate_one * (1.0 + pre_one * (1.0 - gate_one))
    grad_pre_one = (grad_act_one * slope_one).astype(jnp.bfloat16)
    g1_ref[...] += lax.dot_general(grad_pre_one, cin_ref[...], contract, preferred_element_type=jnp.float32)
    wide = grad_pre_one.astype(jnp.float32)
    for group in range(groups):
        sums_ref[group : group + 1, :] = jnp.sum(wide[group * cells : (group + 1) * cells], axis=0, keepdims=True)


def patch_pass(xin, skip, scale, emb, conv_one, conv_two, out_proj, group=8, interpret=False):
    rows_all, channels = xin.shape
    cells = PATCH * PATCH
    patches = rows_all // cells
    rows = group * cells
    steps = patches // group
    width = conv_one.shape[1]
    outs = conv_one.shape[0]
    targets = out_proj.shape[0]
    masks = tap_masks(rows)
    block = lambda shape: pl.BlockSpec(shape, lambda i: (i, 0))
    whole = lambda shape: pl.BlockSpec(shape, lambda i: (0, 0))
    return pl.pallas_call(
        patch_kernel,
        grid=(steps,),
        in_specs=[
            block((rows, channels)),
            block((rows, targets)),
            block((rows, 8)),
            block((rows, outs)),
            whole((rows, 16)),
            whole((width, outs)),
            whole((width, outs)),
            whole((outs, width)),
            whole((outs, targets)),
            whole((targets, outs)),
        ],
        out_specs=[
            block((rows, targets)),
            block((group, outs)),
            whole((outs, width)),
            whole((outs, width)),
            whole((targets, outs)),
        ],
        out_shape=[
            jax.ShapeDtypeStruct((rows_all, targets), jnp.float32),
            jax.ShapeDtypeStruct((patches, outs), jnp.float32),
            jax.ShapeDtypeStruct((outs, width), jnp.float32),
            jax.ShapeDtypeStruct((outs, width), jnp.float32),
            jax.ShapeDtypeStruct((targets, outs), jnp.float32),
        ],
        scratch_shapes=[pltpu.VMEM((rows, width), jnp.bfloat16), pltpu.VMEM((rows, width), jnp.bfloat16)],
        compiler_params=pltpu.CompilerParams(dimension_semantics=("arbitrary",)),
        interpret=interpret,
    )(xin, skip, scale, emb, masks, conv_one.T, conv_two.T, conv_two, out_proj.T, out_proj)


def kernel_blocks(mean_part, target_part, noise_part, step_ids, in_use, weights, interpret=False):
    conv_one, conv_two, out_proj, step_embed = weights
    patch_count, targets, cells = mean_part.shape
    level_count = step_embed.shape[0]
    sigma_table = noise_levels(level_count)
    step_hot = (step_ids[:, None] == jnp.arange(level_count, dtype=jnp.int32)[None, :]).astype(
        jnp.float32
    )
    sigma = jnp.sum(step_hot * sigma_table[None, :], axis=1)
    sigma_sq = sigma * sigma + 1.0
    scale_in = (1.0 / jnp.sqrt(sigma_sq))[:, None, None]
    scale_skip = (1.0 / sigma_sq)[:, None, None]
    scale_out = sigma / jnp.sqrt(sigma_sq)
    weight_loss = sigma_sq / (sigma * sigma)
    mean_float = mean_part.astype(jnp.float32)
    residual = target_part.astype(jnp.float32) - mean_float
    noisy = residual + sigma[:, None, None] * noise_part.astype(jnp.float32)
    inputs = jnp.concatenate([scale_in * noisy, mean_float], axis=1).astype(jnp.bfloat16)
    xin = jnp.swapaxes(inputs, 1, 2).reshape(patch_count * cells, 2 * targets)
    skip = jnp.swapaxes(scale_skip * noisy - residual, 1, 2).reshape(patch_count * cells, targets)
    factor = 2.0 * weight_loss * in_use / (targets * cells)
    per_patch = jnp.stack([scale_out, factor * scale_out], axis=1)
    per_patch = jnp.pad(per_patch, ((0, 0), (0, 6)))
    scale = jnp.broadcast_to(per_patch[:, None, :], (patch_count, cells, 8)).reshape(-1, 8)
    embedded = jnp.sum(step_hot[:, :, None] * step_embed[None, :, :], axis=1)
    emb = jnp.broadcast_to(embedded[:, None, :], (patch_count, cells, embedded.shape[1]))
    emb = emb.reshape(patch_count * cells, embedded.shape[1])
    error, pixel_sums, grad_one, grad_two, grad_proj = patch_pass(
        xin, skip, scale, emb, conv_one, conv_two, out_proj, interpret=interpret
    )
    error = error.reshape(patch_count, cells * targets)
    losses = weight_loss * jnp.mean(error * error, axis=1) * in_use
    grad_table = jnp.sum(step_hot[:, :, None] * pixel_sums[:, None, :], axis=0)
    return (losses, (grad_one, grad_two, grad_proj, grad_table))


def owner_tables(region_rows, strips):
    owners = region_rows[:, :, 2]
    owner_hot = (owners[:, :, None] == jnp.arange(strips, dtype=jnp.int32)[None, None, :]).astype(
        jnp.int32
    )
    pair_rank = jnp.sum((jnp.cumsum(owner_hot, axis=1) - owner_hot) * owner_hot, axis=2)
    flat_hot = owner_hot.reshape(-1, strips)
    owner_slot = jnp.sum((jnp.cumsum(flat_hot, axis=0) - flat_hot) * flat_hot, axis=1).reshape(
        owners.shape
    )
    return (owners, pair_rank, owner_slot)


def noise_routes(region_rows, owners, pair_rank, owner_slot, strip_index, capacity):
    hits = (
        (owners == strip_index)[:, :, None]
        & (pair_rank[:, :, None] == jnp.arange(capacity, dtype=jnp.int32)[None, None, :])
    ).astype(jnp.int32)
    return jnp.sum(hits * owner_slot[:, :, None], axis=1)


def exchange_sum(flat, steps):
    spread = 1
    for _, distance in steps:
        spread *= 2
    size = flat.shape[0]
    unit = spread * 8
    padded = (size + unit - 1) // unit * unit
    values = jnp.pad(flat, (0, padded - size))
    places = {axis: lax.axis_index(axis) for axis, _ in steps}
    for axis, distance in steps:
        count = lax.axis_size(axis)
        half = values.shape[0] // 2
        low, high = values[:half], values[half:]
        upper = (places[axis] // distance) % 2 == 1
        route = [(i, i ^ distance) for i in range(count)]
        kept = jnp.where(upper, high, low)
        sent = jnp.where(upper, low, high)
        values = kept + lax.ppermute(sent, axis, route)
    for axis, distance in reversed(steps):
        count = lax.axis_size(axis)
        upper = (places[axis] // distance) % 2 == 1
        route = [(i, i ^ distance) for i in range(count)]
        other = lax.ppermute(values, axis, route)
        values = jnp.where(
            upper, jnp.concatenate([other, values]), jnp.concatenate([values, other])
        )
    return values[:size]


def reduce_steps():
    sizes = {axis: lax.axis_size(axis) for axis in ("segment", "rows", "dp")}
    steps = []
    distance = 1
    while distance < max(sizes.values()):
        for axis in ("segment", "rows", "dp"):
            if distance < sizes[axis]:
                steps.append((axis, distance))
        distance *= 2
    return steps


def cut_patches(source_grid, row_at, col_at, height):
    zero_index = jnp.zeros((), jnp.int32)

    def cut(row_start, col_start):
        piece = lax.dynamic_slice(
            source_grid,
            (zero_index, zero_index, row_start, col_start),
            (2, source_grid.shape[1], height, height),
        )
        return piece.reshape(2, source_grid.shape[1], height * height)

    return jax.vmap(cut)(row_at, col_at)


def per_device(
    coarse, target, noise, regions, reg_conv, reg_out, conv_one, conv_two, out_proj, step_embed
):
    strips = lax.axis_size("rows")
    strip_index = lax.axis_index("rows")
    sample_count = lax.axis_size("segment") * lax.axis_size("dp")
    sample_index = lax.axis_index("segment") * lax.axis_size("dp") + lax.axis_index("dp")
    region_rows = regions[0]
    per_strip = region_rows.shape[1]
    capacity = max(2, (2 * per_strip + strips - 1) // strips)
    weights = (conv_one, conv_two, out_proj, step_embed)
    owners, pair_rank, owner_slot = owner_tables(region_rows, strips)
    send_slot = noise_routes(region_rows, owners, pair_rank, owner_slot, strip_index, capacity)
    outgoing = jnp.take(noise[0, 0], send_slot.reshape(-1), axis=0)
    outgoing = outgoing.reshape((strips, capacity) + outgoing.shape[1:])
    received = lax.all_to_all(outgoing, "rows", split_axis=0, concat_axis=0, tiled=True)
    rimmed = padded_2(coarse, (("rows", 2),), 1)
    mean_strip = regress(rimmed[0], reg_conv, reg_out)[:, 1:-1]
    height = mean_strip.shape[1]
    pair_strip = jnp.stack([mean_strip, target[0]])
    own_regions = lax.dynamic_index_in_dim(region_rows, strip_index, 0, keepdims=False)
    own_pairs = lax.dynamic_index_in_dim(pair_rank, strip_index, 0, keepdims=False)
    below = shifted_2(pair_strip[:, :, : height - 1], "rows", -1)
    extended = jnp.concatenate([pair_strip, below], axis=2)
    patches = cut_patches(extended, own_regions[:, 0], own_regions[:, 1], height)
    flat_recv = received.reshape((strips * capacity,) + received.shape[2:])
    patch_noise = jnp.take(flat_recv, own_regions[:, 2] * capacity + own_pairs, axis=0)
    in_use = jnp.ones((per_strip,), jnp.float32)
    losses, gradients = kernel_blocks(
        patches[:, 0], patches[:, 1], patch_noise, own_regions[:, 3], in_use, weights
    )
    owner_hot = (own_regions[:, 2][:, None] == jnp.arange(strips, dtype=jnp.int32)[None, :])
    owner_part = jnp.sum(owner_hot.astype(jnp.float32) * losses[:, None], axis=0)
    sample_hot = (jnp.arange(sample_count, dtype=jnp.int32) == sample_index).astype(jnp.float32)
    owner_table = sample_hot[:, None] * owner_part[None, :]
    pieces = (gradients[0], gradients[1], gradients[2], gradients[3], owner_table)
    flat = jnp.concatenate([piece.reshape(-1) for piece in pieces])
    summed = exchange_sum(flat, reduce_steps())
    results = []
    offset = 0
    for piece in pieces:
        results.append(summed[offset : offset + piece.size].reshape(piece.shape))
        offset += piece.size
    table = results[4]
    owner_total = lax.dynamic_slice(table, (sample_index, strip_index), (1, 1))
    return (mean_strip[None], owner_total, results[0], results[1], results[2], results[3])


def solution(mesh):
    placed = (
        P(("segment", "dp"), None, "rows", None),
        P(("segment", "dp"), None, "rows", None),
        P(("segment", "dp"), "rows", None, None, None),
        P(("segment", "dp"), None, None, None),
        P(),
        P(),
        P(),
        P(),
        P(),
        P(),
    )
    return jax.shard_map(
        per_device,
        mesh=mesh,
        in_specs=placed,
        out_specs=(
            P(("segment", "dp"), None, "rows", None),
            P(("segment", "dp"), "rows"),
            P(),
            P(),
            P(),
            P(),
        ),
        check_vma=False,
    )
```

```python
import math

import jax
import jax.numpy as jnp
from jax import lax
from jax.experimental import pallas as pl
from jax.experimental.pallas import tpu as pltpu
from jax.sharding import PartitionSpec as P

PATCH = 12


TAPS = ((-1, -1), (-1, 0), (-1, 1), (0, -1), (0, 0), (0, 1), (1, -1), (1, 0), (1, 1))


def padded_2(cells, sides, width):
    for axis, dim in sides:
        count = lax.axis_size(axis)
        ends = count - 1
        head = lax.slice_in_dim(cells, 0, width, axis=dim)
        tail = lax.slice_in_dim(cells, cells.shape[dim] - width, cells.shape[dim], axis=dim)
        cells = jnp.concatenate(
            [
                lax.ppermute(tail, axis, [(i, (i + 1) % count) for i in range(ends)]),
                cells,
                lax.ppermute(head, axis, [((i + 1) % count, i) for i in range(ends)]),
            ],
            axis=dim,
        )
    return cells


def shifted_2(block, axis, distance):
    devices = range(lax.axis_size(axis))
    route = [(i - distance, i) for i in devices if i - distance in devices]
    return lax.ppermute(block, axis, route)


def shifted(values, row_step, col_step, stride):
    length = values.shape[-1]
    margin = stride + 1
    widths = [(0, 0)] * (values.ndim - 1) + [(margin, margin)]
    padded = jnp.pad(values, widths)
    offset = margin + row_step * stride + col_step
    moved = lax.slice_in_dim(padded, offset, offset + length, axis=values.ndim - 1)
    column = jnp.arange(length, dtype=jnp.int32) % stride + col_step
    inside = (column >= 0) & (column < stride)
    return jnp.where(inside, moved, jnp.zeros((), moved.dtype))


def columns(values, stride):
    return jnp.concatenate(
        [shifted(values, row_step, col_step, stride) for row_step, col_step in TAPS], axis=-2
    )


def fold(gradients, stride):
    width = gradients.shape[-2] // 9
    result = jnp.zeros(gradients.shape[:-2] + (width, gradients.shape[-1]), jnp.float32)
    for position, (row_step, col_step) in enumerate(TAPS):
        piece = gradients[..., position * width : (position + 1) * width, :]
        result = result + shifted(piece, -row_step, -col_step, stride)
    return result


def noise_levels(level_count):
    steps_f = jnp.arange(level_count, dtype=jnp.float32)
    return 0.1 * jnp.exp(steps_f * (math.log(100.0) / (level_count - 1)))


def silu_slope(values):
    gate = jax.nn.sigmoid(values)
    return gate * (1.0 + values * (1.0 - gate))


def product(form, left, right):
    return jnp.einsum(form, left, right, preferred_element_type=jnp.float32)


def regress(grid_rows, reg_conv, reg_out):
    channels, height, width = grid_rows.shape
    hidden_count = reg_conv.shape[0]
    kernel = reg_conv.reshape(hidden_count, 3, 3, channels).transpose(0, 3, 1, 2)
    hidden = lax.conv_general_dilated(
        grid_rows[None],
        kernel,
        window_strides=(1, 1),
        padding=((0, 0), (1, 1)),
        dimension_numbers=("NCHW", "OIHW", "NCHW"),
        preferred_element_type=jnp.float32,
    )[0]
    rows = hidden.shape[1]
    activated = jax.nn.silu(hidden).astype(jnp.bfloat16).reshape(hidden_count, rows * width)
    mean_flat = product("co,op->cp", reg_out, activated).astype(jnp.bfloat16)
    return mean_flat.reshape(reg_out.shape[0], rows, width)


def patch_block(mean_part, target_part, noise_part, step_ids, in_use, weights):
    conv_one, conv_two, out_proj, step_embed = weights
    stride = PATCH
    level_count = step_embed.shape[0]
    sigma_table = noise_levels(level_count)
    step_hot = (step_ids[:, None] == jnp.arange(level_count, dtype=jnp.int32)[None, :]).astype(
        jnp.float32
    )
    sigma = jnp.sum(step_hot * sigma_table[None, :], axis=1)
    sigma_sq = sigma * sigma + 1.0
    scale_in = (1.0 / jnp.sqrt(sigma_sq))[:, None, None]
    scale_skip = (1.0 / sigma_sq)[:, None, None]
    scale_out = (sigma / jnp.sqrt(sigma_sq))[:, None, None]
    weight_loss = sigma_sq / (sigma * sigma)
    mean_float = mean_part.astype(jnp.float32)
    residual = target_part.astype(jnp.float32) - mean_float
    noisy = residual + sigma[:, None, None] * noise_part.astype(jnp.float32)
    inputs = jnp.concatenate([scale_in * noisy, mean_float], axis=1).astype(jnp.bfloat16)
    cols_in = columns(inputs, stride)
    embedded = jnp.sum(step_hot[:, :, None] * step_embed[None, :, :], axis=1)
    pre_one = product("ok,bkp->bop", conv_one, cols_in) + embedded[:, :, None]
    act_one = jax.nn.silu(pre_one).astype(jnp.bfloat16)
    cols_one = columns(act_one, stride)
    pre_two = product("ok,bkp->bop", conv_two, cols_one)
    act_two = jax.nn.silu(pre_two).astype(jnp.bfloat16)
    output = product("co,bop->bcp", out_proj, act_two)
    error = scale_skip * noisy + scale_out * output - residual
    losses = weight_loss * jnp.mean(error * error, axis=(1, 2)) * in_use
    factor = 2.0 * weight_loss * in_use / (error.shape[1] * error.shape[2])
    grad_output = (factor[:, None, None] * scale_out * error).astype(jnp.bfloat16)
    grad_proj = product("bcp,bop->co", grad_output, act_two)
    grad_act_two = product("co,bcp->bop", out_proj, grad_output)
    grad_pre_two = (grad_act_two * silu_slope(pre_two)).astype(jnp.bfloat16)
    grad_two = product("bop,bkp->ok", grad_pre_two, cols_one)
    grad_cols = product("ok,bop->bkp", conv_two, grad_pre_two)
    grad_act_one = fold(grad_cols, stride)
    grad_pre_one = (grad_act_one * silu_slope(pre_one)).astype(jnp.bfloat16)
    grad_one = product("bop,bkp->ok", grad_pre_one, cols_in)
    pixel_sums = jnp.sum(grad_pre_one, axis=2, dtype=jnp.float32)
    grad_table = jnp.sum(step_hot[:, :, None] * pixel_sums[:, None, :], axis=0)
    return (losses, (grad_one, grad_two, grad_proj, grad_table))


def run_blocks(mean_part, target_part, noise_part, step_ids, in_use, weights):
    patch_count = mean_part.shape[0]
    blocks = patch_count // 4

    def regroup(values):
        return values.reshape((blocks, 4) + values.shape[1:])

    def advance(running, group_block):
        losses, gradients = patch_block(
            group_block[0], group_block[1], group_block[2], group_block[3], group_block[4], weights
        )
        summed = (
            running[0] + gradients[0],
            running[1] + gradients[1],
            running[2] + gradients[2],
            running[3] + gradients[3],
        )
        return (summed, losses)

    initial = (
        jnp.zeros(weights[0].shape, jnp.float32),
        jnp.zeros(weights[1].shape, jnp.float32),
        jnp.zeros(weights[2].shape, jnp.float32),
        jnp.zeros(weights[3].shape, jnp.float32),
    )
    stacked = (
        regroup(mean_part),
        regroup(target_part),
        regroup(noise_part),
        regroup(step_ids),
        regroup(in_use),
    )
    gradients, losses = lax.scan(advance, initial, stacked)
    return (losses.reshape(patch_count), gradients)


def tap_masks(rows):
    cell = jnp.arange(rows, dtype=jnp.int32) % (PATCH * PATCH)
    line = cell // PATCH
    place = cell % PATCH
    cols = []
    for row_step, col_step in TAPS:
        inside = (line + row_step >= 0) & (line + row_step < PATCH)
        inside = inside & (place + col_step >= 0) & (place + col_step < PATCH)
        cols.append(inside.astype(jnp.float32))
    cols += [jnp.zeros((rows,), jnp.float32)] * (16 - len(cols))
    return jnp.stack(cols, axis=1)


def sig(values):
    return 1.0 / (1.0 + jnp.exp(-values))


def patch_kernel(xin_ref, skip_ref, scale_ref, emb_ref, mask_ref, w1t_ref, w2t_ref, w2_ref,
                 pt_ref, pm_ref, err_ref, sums_ref, g1_ref, g2_ref, gp_ref, cin_ref, cone_ref):
    rows = xin_ref.shape[0]
    groups = sums_ref.shape[0]
    cells = rows // groups
    channels = xin_ref.shape[1]

    @pl.when(pl.program_id(0) == 0)
    def _():
        g1_ref[...] = jnp.zeros_like(g1_ref)
        g2_ref[...] = jnp.zeros_like(g2_ref)
        gp_ref[...] = jnp.zeros_like(gp_ref)

    def stack(values, target):
        for tap, (row_step, col_step) in enumerate(TAPS):
            shift = row_step * PATCH + col_step
            moved = values if shift == 0 else pltpu.roll(values, (-shift) % rows, 0)
            moved = moved * mask_ref[:, tap : tap + 1]
            target[:, tap * channels : (tap + 1) * channels] = moved.astype(target.dtype)

    stack(xin_ref[...].astype(jnp.float32), cin_ref)
    pre_one = jnp.dot(cin_ref[...], w1t_ref[...], preferred_element_type=jnp.float32)
    pre_one = pre_one + emb_ref[...]
    gate_one = sig(pre_one)
    act_one = (pre_one * gate_one).astype(jnp.bfloat16)
    stack(act_one.astype(jnp.float32), cone_ref)
    pre_two = jnp.dot(cone_ref[...], w2t_ref[...], preferred_element_type=jnp.float32)
    gate_two = sig(pre_two)
    act_two = (pre_two * gate_two).astype(jnp.bfloat16)
    output = jnp.dot(act_two, pt_ref[...], preferred_element_type=jnp.float32)
    error = skip_ref[...] + scale_ref[:, 0:1] * output
    err_ref[...] = error
    grad_output = (scale_ref[:, 1:2] * error).astype(jnp.bfloat16)
    contract = (((0,), (0,)), ((), ()))
    gp_ref[...] += lax.dot_general(grad_output, act_two, contract, preferred_element_type=jnp.float32)
    grad_act_two = jnp.dot(grad_output, pm_ref[...], preferred_element_type=jnp.float32)
    slope_two = gate_two * (1.0 + pre_two * (1.0 - gate_two))
    grad_pre_two = (grad_act_two * slope_two).astype(jnp.bfloat16)
    g2_ref[...] += lax.dot_general(grad_pre_two, cone_ref[...], contract, preferred_element_type=jnp.float32)
    grad_act_one = jnp.zeros((rows, channels), jnp.float32)
    for tap, (row_step, col_step) in enumerate(TAPS):
        shift = row_step * PATCH + col_step
        piece = jnp.dot(grad_pre_two, w2_ref[:, tap * channels : (tap + 1) * channels],
                        preferred_element_type=jnp.float32)
        moved = piece if shift == 0 else pltpu.roll(piece, shift % rows, 0)
        grad_act_one = grad_act_one + moved * mask_ref[:, 8 - tap : 9 - tap]
    slope_one = gate_one * (1.0 + pre_one * (1.0 - gate_one))
    grad_pre_one = (grad_act_one * slope_one).astype(jnp.bfloat16)
    g1_ref[...] += lax.dot_general(grad_pre_one, cin_ref[...], contract, preferred_element_type=jnp.float32)
    wide = grad_pre_one.astype(jnp.float32)
    for group in range(groups):
        sums_ref[group : group + 1, :] = jnp.sum(wide[group * cells : (group + 1) * cells], axis=0, keepdims=True)


def patch_pass(xin, skip, scale, emb, conv_one, conv_two, out_proj, group=8, interpret=False):
    rows_all, channels = xin.shape
    cells = PATCH * PATCH
    patches = rows_all // cells
    rows = group * cells
    steps = patches // group
    width = conv_one.shape[1]
    outs = conv_one.shape[0]
    targets = out_proj.shape[0]
    masks = tap_masks(rows)
    block = lambda shape: pl.BlockSpec(shape, lambda i: (i, 0))
    whole = lambda shape: pl.BlockSpec(shape, lambda i: (0, 0))
    return pl.pallas_call(
        patch_kernel,
        grid=(steps,),
        in_specs=[
            block((rows, channels)),
            block((rows, targets)),
            block((rows, 8)),
            block((rows, outs)),
            whole((rows, 16)),
            whole((width, outs)),
            whole((width, outs)),
            whole((outs, width)),
            whole((outs, targets)),
            whole((targets, outs)),
        ],
        out_specs=[
            block((rows, targets)),
            block((group, outs)),
            whole((outs, width)),
            whole((outs, width)),
            whole((targets, outs)),
        ],
        out_shape=[
            jax.ShapeDtypeStruct((rows_all, targets), jnp.float32),
            jax.ShapeDtypeStruct((patches, outs), jnp.float32),
            jax.ShapeDtypeStruct((outs, width), jnp.float32),
            jax.ShapeDtypeStruct((outs, width), jnp.float32),
            jax.ShapeDtypeStruct((targets, outs), jnp.float32),
        ],
        scratch_shapes=[pltpu.VMEM((rows, width), jnp.bfloat16), pltpu.VMEM((rows, width), jnp.bfloat16)],
        compiler_params=pltpu.CompilerParams(dimension_semantics=("arbitrary",)),
        interpret=interpret,
    )(xin, skip, scale, emb, masks, conv_one.T, conv_two.T, conv_two, out_proj.T, out_proj)


def kernel_blocks(mean_part, target_part, noise_part, step_ids, in_use, weights, interpret=False):
    conv_one, conv_two, out_proj, step_embed = weights
    patch_count, targets, cells = mean_part.shape
    level_count = step_embed.shape[0]
    sigma_table = noise_levels(level_count)
    step_hot = (step_ids[:, None] == jnp.arange(level_count, dtype=jnp.int32)[None, :]).astype(
        jnp.float32
    )
    sigma = jnp.sum(step_hot * sigma_table[None, :], axis=1)
    sigma_sq = sigma * sigma + 1.0
    scale_in = (1.0 / jnp.sqrt(sigma_sq))[:, None, None]
    scale_skip = (1.0 / sigma_sq)[:, None, None]
    scale_out = sigma / jnp.sqrt(sigma_sq)
    weight_loss = sigma_sq / (sigma * sigma)
    mean_float = mean_part.astype(jnp.float32)
    residual = target_part.astype(jnp.float32) - mean_float
    noisy = residual + sigma[:, None, None] * noise_part.astype(jnp.float32)
    inputs = jnp.concatenate([scale_in * noisy, mean_float], axis=1).astype(jnp.bfloat16)
    xin = jnp.swapaxes(inputs, 1, 2).reshape(patch_count * cells, 2 * targets)
    skip = jnp.swapaxes(scale_skip * noisy - residual, 1, 2).reshape(patch_count * cells, targets)
    factor = 2.0 * weight_loss * in_use / (targets * cells)
    per_patch = jnp.stack([scale_out, factor * scale_out], axis=1)
    per_patch = jnp.pad(per_patch, ((0, 0), (0, 6)))
    scale = jnp.broadcast_to(per_patch[:, None, :], (patch_count, cells, 8)).reshape(-1, 8)
    embedded = jnp.sum(step_hot[:, :, None] * step_embed[None, :, :], axis=1)
    emb = jnp.broadcast_to(embedded[:, None, :], (patch_count, cells, embedded.shape[1]))
    emb = emb.reshape(patch_count * cells, embedded.shape[1])
    error, pixel_sums, grad_one, grad_two, grad_proj = patch_pass(
        xin, skip, scale, emb, conv_one, conv_two, out_proj, interpret=interpret
    )
    error = error.reshape(patch_count, cells * targets)
    losses = weight_loss * jnp.mean(error * error, axis=1) * in_use
    grad_table = jnp.sum(step_hot[:, :, None] * pixel_sums[:, None, :], axis=0)
    return (losses, (grad_one, grad_two, grad_proj, grad_table))


def owner_tables(region_rows, strip_index):
    owners = region_rows[:, :, 2]
    earlier = (
        jnp.arange(owners.shape[1], dtype=jnp.int32)[None, :, None]
        > jnp.arange(owners.shape[1], dtype=jnp.int32)[None, None, :]
    )
    same = owners[:, :, None] == owners[:, None, :]
    pair_rank = jnp.sum((same & earlier).astype(jnp.int32), axis=2)
    mine = (owners == strip_index).astype(jnp.int32)
    flat = mine.reshape(-1)
    owner_slot = (jnp.cumsum(flat) - flat).reshape(owners.shape)
    return (owners, pair_rank, owner_slot)


def noise_routes(region_rows, owners, pair_rank, owner_slot, strip_index, capacity):
    hits = (
        (owners == strip_index)[:, :, None]
        & (pair_rank[:, :, None] == jnp.arange(capacity, dtype=jnp.int32)[None, None, :])
    ).astype(jnp.int32)
    return jnp.sum(hits * owner_slot[:, :, None], axis=1)


def exchange_sum(flat, steps):
    spread = 1
    for _, distance in steps:
        spread *= 2
    size = flat.shape[0]
    unit = spread * 8
    padded = (size + unit - 1) // unit * unit
    values = jnp.pad(flat, (0, padded - size))
    places = {axis: lax.axis_index(axis) for axis, _ in steps}
    for axis, distance in steps:
        count = lax.axis_size(axis)
        half = values.shape[0] // 2
        low, high = values[:half], values[half:]
        upper = (places[axis] // distance) % 2 == 1
        route = [(i, i ^ distance) for i in range(count)]
        kept = jnp.where(upper, high, low)
        sent = jnp.where(upper, low, high)
        values = kept + lax.ppermute(sent, axis, route)
    for axis, distance in reversed(steps):
        count = lax.axis_size(axis)
        upper = (places[axis] // distance) % 2 == 1
        route = [(i, i ^ distance) for i in range(count)]
        other = lax.ppermute(values, axis, route)
        values = jnp.where(
            upper, jnp.concatenate([other, values]), jnp.concatenate([values, other])
        )
    return values[:size]


def reduce_steps():
    sizes = {axis: lax.axis_size(axis) for axis in ("segment", "rows", "dp")}
    steps = []
    distance = 1
    while distance < max(sizes.values()):
        for axis in ("segment", "rows", "dp"):
            if distance < sizes[axis]:
                steps.append((axis, distance))
        distance *= 2
    return steps


def cut_patches(source_grid, row_at, col_at, height):
    zero_index = jnp.zeros((), jnp.int32)

    def cut(row_start, col_start):
        piece = lax.dynamic_slice(
            source_grid,
            (zero_index, zero_index, row_start, col_start),
            (2, source_grid.shape[1], height, height),
        )
        return piece.reshape(2, source_grid.shape[1], height * height)

    return jax.vmap(cut)(row_at, col_at)


def per_device(
    coarse, target, noise, regions, reg_conv, reg_out, conv_one, conv_two, out_proj, step_embed
):
    strips = lax.axis_size("rows")
    strip_index = lax.axis_index("rows")
    sample_count = lax.axis_size("segment") * lax.axis_size("dp")
    sample_index = lax.axis_index("segment") * lax.axis_size("dp") + lax.axis_index("dp")
    region_rows = regions[0]
    per_strip = region_rows.shape[1]
    capacity = max(2, (2 * per_strip + strips - 1) // strips)
    weights = (conv_one, conv_two, out_proj, step_embed)
    owners, pair_rank, owner_slot = owner_tables(region_rows, strip_index)
    send_slot = noise_routes(region_rows, owners, pair_rank, owner_slot, strip_index, capacity)
    outgoing = jnp.take(noise[0, 0], send_slot.reshape(-1), axis=0)
    outgoing = outgoing.reshape((strips, capacity) + outgoing.shape[1:])
    received = lax.all_to_all(outgoing, "rows", split_axis=0, concat_axis=0, tiled=True)
    rimmed = padded_2(coarse, (("rows", 2),), 1)
    mean_strip = regress(rimmed[0], reg_conv, reg_out)
    height = mean_strip.shape[1]
    pair_strip = jnp.stack([mean_strip, target[0]])
    own_regions = lax.dynamic_index_in_dim(region_rows, strip_index, 0, keepdims=False)
    own_pairs = lax.dynamic_index_in_dim(pair_rank, strip_index, 0, keepdims=False)
    below = shifted_2(pair_strip[:, :, : height - 1], "rows", -1)
    extended = jnp.concatenate([pair_strip, below], axis=2)
    patches = cut_patches(extended, own_regions[:, 0], own_regions[:, 1], height)
    flat_recv = received.reshape((strips * capacity,) + received.shape[2:])
    patch_noise = jnp.take(flat_recv, own_regions[:, 2] * capacity + own_pairs, axis=0)
    in_use = jnp.ones((per_strip,), jnp.float32)
    losses, gradients = kernel_blocks(
        patches[:, 0], patches[:, 1], patch_noise, own_regions[:, 3], in_use, weights
    )
    owner_hot = (own_regions[:, 2][:, None] == jnp.arange(strips, dtype=jnp.int32)[None, :])
    owner_part = jnp.sum(owner_hot.astype(jnp.float32) * losses[:, None], axis=0)
    sample_hot = (jnp.arange(sample_count, dtype=jnp.int32) == sample_index).astype(jnp.float32)
    owner_table = sample_hot[:, None] * owner_part[None, :]
    pieces = (gradients[0], gradients[1], gradients[2], gradients[3], owner_table)
    flat = jnp.concatenate([piece.reshape(-1) for piece in pieces])
    summed = exchange_sum(flat, reduce_steps())
    results = []
    offset = 0
    for piece in pieces:
        results.append(summed[offset : offset + piece.size].reshape(piece.shape))
        offset += piece.size
    table = results[4]
    owner_total = lax.dynamic_slice(table, (sample_index, strip_index), (1, 1))
    return (mean_strip[None], owner_total, results[0], results[1], results[2], results[3])


def solution(mesh):
    placed = (
        P(("segment", "dp"), None, "rows", None),
        P(("segment", "dp"), None, "rows", None),
        P(("segment", "dp"), "rows", None, None, None),
        P(("segment", "dp"), None, None, None),
        P(),
        P(),
        P(),
        P(),
        P(),
        P(),
    )
    return jax.shard_map(
        per_device,
        mesh=mesh,
        in_specs=placed,
        out_specs=(
            P(("segment", "dp"), None, "rows", None),
            P(("segment", "dp"), "rows"),
            P(),
            P(),
            P(),
            P(),
        ),
        check_vma=False,
    )
```

```python
import functools
import math

import jax
import jax.numpy as jnp
from jax import lax
from jax.experimental import pallas as pl
from jax.experimental.pallas import tpu as pltpu
from jax.sharding import PartitionSpec as P

PATCH = 12


TAPS = ((-1, -1), (-1, 0), (-1, 1), (0, -1), (0, 0), (0, 1), (1, -1), (1, 0), (1, 1))


def padded_2(cells, sides, width):
    for axis, dim in sides:
        count = lax.axis_size(axis)
        ends = count - 1
        head = lax.slice_in_dim(cells, 0, width, axis=dim)
        tail = lax.slice_in_dim(cells, cells.shape[dim] - width, cells.shape[dim], axis=dim)
        cells = jnp.concatenate(
            [
                lax.ppermute(tail, axis, [(i, (i + 1) % count) for i in range(ends)]),
                cells,
                lax.ppermute(head, axis, [((i + 1) % count, i) for i in range(ends)]),
            ],
            axis=dim,
        )
    return cells


def shifted_2(block, axis, distance):
    devices = range(lax.axis_size(axis))
    route = [(i - distance, i) for i in devices if i - distance in devices]
    return lax.ppermute(block, axis, route)


def shifted(values, row_step, col_step, stride):
    length = values.shape[-1]
    margin = stride + 1
    widths = [(0, 0)] * (values.ndim - 1) + [(margin, margin)]
    padded = jnp.pad(values, widths)
    offset = margin + row_step * stride + col_step
    moved = lax.slice_in_dim(padded, offset, offset + length, axis=values.ndim - 1)
    column = jnp.arange(length, dtype=jnp.int32) % stride + col_step
    inside = (column >= 0) & (column < stride)
    return jnp.where(inside, moved, jnp.zeros((), moved.dtype))


def columns(values, stride):
    return jnp.concatenate(
        [shifted(values, row_step, col_step, stride) for row_step, col_step in TAPS], axis=-2
    )


def fold(gradients, stride):
    width = gradients.shape[-2] // 9
    result = jnp.zeros(gradients.shape[:-2] + (width, gradients.shape[-1]), jnp.float32)
    for position, (row_step, col_step) in enumerate(TAPS):
        piece = gradients[..., position * width : (position + 1) * width, :]
        result = result + shifted(piece, -row_step, -col_step, stride)
    return result


def noise_levels(level_count):
    steps_f = jnp.arange(level_count, dtype=jnp.float32)
    return 0.1 * jnp.exp(steps_f * (math.log(100.0) / (level_count - 1)))


def silu_slope(values):
    gate = jax.nn.sigmoid(values)
    return gate * (1.0 + values * (1.0 - gate))


def product(form, left, right):
    return jnp.einsum(form, left, right, preferred_element_type=jnp.float32)


def regress(grid_rows, reg_conv, reg_out):
    channels, height, width = grid_rows.shape
    hidden_count = reg_conv.shape[0]
    kernel = reg_conv.reshape(hidden_count, 3, 3, channels).transpose(0, 3, 1, 2)
    hidden = lax.conv_general_dilated(
        grid_rows[None],
        kernel,
        window_strides=(1, 1),
        padding=((0, 0), (1, 1)),
        dimension_numbers=("NCHW", "OIHW", "NCHW"),
        preferred_element_type=jnp.float32,
    )[0]
    rows = hidden.shape[1]
    activated = jax.nn.silu(hidden).astype(jnp.bfloat16).reshape(hidden_count, rows * width)
    mean_flat = product("co,op->cp", reg_out, activated).astype(jnp.bfloat16)
    return mean_flat.reshape(reg_out.shape[0], rows, width)


def patch_block(mean_part, target_part, noise_part, step_ids, in_use, weights):
    conv_one, conv_two, out_proj, step_embed = weights
    stride = PATCH
    level_count = step_embed.shape[0]
    sigma_table = noise_levels(level_count)
    step_hot = (step_ids[:, None] == jnp.arange(level_count, dtype=jnp.int32)[None, :]).astype(
        jnp.float32
    )
    sigma = jnp.sum(step_hot * sigma_table[None, :], axis=1)
    sigma_sq = sigma * sigma + 1.0
    scale_in = (1.0 / jnp.sqrt(sigma_sq))[:, None, None]
    scale_skip = (1.0 / sigma_sq)[:, None, None]
    scale_out = (sigma / jnp.sqrt(sigma_sq))[:, None, None]
    weight_loss = sigma_sq / (sigma * sigma)
    mean_float = mean_part.astype(jnp.float32)
    residual = target_part.astype(jnp.float32) - mean_float
    noisy = residual + sigma[:, None, None] * noise_part.astype(jnp.float32)
    inputs = jnp.concatenate([scale_in * noisy, mean_float], axis=1).astype(jnp.bfloat16)
    cols_in = columns(inputs, stride)
    embedded = jnp.sum(step_hot[:, :, None] * step_embed[None, :, :], axis=1)
    pre_one = product("ok,bkp->bop", conv_one, cols_in) + embedded[:, :, None]
    act_one = jax.nn.silu(pre_one).astype(jnp.bfloat16)
    cols_one = columns(act_one, stride)
    pre_two = product("ok,bkp->bop", conv_two, cols_one)
    act_two = jax.nn.silu(pre_two).astype(jnp.bfloat16)
    output = product("co,bop->bcp", out_proj, act_two)
    error = scale_skip * noisy + scale_out * output - residual
    losses = weight_loss * jnp.mean(error * error, axis=(1, 2)) * in_use
    factor = 2.0 * weight_loss * in_use / (error.shape[1] * error.shape[2])
    grad_output = (factor[:, None, None] * scale_out * error).astype(jnp.bfloat16)
    grad_proj = product("bcp,bop->co", grad_output, act_two)
    grad_act_two = product("co,bcp->bop", out_proj, grad_output)
    grad_pre_two = (grad_act_two * silu_slope(pre_two)).astype(jnp.bfloat16)
    grad_two = product("bop,bkp->ok", grad_pre_two, cols_one)
    grad_cols = product("ok,bop->bkp", conv_two, grad_pre_two)
    grad_act_one = fold(grad_cols, stride)
    grad_pre_one = (grad_act_one * silu_slope(pre_one)).astype(jnp.bfloat16)
    grad_one = product("bop,bkp->ok", grad_pre_one, cols_in)
    pixel_sums = jnp.sum(grad_pre_one, axis=2, dtype=jnp.float32)
    grad_table = jnp.sum(step_hot[:, :, None] * pixel_sums[:, None, :], axis=0)
    return (losses, (grad_one, grad_two, grad_proj, grad_table))


def run_blocks(mean_part, target_part, noise_part, step_ids, in_use, weights):
    patch_count = mean_part.shape[0]
    blocks = patch_count // 4

    def regroup(values):
        return values.reshape((blocks, 4) + values.shape[1:])

    def advance(running, group_block):
        losses, gradients = patch_block(
            group_block[0], group_block[1], group_block[2], group_block[3], group_block[4], weights
        )
        summed = (
            running[0] + gradients[0],
            running[1] + gradients[1],
            running[2] + gradients[2],
            running[3] + gradients[3],
        )
        return (summed, losses)

    initial = (
        jnp.zeros(weights[0].shape, jnp.float32),
        jnp.zeros(weights[1].shape, jnp.float32),
        jnp.zeros(weights[2].shape, jnp.float32),
        jnp.zeros(weights[3].shape, jnp.float32),
    )
    stacked = (
        regroup(mean_part),
        regroup(target_part),
        regroup(noise_part),
        regroup(step_ids),
        regroup(in_use),
    )
    gradients, losses = lax.scan(advance, initial, stacked)
    return (losses.reshape(patch_count), gradients)


def tap_masks(rows):
    cell = jnp.arange(rows, dtype=jnp.int32) % (PATCH * PATCH)
    line = cell // PATCH
    place = cell % PATCH
    cols = []
    for row_step, col_step in TAPS:
        inside = (line + row_step >= 0) & (line + row_step < PATCH)
        inside = inside & (place + col_step >= 0) & (place + col_step < PATCH)
        cols.append(inside.astype(jnp.float32))
    cols += [jnp.zeros((rows,), jnp.float32)] * (16 - len(cols))
    return jnp.stack(cols, axis=1)


def sig(values):
    return 1.0 / (1.0 + jnp.exp(-values))


def patch_kernel(xin_ref, skip_ref, scale_ref, emb_ref, mask_ref, w1t_ref, w2t_ref, w2_ref,
                 pt_ref, pm_ref, err_ref, sums_ref, g1_ref, g2_ref, gp_ref, cin_ref, cone_ref):
    rows = xin_ref.shape[0]
    groups = sums_ref.shape[0]
    cells = rows // groups
    channels = xin_ref.shape[1]

    @pl.when(pl.program_id(0) == 0)
    def _():
        g1_ref[...] = jnp.zeros_like(g1_ref)
        g2_ref[...] = jnp.zeros_like(g2_ref)
        gp_ref[...] = jnp.zeros_like(gp_ref)

    def stack(values, target):
        for tap, (row_step, col_step) in enumerate(TAPS):
            shift = row_step * PATCH + col_step
            moved = values if shift == 0 else pltpu.roll(values, (-shift) % rows, 0)
            moved = moved * mask_ref[:, tap : tap + 1]
            target[:, tap * channels : (tap + 1) * channels] = moved.astype(target.dtype)

    stack(xin_ref[...].astype(jnp.float32), cin_ref)
    pre_one = jnp.dot(cin_ref[...], w1t_ref[...], preferred_element_type=jnp.float32)
    pre_one = pre_one + emb_ref[...]
    gate_one = sig(pre_one)
    act_one = (pre_one * gate_one).astype(jnp.bfloat16)
    stack(act_one.astype(jnp.float32), cone_ref)
    pre_two = jnp.dot(cone_ref[...], w2t_ref[...], preferred_element_type=jnp.float32)
    gate_two = sig(pre_two)
    act_two = (pre_two * gate_two).astype(jnp.bfloat16)
    output = jnp.dot(act_two, pt_ref[...], preferred_element_type=jnp.float32)
    error = skip_ref[...] + scale_ref[:, 0:1] * output
    err_ref[...] = error
    grad_output = (scale_ref[:, 1:2] * error).astype(jnp.bfloat16)
    contract = (((0,), (0,)), ((), ()))
    gp_ref[...] += lax.dot_general(grad_output, act_two, contract, preferred_element_type=jnp.float32)
    grad_act_two = jnp.dot(grad_output, pm_ref[...], preferred_element_type=jnp.float32)
    slope_two = gate_two * (1.0 + pre_two * (1.0 - gate_two))
    grad_pre_two = (grad_act_two * slope_two).astype(jnp.bfloat16)
    g2_ref[...] += lax.dot_general(grad_pre_two, cone_ref[...], contract, preferred_element_type=jnp.float32)
    grad_act_one = jnp.zeros((rows, channels), jnp.float32)
    for tap, (row_step, col_step) in enumerate(TAPS):
        shift = row_step * PATCH + col_step
        piece = jnp.dot(grad_pre_two, w2_ref[:, tap * channels : (tap + 1) * channels],
                        preferred_element_type=jnp.float32)
        moved = piece if shift == 0 else pltpu.roll(piece, shift % rows, 0)
        grad_act_one = grad_act_one + moved * mask_ref[:, 8 - tap : 9 - tap]
    slope_one = gate_one * (1.0 + pre_one * (1.0 - gate_one))
    grad_pre_one = (grad_act_one * slope_one).astype(jnp.bfloat16)
    g1_ref[...] += lax.dot_general(grad_pre_one, cin_ref[...], contract, preferred_element_type=jnp.float32)
    wide = grad_pre_one.astype(jnp.float32)
    for group in range(groups):
        sums_ref[group : group + 1, :] = jnp.sum(wide[group * cells : (group + 1) * cells], axis=0, keepdims=True)


def patch_pass(xin, skip, scale, emb, conv_one, conv_two, out_proj, group=8, interpret=False):
    rows_all, channels = xin.shape
    cells = PATCH * PATCH
    patches = rows_all // cells
    rows = group * cells
    steps = patches // group
    width = conv_one.shape[1]
    outs = conv_one.shape[0]
    targets = out_proj.shape[0]
    masks = tap_masks(rows)
    block = lambda shape: pl.BlockSpec(shape, lambda i: (i, 0))
    whole = lambda shape: pl.BlockSpec(shape, lambda i: (0, 0))
    return pl.pallas_call(
        patch_kernel,
        grid=(steps,),
        in_specs=[
            block((rows, channels)),
            block((rows, targets)),
            block((rows, 8)),
            block((rows, outs)),
            whole((rows, 16)),
            whole((width, outs)),
            whole((width, outs)),
            whole((outs, width)),
            whole((outs, targets)),
            whole((targets, outs)),
        ],
        out_specs=[
            block((rows, targets)),
            block((group, outs)),
            whole((outs, width)),
            whole((outs, width)),
            whole((targets, outs)),
        ],
        out_shape=[
            jax.ShapeDtypeStruct((rows_all, targets), jnp.float32),
            jax.ShapeDtypeStruct((patches, outs), jnp.float32),
            jax.ShapeDtypeStruct((outs, width), jnp.float32),
            jax.ShapeDtypeStruct((outs, width), jnp.float32),
            jax.ShapeDtypeStruct((targets, outs), jnp.float32),
        ],
        scratch_shapes=[pltpu.VMEM((rows, width), jnp.bfloat16), pltpu.VMEM((rows, width), jnp.bfloat16)],
        compiler_params=pltpu.CompilerParams(dimension_semantics=("arbitrary",)),
        interpret=interpret,
    )(xin, skip, scale, emb, masks, conv_one.T, conv_two.T, conv_two, out_proj.T, out_proj)


def kernel_blocks(mean_part, target_part, noise_part, step_ids, in_use, weights, interpret=False):
    conv_one, conv_two, out_proj, step_embed = weights
    patch_count, targets, cells = mean_part.shape
    level_count = step_embed.shape[0]
    sigma_table = noise_levels(level_count)
    step_hot = (step_ids[:, None] == jnp.arange(level_count, dtype=jnp.int32)[None, :]).astype(
        jnp.float32
    )
    sigma = jnp.sum(step_hot * sigma_table[None, :], axis=1)
    sigma_sq = sigma * sigma + 1.0
    scale_in = (1.0 / jnp.sqrt(sigma_sq))[:, None, None]
    scale_skip = (1.0 / sigma_sq)[:, None, None]
    scale_out = sigma / jnp.sqrt(sigma_sq)
    weight_loss = sigma_sq / (sigma * sigma)
    mean_float = mean_part.astype(jnp.float32)
    residual = target_part.astype(jnp.float32) - mean_float
    noisy = residual + sigma[:, None, None] * noise_part.astype(jnp.float32)
    inputs = jnp.concatenate([scale_in * noisy, mean_float], axis=1).astype(jnp.bfloat16)
    xin = jnp.swapaxes(inputs, 1, 2).reshape(patch_count * cells, 2 * targets)
    skip = jnp.swapaxes(scale_skip * noisy - residual, 1, 2).reshape(patch_count * cells, targets)
    factor = 2.0 * weight_loss * in_use / (targets * cells)
    per_patch = jnp.stack([scale_out, factor * scale_out], axis=1)
    per_patch = jnp.pad(per_patch, ((0, 0), (0, 6)))
    scale = jnp.broadcast_to(per_patch[:, None, :], (patch_count, cells, 8)).reshape(-1, 8)
    embedded = jnp.sum(step_hot[:, :, None] * step_embed[None, :, :], axis=1)
    emb = jnp.broadcast_to(embedded[:, None, :], (patch_count, cells, embedded.shape[1]))
    emb = emb.reshape(patch_count * cells, embedded.shape[1])
    error, pixel_sums, grad_one, grad_two, grad_proj = patch_pass(
        xin, skip, scale, emb, conv_one, conv_two, out_proj, interpret=interpret
    )
    error = error.reshape(patch_count, cells * targets)
    losses = weight_loss * jnp.mean(error * error, axis=1) * in_use
    grad_table = jnp.sum(step_hot[:, :, None] * pixel_sums[:, None, :], axis=0)
    return (losses, (grad_one, grad_two, grad_proj, grad_table))


def owner_tables(region_rows, strip_index):
    owners = region_rows[:, :, 2]
    earlier = (
        jnp.arange(owners.shape[1], dtype=jnp.int32)[None, :, None]
        > jnp.arange(owners.shape[1], dtype=jnp.int32)[None, None, :]
    )
    same = owners[:, :, None] == owners[:, None, :]
    pair_rank = jnp.sum((same & earlier).astype(jnp.int32), axis=2)
    mine = (owners == strip_index).astype(jnp.int32)
    flat = mine.reshape(-1)
    owner_slot = (jnp.cumsum(flat) - flat).reshape(owners.shape)
    return (owners, pair_rank, owner_slot)


def noise_routes(region_rows, owners, pair_rank, owner_slot, strip_index, capacity):
    hits = (
        (owners == strip_index)[:, :, None]
        & (pair_rank[:, :, None] == jnp.arange(capacity, dtype=jnp.int32)[None, None, :])
    ).astype(jnp.int32)
    return jnp.sum(hits * owner_slot[:, :, None], axis=1)


def exchange_sum(flat, steps):
    spread = 1
    for _, distance in steps:
        spread *= 2
    size = flat.shape[0]
    unit = spread * 8
    padded = (size + unit - 1) // unit * unit
    values = jnp.pad(flat, (0, padded - size))
    places = {axis: lax.axis_index(axis) for axis, _ in steps}
    for axis, distance in steps:
        count = lax.axis_size(axis)
        half = values.shape[0] // 2
        low, high = values[:half], values[half:]
        upper = (places[axis] // distance) % 2 == 1
        route = [(i, i ^ distance) for i in range(count)]
        kept = jnp.where(upper, high, low)
        sent = jnp.where(upper, low, high)
        values = kept + lax.ppermute(sent, axis, route)
    for axis, distance in reversed(steps):
        count = lax.axis_size(axis)
        upper = (places[axis] // distance) % 2 == 1
        route = [(i, i ^ distance) for i in range(count)]
        other = lax.ppermute(values, axis, route)
        values = jnp.where(
            upper, jnp.concatenate([other, values]), jnp.concatenate([values, other])
        )
    return values[:size]


def reduce_kernel(steps, x_ref, o_ref, other, acc, full, *rest):
    slots = rest[: len(steps)]
    send_sems, recv_sems = rest[len(steps)], rest[len(steps) + 1]
    axes = ("segment", "rows", "dp")
    places = {axis: lax.axis_index(axis) for axis in axes}

    def partner(axis, distance):
        upper = (places[axis] // distance) % 2
        coords = dict(places)
        coords[axis] = places[axis] + distance - 2 * distance * upper
        return tuple(coords[name] for name in axes), upper

    mates = [partner("segment", 1)[0]] + [partner(axis, distance)[0] for axis, distance in steps]
    barrier = pltpu.get_barrier_semaphore()
    for mate in mates:
        pl.semaphore_signal(barrier, inc=1, device_id=mate, device_id_type=pl.DeviceIdType.MESH)
    pl.semaphore_wait(barrier, len(mates))
    total = x_ref.shape[0]
    copy = pltpu.make_async_remote_copy(
        src_ref=x_ref, dst_ref=other, send_sem=send_sems.at[0], recv_sem=recv_sems.at[0],
        device_id=mates[0], device_id_type=pl.DeviceIdType.MESH,
    )
    copy.start()
    copy.wait()
    acc[...] = x_ref[...] + other[...]
    base = 0
    size = total
    for index, (axis, distance) in enumerate(steps):
        mate, upper = partner(axis, distance)
        half = size // 2
        kept = base + upper * half
        sent = base + (1 - upper) * half
        copy = pltpu.make_async_remote_copy(
            src_ref=acc.at[pl.ds(sent, half)], dst_ref=slots[index],
            send_sem=send_sems.at[1 + index], recv_sem=recv_sems.at[1 + index],
            device_id=mate, device_id_type=pl.DeviceIdType.MESH,
        )
        copy.start()
        copy.wait()
        acc[pl.ds(kept, half)] = acc[pl.ds(kept, half)] + slots[index][...]
        base = kept
        size = half
    full[pl.ds(base, size)] = acc[pl.ds(base, size)]
    count = len(steps)
    for index, (axis, distance) in reversed(list(enumerate(steps))):
        mate, upper = partner(axis, distance)
        copy = pltpu.make_async_remote_copy(
            src_ref=full.at[pl.ds(base, size)], dst_ref=full.at[pl.ds(base, size)],
            send_sem=send_sems.at[1 + count + index], recv_sem=recv_sems.at[1 + count + index],
            device_id=mate, device_id_type=pl.DeviceIdType.MESH,
        )
        copy.start()
        copy.wait()
        base = base - upper * size
        size = size * 2
    o_ref[...] = full[...]


def kernel_sum(flat):
    sizes = {axis: lax.axis_size(axis) for axis in ("rows", "dp")}
    steps = []
    distance = 1
    while distance < max(sizes.values()):
        for axis in ("rows", "dp"):
            if distance < sizes[axis]:
                steps.append((axis, distance))
        distance *= 2
    spread = 2 ** len(steps)
    size = flat.shape[0]
    tile = 8 * 128
    tiles = (size + tile * spread - 1) // (tile * spread) * spread
    values = jnp.pad(flat, (0, tiles * tile - size)).reshape(tiles, 8, 128)
    vmem = pl.BlockSpec(memory_space=pltpu.VMEM)
    shapes = [pltpu.VMEM((tiles, 8, 128), jnp.float32)] * 3
    shapes += [pltpu.VMEM((tiles // 2 ** (k + 1), 8, 128), jnp.float32) for k in range(len(steps))]
    shapes += [pltpu.SemaphoreType.DMA((1 + 2 * len(steps),))] * 2
    summed = pl.pallas_call(
        functools.partial(reduce_kernel, tuple(steps)),
        out_shape=jax.ShapeDtypeStruct(values.shape, jnp.float32),
        in_specs=[vmem],
        out_specs=vmem,
        scratch_shapes=shapes,
        compiler_params=pltpu.CompilerParams(collective_id=0, has_side_effects=True),
    )(values)
    return summed.reshape(-1)[:size]


def reduce_steps():
    sizes = {axis: lax.axis_size(axis) for axis in ("segment", "rows", "dp")}
    steps = []
    distance = 1
    while distance < max(sizes.values()):
        for axis in ("segment", "rows", "dp"):
            if distance < sizes[axis]:
                steps.append((axis, distance))
        distance *= 2
    return steps


def cut_patches(source_grid, row_at, col_at, height):
    zero_index = jnp.zeros((), jnp.int32)

    def cut(row_start, col_start):
        piece = lax.dynamic_slice(
            source_grid,
            (zero_index, zero_index, row_start, col_start),
            (2, source_grid.shape[1], height, height),
        )
        return piece.reshape(2, source_grid.shape[1], height * height)

    return jax.vmap(cut)(row_at, col_at)


def per_device(
    coarse, target, noise, regions, reg_conv, reg_out, conv_one, conv_two, out_proj, step_embed
):
    strips = lax.axis_size("rows")
    strip_index = lax.axis_index("rows")
    sample_count = lax.axis_size("segment") * lax.axis_size("dp")
    sample_index = lax.axis_index("segment") * lax.axis_size("dp") + lax.axis_index("dp")
    region_rows = regions[0]
    per_strip = region_rows.shape[1]
    capacity = max(2, (2 * per_strip + strips - 1) // strips)
    weights = (conv_one, conv_two, out_proj, step_embed)
    owners, pair_rank, owner_slot = owner_tables(region_rows, strip_index)
    send_slot = noise_routes(region_rows, owners, pair_rank, owner_slot, strip_index, capacity)
    outgoing = jnp.take(noise[0, 0], send_slot.reshape(-1), axis=0)
    outgoing = outgoing.reshape((strips, capacity) + outgoing.shape[1:])
    received = lax.all_to_all(outgoing, "rows", split_axis=0, concat_axis=0, tiled=True)
    rimmed = padded_2(coarse, (("rows", 2),), 1)
    mean_strip = regress(rimmed[0], reg_conv, reg_out)
    height = mean_strip.shape[1]
    pair_strip = jnp.stack([mean_strip, target[0]])
    own_regions = lax.dynamic_index_in_dim(region_rows, strip_index, 0, keepdims=False)
    own_pairs = lax.dynamic_index_in_dim(pair_rank, strip_index, 0, keepdims=False)
    below = shifted_2(pair_strip[:, :, : height - 1], "rows", -1)
    extended = jnp.concatenate([pair_strip, below], axis=2)
    patches = cut_patches(extended, own_regions[:, 0], own_regions[:, 1], height)
    flat_recv = received.reshape((strips * capacity,) + received.shape[2:])
    patch_noise = jnp.take(flat_recv, own_regions[:, 2] * capacity + own_pairs, axis=0)
    in_use = jnp.ones((per_strip,), jnp.float32)
    losses, gradients = kernel_blocks(
        patches[:, 0], patches[:, 1], patch_noise, own_regions[:, 3], in_use, weights
    )
    owner_hot = (own_regions[:, 2][:, None] == jnp.arange(strips, dtype=jnp.int32)[None, :])
    owner_part = jnp.sum(owner_hot.astype(jnp.float32) * losses[:, None], axis=0)
    sample_hot = (jnp.arange(sample_count, dtype=jnp.int32) == sample_index).astype(jnp.float32)
    owner_table = sample_hot[:, None] * owner_part[None, :]
    pieces = (gradients[0], gradients[1], gradients[2], gradients[3], owner_table)
    flat = jnp.concatenate([piece.reshape(-1) for piece in pieces])
    summed = kernel_sum(flat)
    results = []
    offset = 0
    for piece in pieces:
        results.append(summed[offset : offset + piece.size].reshape(piece.shape))
        offset += piece.size
    table = results[4]
    owner_total = lax.dynamic_slice(table, (sample_index, strip_index), (1, 1))
    return (mean_strip[None], owner_total, results[0], results[1], results[2], results[3])


def solution(mesh):
    placed = (
        P(("segment", "dp"), None, "rows", None),
        P(("segment", "dp"), None, "rows", None),
        P(("segment", "dp"), "rows", None, None, None),
        P(("segment", "dp"), None, None, None),
        P(),
        P(),
        P(),
        P(),
        P(),
        P(),
    )
    return jax.shard_map(
        per_device,
        mesh=mesh,
        in_specs=placed,
        out_specs=(
            P(("segment", "dp"), None, "rows", None),
            P(("segment", "dp"), "rows"),
            P(),
            P(),
            P(),
            P(),
        ),
        check_vma=False,
    )
```

```python
import math

import jax
import jax.numpy as jnp
from jax import lax
from jax.experimental import pallas as pl
from jax.experimental.pallas import tpu as pltpu
from jax.sharding import PartitionSpec as P

PATCH = 12


TAPS = ((-1, -1), (-1, 0), (-1, 1), (0, -1), (0, 0), (0, 1), (1, -1), (1, 0), (1, 1))


def padded_2(cells, sides, width):
    for axis, dim in sides:
        count = lax.axis_size(axis)
        ends = count - 1
        head = lax.slice_in_dim(cells, 0, width, axis=dim)
        tail = lax.slice_in_dim(cells, cells.shape[dim] - width, cells.shape[dim], axis=dim)
        cells = jnp.concatenate(
            [
                lax.ppermute(tail, axis, [(i, (i + 1) % count) for i in range(ends)]),
                cells,
                lax.ppermute(head, axis, [((i + 1) % count, i) for i in range(ends)]),
            ],
            axis=dim,
        )
    return cells


def shifted_2(block, axis, distance):
    devices = range(lax.axis_size(axis))
    route = [(i - distance, i) for i in devices if i - distance in devices]
    return lax.ppermute(block, axis, route)


def shifted(values, row_step, col_step, stride):
    length = values.shape[-1]
    margin = stride + 1
    widths = [(0, 0)] * (values.ndim - 1) + [(margin, margin)]
    padded = jnp.pad(values, widths)
    offset = margin + row_step * stride + col_step
    moved = lax.slice_in_dim(padded, offset, offset + length, axis=values.ndim - 1)
    column = jnp.arange(length, dtype=jnp.int32) % stride + col_step
    inside = (column >= 0) & (column < stride)
    return jnp.where(inside, moved, jnp.zeros((), moved.dtype))


def columns(values, stride):
    return jnp.concatenate(
        [shifted(values, row_step, col_step, stride) for row_step, col_step in TAPS], axis=-2
    )


def fold(gradients, stride):
    width = gradients.shape[-2] // 9
    result = jnp.zeros(gradients.shape[:-2] + (width, gradients.shape[-1]), jnp.float32)
    for position, (row_step, col_step) in enumerate(TAPS):
        piece = gradients[..., position * width : (position + 1) * width, :]
        result = result + shifted(piece, -row_step, -col_step, stride)
    return result


def noise_levels(level_count):
    steps_f = jnp.arange(level_count, dtype=jnp.float32)
    return 0.1 * jnp.exp(steps_f * (math.log(100.0) / (level_count - 1)))


def silu_slope(values):
    gate = jax.nn.sigmoid(values)
    return gate * (1.0 + values * (1.0 - gate))


def product(form, left, right):
    return jnp.einsum(form, left, right, preferred_element_type=jnp.float32)


def regress(grid_rows, reg_conv, reg_out):
    channels, height, width = grid_rows.shape
    hidden_count = reg_conv.shape[0]
    kernel = reg_conv.reshape(hidden_count, 3, 3, channels).transpose(1, 2, 3, 0)
    hidden = lax.conv_general_dilated(
        grid_rows[None],
        kernel,
        window_strides=(1, 1),
        padding=((0, 0), (1, 1)),
        dimension_numbers=("NCHW", "HWIO", "NHWC"),
        preferred_element_type=jnp.float32,
    )[0]
    activated = jax.nn.silu(hidden).astype(jnp.bfloat16)
    return product("rqo,co->rqc", activated, reg_out).astype(jnp.bfloat16)


def patch_block(mean_part, target_part, noise_part, step_ids, in_use, weights):
    conv_one, conv_two, out_proj, step_embed = weights
    stride = PATCH
    level_count = step_embed.shape[0]
    sigma_table = noise_levels(level_count)
    step_hot = (step_ids[:, None] == jnp.arange(level_count, dtype=jnp.int32)[None, :]).astype(
        jnp.float32
    )
    sigma = jnp.sum(step_hot * sigma_table[None, :], axis=1)
    sigma_sq = sigma * sigma + 1.0
    scale_in = (1.0 / jnp.sqrt(sigma_sq))[:, None, None]
    scale_skip = (1.0 / sigma_sq)[:, None, None]
    scale_out = (sigma / jnp.sqrt(sigma_sq))[:, None, None]
    weight_loss = sigma_sq / (sigma * sigma)
    mean_float = mean_part.astype(jnp.float32)
    residual = target_part.astype(jnp.float32) - mean_float
    noisy = residual + sigma[:, None, None] * noise_part.astype(jnp.float32)
    inputs = jnp.concatenate([scale_in * noisy, mean_float], axis=1).astype(jnp.bfloat16)
    cols_in = columns(inputs, stride)
    embedded = jnp.sum(step_hot[:, :, None] * step_embed[None, :, :], axis=1)
    pre_one = product("ok,bkp->bop", conv_one, cols_in) + embedded[:, :, None]
    act_one = jax.nn.silu(pre_one).astype(jnp.bfloat16)
    cols_one = columns(act_one, stride)
    pre_two = product("ok,bkp->bop", conv_two, cols_one)
    act_two = jax.nn.silu(pre_two).astype(jnp.bfloat16)
    output = product("co,bop->bcp", out_proj, act_two)
    error = scale_skip * noisy + scale_out * output - residual
    losses = weight_loss * jnp.mean(error * error, axis=(1, 2)) * in_use
    factor = 2.0 * weight_loss * in_use / (error.shape[1] * error.shape[2])
    grad_output = (factor[:, None, None] * scale_out * error).astype(jnp.bfloat16)
    grad_proj = product("bcp,bop->co", grad_output, act_two)
    grad_act_two = product("co,bcp->bop", out_proj, grad_output)
    grad_pre_two = (grad_act_two * silu_slope(pre_two)).astype(jnp.bfloat16)
    grad_two = product("bop,bkp->ok", grad_pre_two, cols_one)
    grad_cols = product("ok,bop->bkp", conv_two, grad_pre_two)
    grad_act_one = fold(grad_cols, stride)
    grad_pre_one = (grad_act_one * silu_slope(pre_one)).astype(jnp.bfloat16)
    grad_one = product("bop,bkp->ok", grad_pre_one, cols_in)
    pixel_sums = jnp.sum(grad_pre_one, axis=2, dtype=jnp.float32)
    grad_table = jnp.sum(step_hot[:, :, None] * pixel_sums[:, None, :], axis=0)
    return (losses, (grad_one, grad_two, grad_proj, grad_table))


def run_blocks(mean_part, target_part, noise_part, step_ids, in_use, weights):
    patch_count = mean_part.shape[0]
    blocks = patch_count // 4

    def regroup(values):
        return values.reshape((blocks, 4) + values.shape[1:])

    def advance(running, group_block):
        losses, gradients = patch_block(
            group_block[0], group_block[1], group_block[2], group_block[3], group_block[4], weights
        )
        summed = (
            running[0] + gradients[0],
            running[1] + gradients[1],
            running[2] + gradients[2],
            running[3] + gradients[3],
        )
        return (summed, losses)

    initial = (
        jnp.zeros(weights[0].shape, jnp.float32),
        jnp.zeros(weights[1].shape, jnp.float32),
        jnp.zeros(weights[2].shape, jnp.float32),
        jnp.zeros(weights[3].shape, jnp.float32),
    )
    stacked = (
        regroup(mean_part),
        regroup(target_part),
        regroup(noise_part),
        regroup(step_ids),
        regroup(in_use),
    )
    gradients, losses = lax.scan(advance, initial, stacked)
    return (losses.reshape(patch_count), gradients)


def tap_masks(rows):
    cell = jnp.arange(rows, dtype=jnp.int32) % (PATCH * PATCH)
    line = cell // PATCH
    place = cell % PATCH
    cols = []
    for row_step, col_step in TAPS:
        inside = (line + row_step >= 0) & (line + row_step < PATCH)
        inside = inside & (place + col_step >= 0) & (place + col_step < PATCH)
        cols.append(inside.astype(jnp.float32))
    cols += [jnp.zeros((rows,), jnp.float32)] * (16 - len(cols))
    return jnp.stack(cols, axis=1)


def sig(values):
    return 1.0 / (1.0 + jnp.exp(-values))


def patch_kernel(xin_ref, skip_ref, scale_ref, emb_ref, mask_ref, w1t_ref, w2t_ref, w2_ref,
                 pt_ref, pm_ref, err_ref, sums_ref, g1_ref, g2_ref, gp_ref, cin_ref, cone_ref):
    rows = xin_ref.shape[0]
    groups = sums_ref.shape[0]
    cells = rows // groups
    channels = xin_ref.shape[1]

    @pl.when(pl.program_id(0) == 0)
    def _():
        g1_ref[...] = jnp.zeros_like(g1_ref)
        g2_ref[...] = jnp.zeros_like(g2_ref)
        gp_ref[...] = jnp.zeros_like(gp_ref)

    def stack(values, target):
        for tap, (row_step, col_step) in enumerate(TAPS):
            shift = row_step * PATCH + col_step
            moved = values if shift == 0 else pltpu.roll(values, (-shift) % rows, 0)
            moved = moved * mask_ref[:, tap : tap + 1]
            target[:, tap * channels : (tap + 1) * channels] = moved.astype(target.dtype)

    stack(xin_ref[...].astype(jnp.float32), cin_ref)
    pre_one = jnp.dot(cin_ref[...], w1t_ref[...], preferred_element_type=jnp.float32)
    pre_one = pre_one + emb_ref[...]
    gate_one = sig(pre_one)
    act_one = (pre_one * gate_one).astype(jnp.bfloat16)
    stack(act_one.astype(jnp.float32), cone_ref)
    pre_two = jnp.dot(cone_ref[...], w2t_ref[...], preferred_element_type=jnp.float32)
    gate_two = sig(pre_two)
    act_two = (pre_two * gate_two).astype(jnp.bfloat16)
    output = jnp.dot(act_two, pt_ref[...], preferred_element_type=jnp.float32)
    error = skip_ref[...] + scale_ref[:, 0:1] * output
    err_ref[...] = error
    grad_output = (scale_ref[:, 1:2] * error).astype(jnp.bfloat16)
    contract = (((0,), (0,)), ((), ()))
    gp_ref[...] += lax.dot_general(grad_output, act_two, contract, preferred_element_type=jnp.float32)
    grad_act_two = jnp.dot(grad_output, pm_ref[...], preferred_element_type=jnp.float32)
    slope_two = gate_two * (1.0 + pre_two * (1.0 - gate_two))
    grad_pre_two = (grad_act_two * slope_two).astype(jnp.bfloat16)
    g2_ref[...] += lax.dot_general(grad_pre_two, cone_ref[...], contract, preferred_element_type=jnp.float32)
    grad_act_one = jnp.zeros((rows, channels), jnp.float32)
    for tap, (row_step, col_step) in enumerate(TAPS):
        shift = row_step * PATCH + col_step
        piece = jnp.dot(grad_pre_two, w2_ref[:, tap * channels : (tap + 1) * channels],
                        preferred_element_type=jnp.float32)
        moved = piece if shift == 0 else pltpu.roll(piece, shift % rows, 0)
        grad_act_one = grad_act_one + moved * mask_ref[:, 8 - tap : 9 - tap]
    slope_one = gate_one * (1.0 + pre_one * (1.0 - gate_one))
    grad_pre_one = (grad_act_one * slope_one).astype(jnp.bfloat16)
    g1_ref[...] += lax.dot_general(grad_pre_one, cin_ref[...], contract, preferred_element_type=jnp.float32)
    wide = grad_pre_one.astype(jnp.float32)
    for group in range(groups):
        sums_ref[group : group + 1, :] = jnp.sum(wide[group * cells : (group + 1) * cells], axis=0, keepdims=True)


def patch_pass(xin, skip, scale, emb, conv_one, conv_two, out_proj, group=8, interpret=False):
    rows_all, channels = xin.shape
    cells = PATCH * PATCH
    patches = rows_all // cells
    rows = group * cells
    steps = patches // group
    width = conv_one.shape[1]
    outs = conv_one.shape[0]
    targets = out_proj.shape[0]
    masks = tap_masks(rows)
    block = lambda shape: pl.BlockSpec(shape, lambda i: (i, 0))
    whole = lambda shape: pl.BlockSpec(shape, lambda i: (0, 0))
    return pl.pallas_call(
        patch_kernel,
        grid=(steps,),
        in_specs=[
            block((rows, channels)),
            block((rows, targets)),
            block((rows, 8)),
            block((rows, outs)),
            whole((rows, 16)),
            whole((width, outs)),
            whole((width, outs)),
            whole((outs, width)),
            whole((outs, targets)),
            whole((targets, outs)),
        ],
        out_specs=[
            block((rows, targets)),
            block((group, outs)),
            whole((outs, width)),
            whole((outs, width)),
            whole((targets, outs)),
        ],
        out_shape=[
            jax.ShapeDtypeStruct((rows_all, targets), jnp.float32),
            jax.ShapeDtypeStruct((patches, outs), jnp.float32),
            jax.ShapeDtypeStruct((outs, width), jnp.float32),
            jax.ShapeDtypeStruct((outs, width), jnp.float32),
            jax.ShapeDtypeStruct((targets, outs), jnp.float32),
        ],
        scratch_shapes=[pltpu.VMEM((rows, width), jnp.bfloat16), pltpu.VMEM((rows, width), jnp.bfloat16)],
        compiler_params=pltpu.CompilerParams(dimension_semantics=("arbitrary",)),
        interpret=interpret,
    )(xin, skip, scale, emb, masks, conv_one.T, conv_two.T, conv_two, out_proj.T, out_proj)


def kernel_blocks(mean_part, target_part, noise_part, step_ids, in_use, weights, interpret=False):
    conv_one, conv_two, out_proj, step_embed = weights
    patch_count, cells, targets = mean_part.shape
    level_count = step_embed.shape[0]
    sigma_table = noise_levels(level_count)
    step_hot = (step_ids[:, None] == jnp.arange(level_count, dtype=jnp.int32)[None, :]).astype(
        jnp.float32
    )
    sigma = jnp.sum(step_hot * sigma_table[None, :], axis=1)
    sigma_sq = sigma * sigma + 1.0
    scale_in = (1.0 / jnp.sqrt(sigma_sq))[:, None, None]
    scale_skip = (1.0 / sigma_sq)[:, None, None]
    scale_out = sigma / jnp.sqrt(sigma_sq)
    weight_loss = sigma_sq / (sigma * sigma)
    mean_float = mean_part.astype(jnp.float32)
    residual = target_part.astype(jnp.float32) - mean_float
    noisy = residual + sigma[:, None, None] * noise_part.astype(jnp.float32)
    inputs = jnp.concatenate([scale_in * noisy, mean_float], axis=2).astype(jnp.bfloat16)
    xin = inputs.reshape(patch_count * cells, 2 * targets)
    skip = (scale_skip * noisy - residual).reshape(patch_count * cells, targets)
    factor = 2.0 * weight_loss * in_use / (targets * cells)
    per_patch = jnp.stack([scale_out, factor * scale_out], axis=1)
    per_patch = jnp.pad(per_patch, ((0, 0), (0, 6)))
    scale = jnp.broadcast_to(per_patch[:, None, :], (patch_count, cells, 8)).reshape(-1, 8)
    embedded = jnp.sum(step_hot[:, :, None] * step_embed[None, :, :], axis=1)
    emb = jnp.broadcast_to(embedded[:, None, :], (patch_count, cells, embedded.shape[1]))
    emb = emb.reshape(patch_count * cells, embedded.shape[1])
    error, pixel_sums, grad_one, grad_two, grad_proj = patch_pass(
        xin, skip, scale, emb, conv_one, conv_two, out_proj, interpret=interpret
    )
    error = error.reshape(patch_count, cells * targets)
    losses = weight_loss * jnp.mean(error * error, axis=1) * in_use
    grad_table = jnp.sum(step_hot[:, :, None] * pixel_sums[:, None, :], axis=0)
    return (losses, (grad_one, grad_two, grad_proj, grad_table))


def owner_tables(region_rows, strip_index):
    owners = region_rows[:, :, 2]
    earlier = (
        jnp.arange(owners.shape[1], dtype=jnp.int32)[None, :, None]
        > jnp.arange(owners.shape[1], dtype=jnp.int32)[None, None, :]
    )
    same = owners[:, :, None] == owners[:, None, :]
    pair_rank = jnp.sum((same & earlier).astype(jnp.int32), axis=2)
    mine = (owners == strip_index).astype(jnp.int32)
    flat = mine.reshape(-1)
    owner_slot = (jnp.cumsum(flat) - flat).reshape(owners.shape)
    return (owners, pair_rank, owner_slot)


def noise_routes(region_rows, owners, pair_rank, owner_slot, strip_index, capacity):
    hits = (
        (owners == strip_index)[:, :, None]
        & (pair_rank[:, :, None] == jnp.arange(capacity, dtype=jnp.int32)[None, None, :])
    ).astype(jnp.int32)
    return jnp.sum(hits * owner_slot[:, :, None], axis=1)


def exchange_sum(flat, steps):
    spread = 1
    for _, distance in steps:
        spread *= 2
    size = flat.shape[0]
    unit = spread * 8
    padded = (size + unit - 1) // unit * unit
    values = jnp.pad(flat, (0, padded - size))
    places = {axis: lax.axis_index(axis) for axis, _ in steps}
    for axis, distance in steps:
        count = lax.axis_size(axis)
        half = values.shape[0] // 2
        low, high = values[:half], values[half:]
        upper = (places[axis] // distance) % 2 == 1
        route = [(i, i ^ distance) for i in range(count)]
        kept = jnp.where(upper, high, low)
        sent = jnp.where(upper, low, high)
        values = kept + lax.ppermute(sent, axis, route)
    for axis, distance in reversed(steps):
        count = lax.axis_size(axis)
        upper = (places[axis] // distance) % 2 == 1
        route = [(i, i ^ distance) for i in range(count)]
        other = lax.ppermute(values, axis, route)
        values = jnp.where(
            upper, jnp.concatenate([other, values]), jnp.concatenate([values, other])
        )
    return values[:size]


def reduce_steps():
    sizes = {axis: lax.axis_size(axis) for axis in ("segment", "rows", "dp")}
    steps = []
    distance = 1
    while distance < max(sizes.values()):
        for axis in ("segment", "rows", "dp"):
            if distance < sizes[axis]:
                steps.append((axis, distance))
        distance *= 2
    return steps


def cut_patches(source_grid, row_at, col_at, height):
    zero_index = jnp.zeros((), jnp.int32)

    def cut(row_start, col_start):
        piece = lax.dynamic_slice(
            source_grid,
            (zero_index, zero_index, row_start, col_start),
            (2, source_grid.shape[1], height, height),
        )
        return piece.reshape(2, source_grid.shape[1], height * height)

    return jax.vmap(cut)(row_at, col_at)


def per_device(
    coarse, target, noise, regions, reg_conv, reg_out, conv_one, conv_two, out_proj, step_embed
):
    strips = lax.axis_size("rows")
    strip_index = lax.axis_index("rows")
    sample_count = lax.axis_size("segment") * lax.axis_size("dp")
    sample_index = lax.axis_index("segment") * lax.axis_size("dp") + lax.axis_index("dp")
    region_rows = regions[0]
    per_strip = region_rows.shape[1]
    capacity = max(2, (2 * per_strip + strips - 1) // strips)
    weights = (conv_one, conv_two, out_proj, step_embed)
    owners, pair_rank, owner_slot = owner_tables(region_rows, strip_index)
    send_slot = noise_routes(region_rows, owners, pair_rank, owner_slot, strip_index, capacity)
    outgoing = jnp.take(noise[0, 0], send_slot.reshape(-1), axis=0)
    outgoing = outgoing.reshape((strips, capacity) + outgoing.shape[1:])
    received = lax.all_to_all(outgoing, "rows", split_axis=0, concat_axis=0, tiled=True)
    rimmed = padded_2(coarse, (("rows", 2),), 1)
    mean_cells = regress(rimmed[0], reg_conv, reg_out)
    height = mean_cells.shape[0]
    mean_strip = jnp.transpose(mean_cells, (2, 0, 1))
    pair_strip = jnp.concatenate([mean_cells, jnp.transpose(target[0], (1, 2, 0))], axis=2)
    own_regions = lax.dynamic_index_in_dim(region_rows, strip_index, 0, keepdims=False)
    own_pairs = lax.dynamic_index_in_dim(pair_rank, strip_index, 0, keepdims=False)
    below = shifted_2(pair_strip[: height - 1], "rows", -1)
    extended = jnp.concatenate([pair_strip, below], axis=0)
    zero_index = jnp.zeros((), jnp.int32)

    def cut(row_start, col_start):
        piece = lax.dynamic_slice(
            extended, (row_start, col_start, zero_index), (height, height, extended.shape[2])
        )
        return piece.reshape(height * height, extended.shape[2])

    patches = jax.vmap(cut)(own_regions[:, 0], own_regions[:, 1])
    targets = mean_cells.shape[2]
    flat_recv = received.reshape((strips * capacity,) + received.shape[2:])
    patch_noise = jnp.take(flat_recv, own_regions[:, 2] * capacity + own_pairs, axis=0)
    patch_noise = jnp.swapaxes(patch_noise, 1, 2)
    in_use = jnp.ones((per_strip,), jnp.float32)
    losses, gradients = kernel_blocks(
        patches[:, :, :targets], patches[:, :, targets:], patch_noise, own_regions[:, 3], in_use,
        weights,
    )
    owner_hot = (own_regions[:, 2][:, None] == jnp.arange(strips, dtype=jnp.int32)[None, :])
    owner_part = jnp.sum(owner_hot.astype(jnp.float32) * losses[:, None], axis=0)
    sample_hot = (jnp.arange(sample_count, dtype=jnp.int32) == sample_index).astype(jnp.float32)
    owner_table = sample_hot[:, None] * owner_part[None, :]
    pieces = (gradients[0], gradients[1], gradients[2], gradients[3], owner_table)
    flat = jnp.concatenate([piece.reshape(-1) for piece in pieces])
    summed = exchange_sum(flat, reduce_steps())
    results = []
    offset = 0
    for piece in pieces:
        results.append(summed[offset : offset + piece.size].reshape(piece.shape))
        offset += piece.size
    table = results[4]
    owner_total = lax.dynamic_slice(table, (sample_index, strip_index), (1, 1))
    return (mean_strip[None], owner_total, results[0], results[1], results[2], results[3])


def solution(mesh):
    placed = (
        P(("segment", "dp"), None, "rows", None),
        P(("segment", "dp"), None, "rows", None),
        P(("segment", "dp"), "rows", None, None, None),
        P(("segment", "dp"), None, None, None),
        P(),
        P(),
        P(),
        P(),
        P(),
        P(),
    )
    return jax.shard_map(
        per_device,
        mesh=mesh,
        in_specs=placed,
        out_specs=(
            P(("segment", "dp"), None, "rows", None),
            P(("segment", "dp"), "rows"),
            P(),
            P(),
            P(),
            P(),
        ),
        check_vma=False,
    )
```

```python
import math

import jax
import jax.numpy as jnp
from jax import lax
from jax.experimental import pallas as pl
from jax.experimental.pallas import tpu as pltpu
from jax.sharding import PartitionSpec as P

PATCH = 12


TAPS = ((-1, -1), (-1, 0), (-1, 1), (0, -1), (0, 0), (0, 1), (1, -1), (1, 0), (1, 1))


def padded_2(cells, sides, width):
    for axis, dim in sides:
        count = lax.axis_size(axis)
        ends = count - 1
        head = lax.slice_in_dim(cells, 0, width, axis=dim)
        tail = lax.slice_in_dim(cells, cells.shape[dim] - width, cells.shape[dim], axis=dim)
        cells = jnp.concatenate(
            [
                lax.ppermute(tail, axis, [(i, (i + 1) % count) for i in range(ends)]),
                cells,
                lax.ppermute(head, axis, [((i + 1) % count, i) for i in range(ends)]),
            ],
            axis=dim,
        )
    return cells


def shifted_2(block, axis, distance):
    devices = range(lax.axis_size(axis))
    route = [(i - distance, i) for i in devices if i - distance in devices]
    return lax.ppermute(block, axis, route)


def shifted(values, row_step, col_step, stride):
    length = values.shape[-1]
    margin = stride + 1
    widths = [(0, 0)] * (values.ndim - 1) + [(margin, margin)]
    padded = jnp.pad(values, widths)
    offset = margin + row_step * stride + col_step
    moved = lax.slice_in_dim(padded, offset, offset + length, axis=values.ndim - 1)
    column = jnp.arange(length, dtype=jnp.int32) % stride + col_step
    inside = (column >= 0) & (column < stride)
    return jnp.where(inside, moved, jnp.zeros((), moved.dtype))


def columns(values, stride):
    return jnp.concatenate(
        [shifted(values, row_step, col_step, stride) for row_step, col_step in TAPS], axis=-2
    )


def fold(gradients, stride):
    width = gradients.shape[-2] // 9
    result = jnp.zeros(gradients.shape[:-2] + (width, gradients.shape[-1]), jnp.float32)
    for position, (row_step, col_step) in enumerate(TAPS):
        piece = gradients[..., position * width : (position + 1) * width, :]
        result = result + shifted(piece, -row_step, -col_step, stride)
    return result


def noise_levels(level_count):
    steps_f = jnp.arange(level_count, dtype=jnp.float32)
    return 0.1 * jnp.exp(steps_f * (math.log(100.0) / (level_count - 1)))


def silu_slope(values):
    gate = jax.nn.sigmoid(values)
    return gate * (1.0 + values * (1.0 - gate))


def product(form, left, right):
    return jnp.einsum(form, left, right, preferred_element_type=jnp.float32)


def regress(grid_rows, reg_conv, reg_out):
    channels, height, width = grid_rows.shape
    hidden_count = reg_conv.shape[0]
    kernel = reg_conv.reshape(hidden_count, 3, 3, channels).transpose(1, 2, 3, 0)
    hidden = lax.conv_general_dilated(
        grid_rows[None],
        kernel,
        window_strides=(1, 1),
        padding=((0, 0), (1, 1)),
        dimension_numbers=("NCHW", "HWIO", "NHWC"),
        preferred_element_type=jnp.float32,
    )[0]
    activated = jax.nn.silu(hidden).astype(jnp.bfloat16)
    return product("rqo,co->rqc", activated, reg_out).astype(jnp.bfloat16)


def patch_block(mean_part, target_part, noise_part, step_ids, in_use, weights):
    conv_one, conv_two, out_proj, step_embed = weights
    stride = PATCH
    level_count = step_embed.shape[0]
    sigma_table = noise_levels(level_count)
    step_hot = (step_ids[:, None] == jnp.arange(level_count, dtype=jnp.int32)[None, :]).astype(
        jnp.float32
    )
    sigma = jnp.sum(step_hot * sigma_table[None, :], axis=1)
    sigma_sq = sigma * sigma + 1.0
    scale_in = (1.0 / jnp.sqrt(sigma_sq))[:, None, None]
    scale_skip = (1.0 / sigma_sq)[:, None, None]
    scale_out = (sigma / jnp.sqrt(sigma_sq))[:, None, None]
    weight_loss = sigma_sq / (sigma * sigma)
    mean_float = mean_part.astype(jnp.float32)
    residual = target_part.astype(jnp.float32) - mean_float
    noisy = residual + sigma[:, None, None] * noise_part.astype(jnp.float32)
    inputs = jnp.concatenate([scale_in * noisy, mean_float], axis=1).astype(jnp.bfloat16)
    cols_in = columns(inputs, stride)
    embedded = jnp.sum(step_hot[:, :, None] * step_embed[None, :, :], axis=1)
    pre_one = product("ok,bkp->bop", conv_one, cols_in) + embedded[:, :, None]
    act_one = jax.nn.silu(pre_one).astype(jnp.bfloat16)
    cols_one = columns(act_one, stride)
    pre_two = product("ok,bkp->bop", conv_two, cols_one)
    act_two = jax.nn.silu(pre_two).astype(jnp.bfloat16)
    output = product("co,bop->bcp", out_proj, act_two)
    error = scale_skip * noisy + scale_out * output - residual
    losses = weight_loss * jnp.mean(error * error, axis=(1, 2)) * in_use
    factor = 2.0 * weight_loss * in_use / (error.shape[1] * error.shape[2])
    grad_output = (factor[:, None, None] * scale_out * error).astype(jnp.bfloat16)
    grad_proj = product("bcp,bop->co", grad_output, act_two)
    grad_act_two = product("co,bcp->bop", out_proj, grad_output)
    grad_pre_two = (grad_act_two * silu_slope(pre_two)).astype(jnp.bfloat16)
    grad_two = product("bop,bkp->ok", grad_pre_two, cols_one)
    grad_cols = product("ok,bop->bkp", conv_two, grad_pre_two)
    grad_act_one = fold(grad_cols, stride)
    grad_pre_one = (grad_act_one * silu_slope(pre_one)).astype(jnp.bfloat16)
    grad_one = product("bop,bkp->ok", grad_pre_one, cols_in)
    pixel_sums = jnp.sum(grad_pre_one, axis=2, dtype=jnp.float32)
    grad_table = jnp.sum(step_hot[:, :, None] * pixel_sums[:, None, :], axis=0)
    return (losses, (grad_one, grad_two, grad_proj, grad_table))


def run_blocks(mean_part, target_part, noise_part, step_ids, in_use, weights):
    patch_count = mean_part.shape[0]
    blocks = patch_count // 4

    def regroup(values):
        return values.reshape((blocks, 4) + values.shape[1:])

    def advance(running, group_block):
        losses, gradients = patch_block(
            group_block[0], group_block[1], group_block[2], group_block[3], group_block[4], weights
        )
        summed = (
            running[0] + gradients[0],
            running[1] + gradients[1],
            running[2] + gradients[2],
            running[3] + gradients[3],
        )
        return (summed, losses)

    initial = (
        jnp.zeros(weights[0].shape, jnp.float32),
        jnp.zeros(weights[1].shape, jnp.float32),
        jnp.zeros(weights[2].shape, jnp.float32),
        jnp.zeros(weights[3].shape, jnp.float32),
    )
    stacked = (
        regroup(mean_part),
        regroup(target_part),
        regroup(noise_part),
        regroup(step_ids),
        regroup(in_use),
    )
    gradients, losses = lax.scan(advance, initial, stacked)
    return (losses.reshape(patch_count), gradients)


def tap_masks(rows):
    cell = jnp.arange(rows, dtype=jnp.int32) % (PATCH * PATCH)
    line = cell // PATCH
    place = cell % PATCH
    cols = []
    for row_step, col_step in TAPS:
        inside = (line + row_step >= 0) & (line + row_step < PATCH)
        inside = inside & (place + col_step >= 0) & (place + col_step < PATCH)
        cols.append(inside.astype(jnp.float32))
    cols += [jnp.zeros((rows,), jnp.float32)] * (16 - len(cols))
    return jnp.stack(cols, axis=1)


def sig(values):
    return 1.0 / (1.0 + jnp.exp(-values))


def patch_kernel(xin_ref, skip_ref, scale_ref, emb_ref, mask_ref, w1t_ref, w2t_ref, w2_ref,
                 pt_ref, pm_ref, err_ref, sums_ref, g1_ref, g2_ref, gp_ref, cin_ref, cone_ref):
    rows = xin_ref.shape[0]
    groups = sums_ref.shape[0]
    cells = rows // groups
    channels = xin_ref.shape[1]

    @pl.when(pl.program_id(0) == 0)
    def _():
        g1_ref[...] = jnp.zeros_like(g1_ref)
        g2_ref[...] = jnp.zeros_like(g2_ref)
        gp_ref[...] = jnp.zeros_like(gp_ref)

    def stack(values, target):
        for tap, (row_step, col_step) in enumerate(TAPS):
            shift = row_step * PATCH + col_step
            moved = values if shift == 0 else pltpu.roll(values, (-shift) % rows, 0)
            moved = moved * mask_ref[:, tap : tap + 1]
            target[:, tap * channels : (tap + 1) * channels] = moved.astype(target.dtype)

    stack(xin_ref[...].astype(jnp.float32), cin_ref)
    pre_one = jnp.dot(cin_ref[...], w1t_ref[...], preferred_element_type=jnp.float32)
    pre_one = pre_one + emb_ref[...]
    gate_one = sig(pre_one)
    act_one = (pre_one * gate_one).astype(jnp.bfloat16)
    stack(act_one.astype(jnp.float32), cone_ref)
    pre_two = jnp.dot(cone_ref[...], w2t_ref[...], preferred_element_type=jnp.float32)
    gate_two = sig(pre_two)
    act_two = (pre_two * gate_two).astype(jnp.bfloat16)
    output = jnp.dot(act_two, pt_ref[...], preferred_element_type=jnp.float32)
    error = skip_ref[...] + scale_ref[:, 0:1] * output
    err_ref[...] = error
    grad_output = (scale_ref[:, 1:2] * error).astype(jnp.bfloat16)
    contract = (((0,), (0,)), ((), ()))
    gp_ref[...] += lax.dot_general(grad_output, act_two, contract, preferred_element_type=jnp.float32)
    grad_act_two = jnp.dot(grad_output, pm_ref[...], preferred_element_type=jnp.float32)
    slope_two = gate_two * (1.0 + pre_two * (1.0 - gate_two))
    grad_pre_two = (grad_act_two * slope_two).astype(jnp.bfloat16)
    g2_ref[...] += lax.dot_general(grad_pre_two, cone_ref[...], contract, preferred_element_type=jnp.float32)
    grad_act_one = jnp.zeros((rows, channels), jnp.float32)
    for tap, (row_step, col_step) in enumerate(TAPS):
        shift = row_step * PATCH + col_step
        piece = jnp.dot(grad_pre_two, w2_ref[:, tap * channels : (tap + 1) * channels],
                        preferred_element_type=jnp.float32)
        moved = piece if shift == 0 else pltpu.roll(piece, shift % rows, 0)
        grad_act_one = grad_act_one + moved * mask_ref[:, 8 - tap : 9 - tap]
    slope_one = gate_one * (1.0 + pre_one * (1.0 - gate_one))
    grad_pre_one = (grad_act_one * slope_one).astype(jnp.bfloat16)
    g1_ref[...] += lax.dot_general(grad_pre_one, cin_ref[...], contract, preferred_element_type=jnp.float32)
    wide = grad_pre_one.astype(jnp.float32)
    for group in range(groups):
        sums_ref[group : group + 1, :] = jnp.sum(wide[group * cells : (group + 1) * cells], axis=0, keepdims=True)


def patch_pass(xin, skip, scale, emb, conv_one, conv_two, out_proj, group=8, interpret=False):
    rows_all, channels = xin.shape
    cells = PATCH * PATCH
    patches = rows_all // cells
    rows = group * cells
    steps = patches // group
    width = conv_one.shape[1]
    outs = conv_one.shape[0]
    targets = out_proj.shape[0]
    masks = tap_masks(rows)
    block = lambda shape: pl.BlockSpec(shape, lambda i: (i, 0))
    whole = lambda shape: pl.BlockSpec(shape, lambda i: (0, 0))
    return pl.pallas_call(
        patch_kernel,
        grid=(steps,),
        in_specs=[
            block((rows, channels)),
            block((rows, targets)),
            block((rows, 8)),
            block((rows, outs)),
            whole((rows, 16)),
            whole((width, outs)),
            whole((width, outs)),
            whole((outs, width)),
            whole((outs, targets)),
            whole((targets, outs)),
        ],
        out_specs=[
            block((rows, targets)),
            block((group, outs)),
            whole((outs, width)),
            whole((outs, width)),
            whole((targets, outs)),
        ],
        out_shape=[
            jax.ShapeDtypeStruct((rows_all, targets), jnp.float32),
            jax.ShapeDtypeStruct((patches, outs), jnp.float32),
            jax.ShapeDtypeStruct((outs, width), jnp.float32),
            jax.ShapeDtypeStruct((outs, width), jnp.float32),
            jax.ShapeDtypeStruct((targets, outs), jnp.float32),
        ],
        scratch_shapes=[pltpu.VMEM((rows, width), jnp.bfloat16), pltpu.VMEM((rows, width), jnp.bfloat16)],
        compiler_params=pltpu.CompilerParams(dimension_semantics=("arbitrary",)),
        interpret=interpret,
    )(xin, skip, scale, emb, masks, conv_one.T, conv_two.T, conv_two, out_proj.T, out_proj)


def kernel_blocks(mean_part, target_part, noise_part, step_ids, in_use, weights, interpret=False):
    conv_one, conv_two, out_proj, step_embed = weights
    patch_count, targets, cells = mean_part.shape
    level_count = step_embed.shape[0]
    sigma_table = noise_levels(level_count)
    step_hot = (step_ids[:, None] == jnp.arange(level_count, dtype=jnp.int32)[None, :]).astype(
        jnp.float32
    )
    sigma = jnp.sum(step_hot * sigma_table[None, :], axis=1)
    sigma_sq = sigma * sigma + 1.0
    scale_in = (1.0 / jnp.sqrt(sigma_sq))[:, None, None]
    scale_skip = (1.0 / sigma_sq)[:, None, None]
    scale_out = sigma / jnp.sqrt(sigma_sq)
    weight_loss = sigma_sq / (sigma * sigma)
    mean_float = mean_part.astype(jnp.float32)
    residual = target_part.astype(jnp.float32) - mean_float
    noisy = residual + sigma[:, None, None] * noise_part.astype(jnp.float32)
    inputs = jnp.concatenate([scale_in * noisy, mean_float], axis=1).astype(jnp.bfloat16)
    xin = jnp.swapaxes(inputs, 1, 2).reshape(patch_count * cells, 2 * targets)
    skip = jnp.swapaxes(scale_skip * noisy - residual, 1, 2).reshape(patch_count * cells, targets)
    factor = 2.0 * weight_loss * in_use / (targets * cells)
    per_patch = jnp.stack([scale_out, factor * scale_out], axis=1)
    per_patch = jnp.pad(per_patch, ((0, 0), (0, 6)))
    scale = jnp.broadcast_to(per_patch[:, None, :], (patch_count, cells, 8)).reshape(-1, 8)
    embedded = jnp.sum(step_hot[:, :, None] * step_embed[None, :, :], axis=1)
    emb = jnp.broadcast_to(embedded[:, None, :], (patch_count, cells, embedded.shape[1]))
    emb = emb.reshape(patch_count * cells, embedded.shape[1])
    error, pixel_sums, grad_one, grad_two, grad_proj = patch_pass(
        xin, skip, scale, emb, conv_one, conv_two, out_proj, interpret=interpret
    )
    error = error.reshape(patch_count, cells * targets)
    losses = weight_loss * jnp.mean(error * error, axis=1) * in_use
    grad_table = jnp.sum(step_hot[:, :, None] * pixel_sums[:, None, :], axis=0)
    return (losses, (grad_one, grad_two, grad_proj, grad_table))


def owner_tables(region_rows, strip_index):
    owners = region_rows[:, :, 2]
    earlier = (
        jnp.arange(owners.shape[1], dtype=jnp.int32)[None, :, None]
        > jnp.arange(owners.shape[1], dtype=jnp.int32)[None, None, :]
    )
    same = owners[:, :, None] == owners[:, None, :]
    pair_rank = jnp.sum((same & earlier).astype(jnp.int32), axis=2)
    mine = (owners == strip_index).astype(jnp.int32)
    flat = mine.reshape(-1)
    owner_slot = (jnp.cumsum(flat) - flat).reshape(owners.shape)
    return (owners, pair_rank, owner_slot)


def noise_routes(region_rows, owners, pair_rank, owner_slot, strip_index, capacity):
    hits = (
        (owners == strip_index)[:, :, None]
        & (pair_rank[:, :, None] == jnp.arange(capacity, dtype=jnp.int32)[None, None, :])
    ).astype(jnp.int32)
    return jnp.sum(hits * owner_slot[:, :, None], axis=1)


def exchange_sum(flat, steps):
    spread = 1
    for _, distance in steps:
        spread *= 2
    size = flat.shape[0]
    unit = spread * 8
    padded = (size + unit - 1) // unit * unit
    values = jnp.pad(flat, (0, padded - size))
    places = {axis: lax.axis_index(axis) for axis, _ in steps}
    for axis, distance in steps:
        count = lax.axis_size(axis)
        half = values.shape[0] // 2
        low, high = values[:half], values[half:]
        upper = (places[axis] // distance) % 2 == 1
        route = [(i, i ^ distance) for i in range(count)]
        kept = jnp.where(upper, high, low)
        sent = jnp.where(upper, low, high)
        values = kept + lax.ppermute(sent, axis, route)
    for axis, distance in reversed(steps):
        count = lax.axis_size(axis)
        upper = (places[axis] // distance) % 2 == 1
        route = [(i, i ^ distance) for i in range(count)]
        other = lax.ppermute(values, axis, route)
        values = jnp.where(
            upper, jnp.concatenate([other, values]), jnp.concatenate([values, other])
        )
    return values[:size]


def reduce_steps():
    sizes = {axis: lax.axis_size(axis) for axis in ("segment", "rows", "dp")}
    steps = []
    distance = 1
    while distance < max(sizes.values()):
        for axis in ("segment", "rows", "dp"):
            if distance < sizes[axis]:
                steps.append((axis, distance))
        distance *= 2
    return steps


def cut_patches(source_grid, row_at, col_at, height):
    zero_index = jnp.zeros((), jnp.int32)

    def cut(row_start, col_start):
        piece = lax.dynamic_slice(
            source_grid,
            (zero_index, zero_index, row_start, col_start),
            (2, source_grid.shape[1], height, height),
        )
        return piece.reshape(2, source_grid.shape[1], height * height)

    return jax.vmap(cut)(row_at, col_at)


def per_device(
    coarse, target, noise, regions, reg_conv, reg_out, conv_one, conv_two, out_proj, step_embed
):
    strips = lax.axis_size("rows")
    strip_index = lax.axis_index("rows")
    sample_count = lax.axis_size("segment") * lax.axis_size("dp")
    sample_index = lax.axis_index("segment") * lax.axis_size("dp") + lax.axis_index("dp")
    region_rows = regions[0]
    per_strip = region_rows.shape[1]
    capacity = max(2, (2 * per_strip + strips - 1) // strips)
    weights = (conv_one, conv_two, out_proj, step_embed)
    owners, pair_rank, owner_slot = owner_tables(region_rows, strip_index)
    send_slot = noise_routes(region_rows, owners, pair_rank, owner_slot, strip_index, capacity)
    outgoing = jnp.take(noise[0, 0], send_slot.reshape(-1), axis=0)
    outgoing = outgoing.reshape((strips, capacity) + outgoing.shape[1:])
    received = lax.all_to_all(outgoing, "rows", split_axis=0, concat_axis=0, tiled=True)
    rimmed = padded_2(coarse, (("rows", 2),), 1)
    mean_strip = jnp.transpose(regress(rimmed[0], reg_conv, reg_out), (2, 0, 1))
    height = mean_strip.shape[1]
    pair_strip = jnp.stack([mean_strip, target[0]])
    own_regions = lax.dynamic_index_in_dim(region_rows, strip_index, 0, keepdims=False)
    own_pairs = lax.dynamic_index_in_dim(pair_rank, strip_index, 0, keepdims=False)
    below = shifted_2(pair_strip[:, :, : height - 1], "rows", -1)
    extended = jnp.concatenate([pair_strip, below], axis=2)
    patches = cut_patches(extended, own_regions[:, 0], own_regions[:, 1], height)
    flat_recv = received.reshape((strips * capacity,) + received.shape[2:])
    patch_noise = jnp.take(flat_recv, own_regions[:, 2] * capacity + own_pairs, axis=0)
    in_use = jnp.ones((per_strip,), jnp.float32)
    losses, gradients = kernel_blocks(
        patches[:, 0], patches[:, 1], patch_noise, own_regions[:, 3], in_use, weights
    )
    owner_hot = (own_regions[:, 2][:, None] == jnp.arange(strips, dtype=jnp.int32)[None, :])
    owner_part = jnp.sum(owner_hot.astype(jnp.float32) * losses[:, None], axis=0)
    sample_hot = (jnp.arange(sample_count, dtype=jnp.int32) == sample_index).astype(jnp.float32)
    owner_table = sample_hot[:, None] * owner_part[None, :]
    pieces = (gradients[0], gradients[1], gradients[2], gradients[3], owner_table)
    flat = jnp.concatenate([piece.reshape(-1) for piece in pieces])
    summed = exchange_sum(flat, reduce_steps())
    results = []
    offset = 0
    for piece in pieces:
        results.append(summed[offset : offset + piece.size].reshape(piece.shape))
        offset += piece.size
    table = results[4]
    owner_total = lax.dynamic_slice(table, (sample_index, strip_index), (1, 1))
    return (mean_strip[None], owner_total, results[0], results[1], results[2], results[3])


def solution(mesh):
    placed = (
        P(("segment", "dp"), None, "rows", None),
        P(("segment", "dp"), None, "rows", None),
        P(("segment", "dp"), "rows", None, None, None),
        P(("segment", "dp"), None, None, None),
        P(),
        P(),
        P(),
        P(),
        P(),
        P(),
    )
    return jax.shard_map(
        per_device,
        mesh=mesh,
        in_specs=placed,
        out_specs=(
            P(("segment", "dp"), None, "rows", None),
            P(("segment", "dp"), "rows"),
            P(),
            P(),
            P(),
            P(),
        ),
        check_vma=False,
    )
```

```python
import math

import jax
import jax.numpy as jnp
from jax import lax
from jax.experimental import pallas as pl
from jax.experimental.pallas import tpu as pltpu
from jax.sharding import PartitionSpec as P

PATCH = 12


TAPS = ((-1, -1), (-1, 0), (-1, 1), (0, -1), (0, 0), (0, 1), (1, -1), (1, 0), (1, 1))


def padded_2(cells, sides, width):
    for axis, dim in sides:
        count = lax.axis_size(axis)
        ends = count - 1
        head = lax.slice_in_dim(cells, 0, width, axis=dim)
        tail = lax.slice_in_dim(cells, cells.shape[dim] - width, cells.shape[dim], axis=dim)
        cells = jnp.concatenate(
            [
                lax.ppermute(tail, axis, [(i, (i + 1) % count) for i in range(ends)]),
                cells,
                lax.ppermute(head, axis, [((i + 1) % count, i) for i in range(ends)]),
            ],
            axis=dim,
        )
    return cells


def shifted_2(block, axis, distance):
    devices = range(lax.axis_size(axis))
    route = [(i - distance, i) for i in devices if i - distance in devices]
    return lax.ppermute(block, axis, route)


def shifted(values, row_step, col_step, stride):
    length = values.shape[-1]
    margin = stride + 1
    widths = [(0, 0)] * (values.ndim - 1) + [(margin, margin)]
    padded = jnp.pad(values, widths)
    offset = margin + row_step * stride + col_step
    moved = lax.slice_in_dim(padded, offset, offset + length, axis=values.ndim - 1)
    column = jnp.arange(length, dtype=jnp.int32) % stride + col_step
    inside = (column >= 0) & (column < stride)
    return jnp.where(inside, moved, jnp.zeros((), moved.dtype))


def columns(values, stride):
    return jnp.concatenate(
        [shifted(values, row_step, col_step, stride) for row_step, col_step in TAPS], axis=-2
    )


def fold(gradients, stride):
    width = gradients.shape[-2] // 9
    result = jnp.zeros(gradients.shape[:-2] + (width, gradients.shape[-1]), jnp.float32)
    for position, (row_step, col_step) in enumerate(TAPS):
        piece = gradients[..., position * width : (position + 1) * width, :]
        result = result + shifted(piece, -row_step, -col_step, stride)
    return result


def noise_levels(level_count):
    steps_f = jnp.arange(level_count, dtype=jnp.float32)
    return 0.1 * jnp.exp(steps_f * (math.log(100.0) / (level_count - 1)))


def silu_slope(values):
    gate = jax.nn.sigmoid(values)
    return gate * (1.0 + values * (1.0 - gate))


def product(form, left, right):
    return jnp.einsum(form, left, right, preferred_element_type=jnp.float32)


def regress(grid_rows, reg_conv, reg_out):
    channels, height, width = grid_rows.shape
    hidden_count = reg_conv.shape[0]
    kernel = reg_conv.reshape(hidden_count, 3, 3, channels).transpose(1, 2, 3, 0)
    hidden = lax.conv_general_dilated(
        grid_rows[None],
        kernel,
        window_strides=(1, 1),
        padding=((0, 0), (1, 1)),
        dimension_numbers=("NCHW", "HWIO", "NHWC"),
        preferred_element_type=jnp.float32,
    )[0]
    activated = jax.nn.silu(hidden).astype(jnp.bfloat16)
    return product("rqo,co->rqc", activated, reg_out).astype(jnp.bfloat16)


def patch_block(mean_part, target_part, noise_part, step_ids, in_use, weights):
    conv_one, conv_two, out_proj, step_embed = weights
    stride = PATCH
    level_count = step_embed.shape[0]
    sigma_table = noise_levels(level_count)
    step_hot = (step_ids[:, None] == jnp.arange(level_count, dtype=jnp.int32)[None, :]).astype(
        jnp.float32
    )
    sigma = jnp.sum(step_hot * sigma_table[None, :], axis=1)
    sigma_sq = sigma * sigma + 1.0
    scale_in = (1.0 / jnp.sqrt(sigma_sq))[:, None, None]
    scale_skip = (1.0 / sigma_sq)[:, None, None]
    scale_out = (sigma / jnp.sqrt(sigma_sq))[:, None, None]
    weight_loss = sigma_sq / (sigma * sigma)
    mean_float = mean_part.astype(jnp.float32)
    residual = target_part.astype(jnp.float32) - mean_float
    noisy = residual + sigma[:, None, None] * noise_part.astype(jnp.float32)
    inputs = jnp.concatenate([scale_in * noisy, mean_float], axis=1).astype(jnp.bfloat16)
    cols_in = columns(inputs, stride)
    embedded = jnp.sum(step_hot[:, :, None] * step_embed[None, :, :], axis=1)
    pre_one = product("ok,bkp->bop", conv_one, cols_in) + embedded[:, :, None]
    act_one = jax.nn.silu(pre_one).astype(jnp.bfloat16)
    cols_one = columns(act_one, stride)
    pre_two = product("ok,bkp->bop", conv_two, cols_one)
    act_two = jax.nn.silu(pre_two).astype(jnp.bfloat16)
    output = product("co,bop->bcp", out_proj, act_two)
    error = scale_skip * noisy + scale_out * output - residual
    losses = weight_loss * jnp.mean(error * error, axis=(1, 2)) * in_use
    factor = 2.0 * weight_loss * in_use / (error.shape[1] * error.shape[2])
    grad_output = (factor[:, None, None] * scale_out * error).astype(jnp.bfloat16)
    grad_proj = product("bcp,bop->co", grad_output, act_two)
    grad_act_two = product("co,bcp->bop", out_proj, grad_output)
    grad_pre_two = (grad_act_two * silu_slope(pre_two)).astype(jnp.bfloat16)
    grad_two = product("bop,bkp->ok", grad_pre_two, cols_one)
    grad_cols = product("ok,bop->bkp", conv_two, grad_pre_two)
    grad_act_one = fold(grad_cols, stride)
    grad_pre_one = (grad_act_one * silu_slope(pre_one)).astype(jnp.bfloat16)
    grad_one = product("bop,bkp->ok", grad_pre_one, cols_in)
    pixel_sums = jnp.sum(grad_pre_one, axis=2, dtype=jnp.float32)
    grad_table = jnp.sum(step_hot[:, :, None] * pixel_sums[:, None, :], axis=0)
    return (losses, (grad_one, grad_two, grad_proj, grad_table))


def run_blocks(mean_part, target_part, noise_part, step_ids, in_use, weights):
    patch_count = mean_part.shape[0]
    blocks = patch_count // 4

    def regroup(values):
        return values.reshape((blocks, 4) + values.shape[1:])

    def advance(running, group_block):
        losses, gradients = patch_block(
            group_block[0], group_block[1], group_block[2], group_block[3], group_block[4], weights
        )
        summed = (
            running[0] + gradients[0],
            running[1] + gradients[1],
            running[2] + gradients[2],
            running[3] + gradients[3],
        )
        return (summed, losses)

    initial = (
        jnp.zeros(weights[0].shape, jnp.float32),
        jnp.zeros(weights[1].shape, jnp.float32),
        jnp.zeros(weights[2].shape, jnp.float32),
        jnp.zeros(weights[3].shape, jnp.float32),
    )
    stacked = (
        regroup(mean_part),
        regroup(target_part),
        regroup(noise_part),
        regroup(step_ids),
        regroup(in_use),
    )
    gradients, losses = lax.scan(advance, initial, stacked)
    return (losses.reshape(patch_count), gradients)


def tap_masks(rows):
    cell = jnp.arange(rows, dtype=jnp.int32) % (PATCH * PATCH)
    line = cell // PATCH
    place = cell % PATCH
    cols = []
    for row_step, col_step in TAPS:
        inside = (line + row_step >= 0) & (line + row_step < PATCH)
        inside = inside & (place + col_step >= 0) & (place + col_step < PATCH)
        cols.append(inside.astype(jnp.float32))
    cols += [jnp.zeros((rows,), jnp.float32)] * (16 - len(cols))
    return jnp.stack(cols, axis=1)


def sig(values):
    return 1.0 / (1.0 + jnp.exp(-values))


def patch_kernel(xin_ref, skip_ref, scale_ref, emb_ref, mask_ref, w1t_ref, w2t_ref, w2_ref,
                 pt_ref, pm_ref, err_ref, sums_ref, g1_ref, g2_ref, gp_ref, cin_ref, cone_ref):
    rows = xin_ref.shape[0]
    groups = sums_ref.shape[0]
    cells = rows // groups
    channels = xin_ref.shape[1]

    @pl.when(pl.program_id(0) == 0)
    def _():
        g1_ref[...] = jnp.zeros_like(g1_ref)
        g2_ref[...] = jnp.zeros_like(g2_ref)
        gp_ref[...] = jnp.zeros_like(gp_ref)

    def stack(values, target):
        for tap, (row_step, col_step) in enumerate(TAPS):
            shift = row_step * PATCH + col_step
            moved = values if shift == 0 else pltpu.roll(values, (-shift) % rows, 0)
            moved = moved * mask_ref[:, tap : tap + 1]
            target[:, tap * channels : (tap + 1) * channels] = moved.astype(target.dtype)

    stack(xin_ref[...].astype(jnp.float32), cin_ref)
    pre_one = jnp.dot(cin_ref[...], w1t_ref[...], preferred_element_type=jnp.float32)
    pre_one = pre_one + emb_ref[...]
    gate_one = sig(pre_one)
    act_one = (pre_one * gate_one).astype(jnp.bfloat16)
    stack(act_one.astype(jnp.float32), cone_ref)
    pre_two = jnp.dot(cone_ref[...], w2t_ref[...], preferred_element_type=jnp.float32)
    gate_two = sig(pre_two)
    act_two = (pre_two * gate_two).astype(jnp.bfloat16)
    output = jnp.dot(act_two, pt_ref[...], preferred_element_type=jnp.float32)
    error = skip_ref[...] + scale_ref[:, 0:1] * output
    err_ref[...] = error
    grad_output = (scale_ref[:, 1:2] * error).astype(jnp.bfloat16)
    contract = (((0,), (0,)), ((), ()))
    gp_ref[...] += lax.dot_general(grad_output, act_two, contract, preferred_element_type=jnp.float32)
    grad_act_two = jnp.dot(grad_output, pm_ref[...], preferred_element_type=jnp.float32)
    slope_two = gate_two * (1.0 + pre_two * (1.0 - gate_two))
    grad_pre_two = (grad_act_two * slope_two).astype(jnp.bfloat16)
    g2_ref[...] += lax.dot_general(grad_pre_two, cone_ref[...], contract, preferred_element_type=jnp.float32)
    grad_act_one = jnp.zeros((rows, channels), jnp.float32)
    for tap, (row_step, col_step) in enumerate(TAPS):
        shift = row_step * PATCH + col_step
        piece = jnp.dot(grad_pre_two, w2_ref[:, tap * channels : (tap + 1) * channels],
                        preferred_element_type=jnp.float32)
        moved = piece if shift == 0 else pltpu.roll(piece, shift % rows, 0)
        grad_act_one = grad_act_one + moved * mask_ref[:, 8 - tap : 9 - tap]
    slope_one = gate_one * (1.0 + pre_one * (1.0 - gate_one))
    grad_pre_one = (grad_act_one * slope_one).astype(jnp.bfloat16)
    g1_ref[...] += lax.dot_general(grad_pre_one, cin_ref[...], contract, preferred_element_type=jnp.float32)
    wide = grad_pre_one.astype(jnp.float32)
    for group in range(groups):
        sums_ref[group : group + 1, :] = jnp.sum(wide[group * cells : (group + 1) * cells], axis=0, keepdims=True)


def patch_pass(xin, skip, scale, emb, conv_one, conv_two, out_proj, group=8, interpret=False):
    rows_all, channels = xin.shape
    cells = PATCH * PATCH
    patches = rows_all // cells
    rows = group * cells
    steps = patches // group
    width = conv_one.shape[1]
    outs = conv_one.shape[0]
    targets = out_proj.shape[0]
    masks = tap_masks(rows)
    block = lambda shape: pl.BlockSpec(shape, lambda i: (i, 0))
    whole = lambda shape: pl.BlockSpec(shape, lambda i: (0, 0))
    return pl.pallas_call(
        patch_kernel,
        grid=(steps,),
        in_specs=[
            block((rows, channels)),
            block((rows, targets)),
            block((rows, 8)),
            block((rows, outs)),
            whole((rows, 16)),
            whole((width, outs)),
            whole((width, outs)),
            whole((outs, width)),
            whole((outs, targets)),
            whole((targets, outs)),
        ],
        out_specs=[
            block((rows, targets)),
            block((group, outs)),
            whole((outs, width)),
            whole((outs, width)),
            whole((targets, outs)),
        ],
        out_shape=[
            jax.ShapeDtypeStruct((rows_all, targets), jnp.float32),
            jax.ShapeDtypeStruct((patches, outs), jnp.float32),
            jax.ShapeDtypeStruct((outs, width), jnp.float32),
            jax.ShapeDtypeStruct((outs, width), jnp.float32),
            jax.ShapeDtypeStruct((targets, outs), jnp.float32),
        ],
        scratch_shapes=[pltpu.VMEM((rows, width), jnp.bfloat16), pltpu.VMEM((rows, width), jnp.bfloat16)],
        compiler_params=pltpu.CompilerParams(dimension_semantics=("arbitrary",)),
        interpret=interpret,
    )(xin, skip, scale, emb, masks, conv_one.T, conv_two.T, conv_two, out_proj.T, out_proj)


def kernel_blocks(mean_part, target_part, noise_part, step_ids, in_use, weights, interpret=False):
    conv_one, conv_two, out_proj, step_embed = weights
    patch_count, targets, cells = mean_part.shape
    level_count = step_embed.shape[0]
    sigma_table = noise_levels(level_count)
    step_hot = (step_ids[:, None] == jnp.arange(level_count, dtype=jnp.int32)[None, :]).astype(
        jnp.float32
    )
    sigma = jnp.sum(step_hot * sigma_table[None, :], axis=1)
    sigma_sq = sigma * sigma + 1.0
    scale_in = (1.0 / jnp.sqrt(sigma_sq))[:, None, None]
    scale_skip = (1.0 / sigma_sq)[:, None, None]
    scale_out = sigma / jnp.sqrt(sigma_sq)
    weight_loss = sigma_sq / (sigma * sigma)
    mean_float = mean_part.astype(jnp.float32)
    residual = target_part.astype(jnp.float32) - mean_float
    noisy = residual + sigma[:, None, None] * noise_part.astype(jnp.float32)
    inputs = jnp.concatenate([scale_in * noisy, mean_float], axis=1).astype(jnp.bfloat16)
    xin = jnp.swapaxes(inputs, 1, 2).reshape(patch_count * cells, 2 * targets)
    skip = jnp.swapaxes(scale_skip * noisy - residual, 1, 2).reshape(patch_count * cells, targets)
    factor = 2.0 * weight_loss * in_use / (targets * cells)
    per_patch = jnp.stack([scale_out, factor * scale_out], axis=1)
    per_patch = jnp.pad(per_patch, ((0, 0), (0, 6)))
    scale = jnp.broadcast_to(per_patch[:, None, :], (patch_count, cells, 8)).reshape(-1, 8)
    embedded = jnp.sum(step_hot[:, :, None] * step_embed[None, :, :], axis=1)
    emb = jnp.broadcast_to(embedded[:, None, :], (patch_count, cells, embedded.shape[1]))
    emb = emb.reshape(patch_count * cells, embedded.shape[1])
    error, pixel_sums, grad_one, grad_two, grad_proj = patch_pass(
        xin, skip, scale, emb, conv_one, conv_two, out_proj, interpret=interpret
    )
    error = error.reshape(patch_count, cells * targets)
    losses = weight_loss * jnp.mean(error * error, axis=1) * in_use
    grad_table = jnp.sum(step_hot[:, :, None] * pixel_sums[:, None, :], axis=0)
    return (losses, (grad_one, grad_two, grad_proj, grad_table))


def owner_tables(region_rows, strip_index):
    owners = region_rows[:, :, 2]
    earlier = (
        jnp.arange(owners.shape[1], dtype=jnp.int32)[None, :, None]
        > jnp.arange(owners.shape[1], dtype=jnp.int32)[None, None, :]
    )
    same = owners[:, :, None] == owners[:, None, :]
    pair_rank = jnp.sum((same & earlier).astype(jnp.int32), axis=2)
    mine = (owners == strip_index).astype(jnp.int32)
    flat = mine.reshape(-1)
    owner_slot = (jnp.cumsum(flat) - flat).reshape(owners.shape)
    return (owners, pair_rank, owner_slot)


def noise_routes(region_rows, owners, pair_rank, owner_slot, strip_index, capacity):
    hits = (
        (owners == strip_index)[:, :, None]
        & (pair_rank[:, :, None] == jnp.arange(capacity, dtype=jnp.int32)[None, None, :])
    ).astype(jnp.int32)
    return jnp.sum(hits * owner_slot[:, :, None], axis=1)


def exchange_sum(flat, steps):
    spread = 1
    for _, distance in steps:
        spread *= 2
    size = flat.shape[0]
    unit = spread * 8
    padded = (size + unit - 1) // unit * unit
    values = jnp.pad(flat, (0, padded - size))
    places = {axis: lax.axis_index(axis) for axis, _ in steps}
    for axis, distance in steps:
        count = lax.axis_size(axis)
        half = values.shape[0] // 2
        low, high = values[:half], values[half:]
        upper = (places[axis] // distance) % 2 == 1
        route = [(i, i ^ distance) for i in range(count)]
        kept = jnp.where(upper, high, low)
        sent = jnp.where(upper, low, high)
        values = kept + lax.ppermute(sent, axis, route)
    for axis, distance in reversed(steps):
        count = lax.axis_size(axis)
        upper = (places[axis] // distance) % 2 == 1
        route = [(i, i ^ distance) for i in range(count)]
        other = lax.ppermute(values, axis, route)
        values = jnp.where(
            upper, jnp.concatenate([other, values]), jnp.concatenate([values, other])
        )
    return values[:size]


def reduce_steps():
    sizes = {axis: lax.axis_size(axis) for axis in ("segment", "rows", "dp")}
    steps = []
    distance = 1
    while distance < max(sizes.values()):
        for axis in ("segment", "rows", "dp"):
            if distance < sizes[axis]:
                steps.append((axis, distance))
        distance *= 2
    return steps


def cut_patches(source_grid, row_at, col_at, height):
    zero_index = jnp.zeros((), jnp.int32)

    def cut(row_start, col_start):
        piece = lax.dynamic_slice(
            source_grid,
            (zero_index, zero_index, row_start, col_start),
            (2, source_grid.shape[1], height, height),
        )
        return piece.reshape(2, source_grid.shape[1], height * height)

    return jax.vmap(cut)(row_at, col_at)


def per_device(
    coarse, target, noise, regions, reg_conv, reg_out, conv_one, conv_two, out_proj, step_embed
):
    strips = lax.axis_size("rows")
    strip_index = lax.axis_index("rows")
    sample_count = lax.axis_size("segment") * lax.axis_size("dp")
    sample_index = lax.axis_index("segment") * lax.axis_size("dp") + lax.axis_index("dp")
    region_rows = regions[0]
    per_strip = region_rows.shape[1]
    capacity = max(2, (2 * per_strip + strips - 1) // strips)
    weights = (conv_one, conv_two, out_proj, step_embed)
    owners, pair_rank, owner_slot = owner_tables(region_rows, strip_index)
    send_slot = noise_routes(region_rows, owners, pair_rank, owner_slot, strip_index, capacity)
    outgoing = jnp.take(noise[0, 0], send_slot.reshape(-1), axis=0)
    outgoing = outgoing.reshape((strips, capacity) + outgoing.shape[1:])
    received = lax.all_to_all(outgoing, "rows", split_axis=0, concat_axis=0, tiled=True)
    count = strips
    above = lax.ppermute(coarse[:, :, -1:], "rows", [(i, i + 1) for i in range(count - 1)])
    after = lax.ppermute(coarse, "rows", [(i + 1, i) for i in range(count - 1)])
    height = coarse.shape[2]
    later = lax.ppermute(target[:, :, : height - 1], "rows", [(i + 1, i) for i in range(count - 1)])
    rimmed = jnp.concatenate([above, coarse, after], axis=2)
    mean_all = jnp.transpose(regress(rimmed[0], reg_conv, reg_out), (2, 0, 1))
    mean_strip = mean_all[:, :height]
    own_regions = lax.dynamic_index_in_dim(region_rows, strip_index, 0, keepdims=False)
    own_pairs = lax.dynamic_index_in_dim(pair_rank, strip_index, 0, keepdims=False)
    extended = jnp.stack([mean_all[:, : 2 * height - 1], jnp.concatenate([target[0], later[0]], axis=1)])
    patches = cut_patches(extended, own_regions[:, 0], own_regions[:, 1], height)
    flat_recv = received.reshape((strips * capacity,) + received.shape[2:])
    patch_noise = jnp.take(flat_recv, own_regions[:, 2] * capacity + own_pairs, axis=0)
    in_use = jnp.ones((per_strip,), jnp.float32)
    losses, gradients = kernel_blocks(
        patches[:, 0], patches[:, 1], patch_noise, own_regions[:, 3], in_use, weights
    )
    owner_hot = (own_regions[:, 2][:, None] == jnp.arange(strips, dtype=jnp.int32)[None, :])
    owner_part = jnp.sum(owner_hot.astype(jnp.float32) * losses[:, None], axis=0)
    sample_hot = (jnp.arange(sample_count, dtype=jnp.int32) == sample_index).astype(jnp.float32)
    owner_table = sample_hot[:, None] * owner_part[None, :]
    pieces = (gradients[0], gradients[1], gradients[2], gradients[3], owner_table)
    flat = jnp.concatenate([piece.reshape(-1) for piece in pieces])
    summed = exchange_sum(flat, reduce_steps())
    results = []
    offset = 0
    for piece in pieces:
        results.append(summed[offset : offset + piece.size].reshape(piece.shape))
        offset += piece.size
    table = results[4]
    owner_total = lax.dynamic_slice(table, (sample_index, strip_index), (1, 1))
    return (mean_strip[None], owner_total, results[0], results[1], results[2], results[3])


def solution(mesh):
    placed = (
        P(("segment", "dp"), None, "rows", None),
        P(("segment", "dp"), None, "rows", None),
        P(("segment", "dp"), "rows", None, None, None),
        P(("segment", "dp"), None, None, None),
        P(),
        P(),
        P(),
        P(),
        P(),
        P(),
    )
    return jax.shard_map(
        per_device,
        mesh=mesh,
        in_specs=placed,
        out_specs=(
            P(("segment", "dp"), None, "rows", None),
            P(("segment", "dp"), "rows"),
            P(),
            P(),
            P(),
            P(),
        ),
        check_vma=False,
    )
```

```python
import math

import jax
import jax.numpy as jnp
from jax import lax
from jax.experimental import pallas as pl
from jax.experimental.pallas import tpu as pltpu
from jax.sharding import PartitionSpec as P

PATCH = 12


TAPS = ((-1, -1), (-1, 0), (-1, 1), (0, -1), (0, 0), (0, 1), (1, -1), (1, 0), (1, 1))


def padded_2(cells, sides, width):
    for axis, dim in sides:
        count = lax.axis_size(axis)
        ends = count - 1
        head = lax.slice_in_dim(cells, 0, width, axis=dim)
        tail = lax.slice_in_dim(cells, cells.shape[dim] - width, cells.shape[dim], axis=dim)
        cells = jnp.concatenate(
            [
                lax.ppermute(tail, axis, [(i, (i + 1) % count) for i in range(ends)]),
                cells,
                lax.ppermute(head, axis, [((i + 1) % count, i) for i in range(ends)]),
            ],
            axis=dim,
        )
    return cells


def shifted_2(block, axis, distance):
    devices = range(lax.axis_size(axis))
    route = [(i - distance, i) for i in devices if i - distance in devices]
    return lax.ppermute(block, axis, route)


def shifted(values, row_step, col_step, stride):
    length = values.shape[-1]
    margin = stride + 1
    widths = [(0, 0)] * (values.ndim - 1) + [(margin, margin)]
    padded = jnp.pad(values, widths)
    offset = margin + row_step * stride + col_step
    moved = lax.slice_in_dim(padded, offset, offset + length, axis=values.ndim - 1)
    column = jnp.arange(length, dtype=jnp.int32) % stride + col_step
    inside = (column >= 0) & (column < stride)
    return jnp.where(inside, moved, jnp.zeros((), moved.dtype))


def columns(values, stride):
    return jnp.concatenate(
        [shifted(values, row_step, col_step, stride) for row_step, col_step in TAPS], axis=-2
    )


def fold(gradients, stride):
    width = gradients.shape[-2] // 9
    result = jnp.zeros(gradients.shape[:-2] + (width, gradients.shape[-1]), jnp.float32)
    for position, (row_step, col_step) in enumerate(TAPS):
        piece = gradients[..., position * width : (position + 1) * width, :]
        result = result + shifted(piece, -row_step, -col_step, stride)
    return result


def noise_levels(level_count):
    steps_f = jnp.arange(level_count, dtype=jnp.float32)
    return 0.1 * jnp.exp(steps_f * (math.log(100.0) / (level_count - 1)))


def silu_slope(values):
    gate = jax.nn.sigmoid(values)
    return gate * (1.0 + values * (1.0 - gate))


def product(form, left, right):
    return jnp.einsum(form, left, right, preferred_element_type=jnp.float32)


def regress(grid_rows, reg_conv, reg_out):
    channels, height, width = grid_rows.shape
    hidden_count = reg_conv.shape[0]
    kernel = reg_conv.reshape(hidden_count, 3, 3, channels).transpose(1, 2, 3, 0)
    hidden = lax.conv_general_dilated(
        grid_rows[None],
        kernel,
        window_strides=(1, 1),
        padding=((0, 0), (1, 1)),
        dimension_numbers=("NCHW", "HWIO", "NHWC"),
        preferred_element_type=jnp.float32,
    )[0]
    activated = jax.nn.silu(hidden).astype(jnp.bfloat16)
    return product("rqo,co->rqc", activated, reg_out).astype(jnp.bfloat16)


def patch_block(mean_part, target_part, noise_part, step_ids, in_use, weights):
    conv_one, conv_two, out_proj, step_embed = weights
    stride = PATCH
    level_count = step_embed.shape[0]
    sigma_table = noise_levels(level_count)
    step_hot = (step_ids[:, None] == jnp.arange(level_count, dtype=jnp.int32)[None, :]).astype(
        jnp.float32
    )
    sigma = jnp.sum(step_hot * sigma_table[None, :], axis=1)
    sigma_sq = sigma * sigma + 1.0
    scale_in = (1.0 / jnp.sqrt(sigma_sq))[:, None, None]
    scale_skip = (1.0 / sigma_sq)[:, None, None]
    scale_out = (sigma / jnp.sqrt(sigma_sq))[:, None, None]
    weight_loss = sigma_sq / (sigma * sigma)
    mean_float = mean_part.astype(jnp.float32)
    residual = target_part.astype(jnp.float32) - mean_float
    noisy = residual + sigma[:, None, None] * noise_part.astype(jnp.float32)
    inputs = jnp.concatenate([scale_in * noisy, mean_float], axis=1).astype(jnp.bfloat16)
    cols_in = columns(inputs, stride)
    embedded = jnp.sum(step_hot[:, :, None] * step_embed[None, :, :], axis=1)
    pre_one = product("ok,bkp->bop", conv_one, cols_in) + embedded[:, :, None]
    act_one = jax.nn.silu(pre_one).astype(jnp.bfloat16)
    cols_one = columns(act_one, stride)
    pre_two = product("ok,bkp->bop", conv_two, cols_one)
    act_two = jax.nn.silu(pre_two).astype(jnp.bfloat16)
    output = product("co,bop->bcp", out_proj, act_two)
    error = scale_skip * noisy + scale_out * output - residual
    losses = weight_loss * jnp.mean(error * error, axis=(1, 2)) * in_use
    factor = 2.0 * weight_loss * in_use / (error.shape[1] * error.shape[2])
    grad_output = (factor[:, None, None] * scale_out * error).astype(jnp.bfloat16)
    grad_proj = product("bcp,bop->co", grad_output, act_two)
    grad_act_two = product("co,bcp->bop", out_proj, grad_output)
    grad_pre_two = (grad_act_two * silu_slope(pre_two)).astype(jnp.bfloat16)
    grad_two = product("bop,bkp->ok", grad_pre_two, cols_one)
    grad_cols = product("ok,bop->bkp", conv_two, grad_pre_two)
    grad_act_one = fold(grad_cols, stride)
    grad_pre_one = (grad_act_one * silu_slope(pre_one)).astype(jnp.bfloat16)
    grad_one = product("bop,bkp->ok", grad_pre_one, cols_in)
    pixel_sums = jnp.sum(grad_pre_one, axis=2, dtype=jnp.float32)
    grad_table = jnp.sum(step_hot[:, :, None] * pixel_sums[:, None, :], axis=0)
    return (losses, (grad_one, grad_two, grad_proj, grad_table))


def run_blocks(mean_part, target_part, noise_part, step_ids, in_use, weights):
    patch_count = mean_part.shape[0]
    blocks = patch_count // 4

    def regroup(values):
        return values.reshape((blocks, 4) + values.shape[1:])

    def advance(running, group_block):
        losses, gradients = patch_block(
            group_block[0], group_block[1], group_block[2], group_block[3], group_block[4], weights
        )
        summed = (
            running[0] + gradients[0],
            running[1] + gradients[1],
            running[2] + gradients[2],
            running[3] + gradients[3],
        )
        return (summed, losses)

    initial = (
        jnp.zeros(weights[0].shape, jnp.float32),
        jnp.zeros(weights[1].shape, jnp.float32),
        jnp.zeros(weights[2].shape, jnp.float32),
        jnp.zeros(weights[3].shape, jnp.float32),
    )
    stacked = (
        regroup(mean_part),
        regroup(target_part),
        regroup(noise_part),
        regroup(step_ids),
        regroup(in_use),
    )
    gradients, losses = lax.scan(advance, initial, stacked)
    return (losses.reshape(patch_count), gradients)


def tap_masks(rows):
    cell = jnp.arange(rows, dtype=jnp.int32) % (PATCH * PATCH)
    line = cell // PATCH
    place = cell % PATCH
    cols = []
    for row_step, col_step in TAPS:
        inside = (line + row_step >= 0) & (line + row_step < PATCH)
        inside = inside & (place + col_step >= 0) & (place + col_step < PATCH)
        cols.append(inside.astype(jnp.float32))
    cols += [jnp.zeros((rows,), jnp.float32)] * (16 - len(cols))
    return jnp.stack(cols, axis=1)


def sig(values):
    return 1.0 / (1.0 + jnp.exp(-values))


def patch_kernel(xin_ref, skip_ref, scale_ref, emb_ref, mask_ref, w1t_ref, w2t_ref, w2_ref,
                 pt_ref, pm_ref, err_ref, sums_ref, g1_ref, g2_ref, gp_ref, cin_ref, cone_ref):
    rows = xin_ref.shape[0]
    groups = sums_ref.shape[0]
    cells = rows // groups
    channels = xin_ref.shape[1]

    @pl.when(pl.program_id(0) == 0)
    def _():
        g1_ref[...] = jnp.zeros_like(g1_ref)
        g2_ref[...] = jnp.zeros_like(g2_ref)
        gp_ref[...] = jnp.zeros_like(gp_ref)

    def stack(values, target):
        for tap, (row_step, col_step) in enumerate(TAPS):
            shift = row_step * PATCH + col_step
            moved = values if shift == 0 else pltpu.roll(values, (-shift) % rows, 0)
            moved = moved * mask_ref[:, tap : tap + 1]
            target[:, tap * channels : (tap + 1) * channels] = moved.astype(target.dtype)

    stack(xin_ref[...].astype(jnp.float32), cin_ref)
    pre_one = jnp.dot(cin_ref[...], w1t_ref[...], preferred_element_type=jnp.float32)
    pre_one = pre_one + emb_ref[...]
    gate_one = sig(pre_one)
    act_one = (pre_one * gate_one).astype(jnp.bfloat16)
    stack(act_one.astype(jnp.float32), cone_ref)
    pre_two = jnp.dot(cone_ref[...], w2t_ref[...], preferred_element_type=jnp.float32)
    gate_two = sig(pre_two)
    act_two = (pre_two * gate_two).astype(jnp.bfloat16)
    output = jnp.dot(act_two, pt_ref[...], preferred_element_type=jnp.float32)
    error = skip_ref[...] + scale_ref[:, 0:1] * output
    err_ref[...] = error
    grad_output = (scale_ref[:, 1:2] * error).astype(jnp.bfloat16)
    contract = (((0,), (0,)), ((), ()))
    gp_ref[...] += lax.dot_general(grad_output, act_two, contract, preferred_element_type=jnp.float32)
    grad_act_two = jnp.dot(grad_output, pm_ref[...], preferred_element_type=jnp.float32)
    slope_two = gate_two * (1.0 + pre_two * (1.0 - gate_two))
    grad_pre_two = (grad_act_two * slope_two).astype(jnp.bfloat16)
    g2_ref[...] += lax.dot_general(grad_pre_two, cone_ref[...], contract, preferred_element_type=jnp.float32)
    grad_act_one = jnp.zeros((rows, channels), jnp.float32)
    for tap, (row_step, col_step) in enumerate(TAPS):
        shift = row_step * PATCH + col_step
        piece = jnp.dot(grad_pre_two, w2_ref[:, tap * channels : (tap + 1) * channels],
                        preferred_element_type=jnp.float32)
        moved = piece if shift == 0 else pltpu.roll(piece, shift % rows, 0)
        grad_act_one = grad_act_one + moved * mask_ref[:, 8 - tap : 9 - tap]
    slope_one = gate_one * (1.0 + pre_one * (1.0 - gate_one))
    grad_pre_one = (grad_act_one * slope_one).astype(jnp.bfloat16)
    g1_ref[...] += lax.dot_general(grad_pre_one, cin_ref[...], contract, preferred_element_type=jnp.float32)
    wide = grad_pre_one.astype(jnp.float32)
    for group in range(groups):
        sums_ref[group : group + 1, :] = jnp.sum(wide[group * cells : (group + 1) * cells], axis=0, keepdims=True)


def patch_pass(xin, skip, scale, emb, conv_one, conv_two, out_proj, group=16, interpret=False):
    rows_all, channels = xin.shape
    cells = PATCH * PATCH
    patches = rows_all // cells
    rows = group * cells
    steps = patches // group
    width = conv_one.shape[1]
    outs = conv_one.shape[0]
    targets = out_proj.shape[0]
    masks = tap_masks(rows)
    block = lambda shape: pl.BlockSpec(shape, lambda i: (i, 0))
    whole = lambda shape: pl.BlockSpec(shape, lambda i: (0, 0))
    return pl.pallas_call(
        patch_kernel,
        grid=(steps,),
        in_specs=[
            block((rows, channels)),
            block((rows, targets)),
            block((rows, 8)),
            block((rows, outs)),
            whole((rows, 16)),
            whole((width, outs)),
            whole((width, outs)),
            whole((outs, width)),
            whole((outs, targets)),
            whole((targets, outs)),
        ],
        out_specs=[
            block((rows, targets)),
            block((group, outs)),
            whole((outs, width)),
            whole((outs, width)),
            whole((targets, outs)),
        ],
        out_shape=[
            jax.ShapeDtypeStruct((rows_all, targets), jnp.float32),
            jax.ShapeDtypeStruct((patches, outs), jnp.float32),
            jax.ShapeDtypeStruct((outs, width), jnp.float32),
            jax.ShapeDtypeStruct((outs, width), jnp.float32),
            jax.ShapeDtypeStruct((targets, outs), jnp.float32),
        ],
        scratch_shapes=[pltpu.VMEM((rows, width), jnp.bfloat16), pltpu.VMEM((rows, width), jnp.bfloat16)],
        compiler_params=pltpu.CompilerParams(dimension_semantics=("arbitrary",)),
        interpret=interpret,
    )(xin, skip, scale, emb, masks, conv_one.T, conv_two.T, conv_two, out_proj.T, out_proj)


def kernel_blocks(mean_part, target_part, noise_part, step_ids, in_use, weights, interpret=False):
    conv_one, conv_two, out_proj, step_embed = weights
    patch_count, targets, cells = mean_part.shape
    level_count = step_embed.shape[0]
    sigma_table = noise_levels(level_count)
    step_hot = (step_ids[:, None] == jnp.arange(level_count, dtype=jnp.int32)[None, :]).astype(
        jnp.float32
    )
    sigma = jnp.sum(step_hot * sigma_table[None, :], axis=1)
    sigma_sq = sigma * sigma + 1.0
    scale_in = (1.0 / jnp.sqrt(sigma_sq))[:, None, None]
    scale_skip = (1.0 / sigma_sq)[:, None, None]
    scale_out = sigma / jnp.sqrt(sigma_sq)
    weight_loss = sigma_sq / (sigma * sigma)
    mean_float = mean_part.astype(jnp.float32)
    residual = target_part.astype(jnp.float32) - mean_float
    noisy = residual + sigma[:, None, None] * noise_part.astype(jnp.float32)
    inputs = jnp.concatenate([scale_in * noisy, mean_float], axis=1).astype(jnp.bfloat16)
    xin = jnp.swapaxes(inputs, 1, 2).reshape(patch_count * cells, 2 * targets)
    skip = jnp.swapaxes(scale_skip * noisy - residual, 1, 2).reshape(patch_count * cells, targets)
    factor = 2.0 * weight_loss * in_use / (targets * cells)
    per_patch = jnp.stack([scale_out, factor * scale_out], axis=1)
    per_patch = jnp.pad(per_patch, ((0, 0), (0, 6)))
    scale = jnp.broadcast_to(per_patch[:, None, :], (patch_count, cells, 8)).reshape(-1, 8)
    embedded = jnp.sum(step_hot[:, :, None] * step_embed[None, :, :], axis=1)
    emb = jnp.broadcast_to(embedded[:, None, :], (patch_count, cells, embedded.shape[1]))
    emb = emb.reshape(patch_count * cells, embedded.shape[1])
    error, pixel_sums, grad_one, grad_two, grad_proj = patch_pass(
        xin, skip, scale, emb, conv_one, conv_two, out_proj, interpret=interpret
    )
    error = error.reshape(patch_count, cells * targets)
    losses = weight_loss * jnp.mean(error * error, axis=1) * in_use
    grad_table = jnp.sum(step_hot[:, :, None] * pixel_sums[:, None, :], axis=0)
    return (losses, (grad_one, grad_two, grad_proj, grad_table))


def owner_tables(region_rows, strip_index):
    owners = region_rows[:, :, 2]
    earlier = (
        jnp.arange(owners.shape[1], dtype=jnp.int32)[None, :, None]
        > jnp.arange(owners.shape[1], dtype=jnp.int32)[None, None, :]
    )
    same = owners[:, :, None] == owners[:, None, :]
    pair_rank = jnp.sum((same & earlier).astype(jnp.int32), axis=2)
    mine = (owners == strip_index).astype(jnp.int32)
    flat = mine.reshape(-1)
    owner_slot = (jnp.cumsum(flat) - flat).reshape(owners.shape)
    return (owners, pair_rank, owner_slot)


def noise_routes(region_rows, owners, pair_rank, owner_slot, strip_index, capacity):
    hits = (
        (owners == strip_index)[:, :, None]
        & (pair_rank[:, :, None] == jnp.arange(capacity, dtype=jnp.int32)[None, None, :])
    ).astype(jnp.int32)
    return jnp.sum(hits * owner_slot[:, :, None], axis=1)


def exchange_sum(flat, steps):
    spread = 1
    for _, distance in steps:
        spread *= 2
    size = flat.shape[0]
    unit = spread * 8
    padded = (size + unit - 1) // unit * unit
    values = jnp.pad(flat, (0, padded - size))
    places = {axis: lax.axis_index(axis) for axis, _ in steps}
    for axis, distance in steps:
        count = lax.axis_size(axis)
        half = values.shape[0] // 2
        low, high = values[:half], values[half:]
        upper = (places[axis] // distance) % 2 == 1
        route = [(i, i ^ distance) for i in range(count)]
        kept = jnp.where(upper, high, low)
        sent = jnp.where(upper, low, high)
        values = kept + lax.ppermute(sent, axis, route)
    for axis, distance in reversed(steps):
        count = lax.axis_size(axis)
        upper = (places[axis] // distance) % 2 == 1
        route = [(i, i ^ distance) for i in range(count)]
        other = lax.ppermute(values, axis, route)
        values = jnp.where(
            upper, jnp.concatenate([other, values]), jnp.concatenate([values, other])
        )
    return values[:size]


def reduce_steps():
    sizes = {axis: lax.axis_size(axis) for axis in ("segment", "rows", "dp")}
    steps = []
    distance = 1
    while distance < max(sizes.values()):
        for axis in ("segment", "rows", "dp"):
            if distance < sizes[axis]:
                steps.append((axis, distance))
        distance *= 2
    return steps


def cut_patches(source_grid, row_at, col_at, height):
    zero_index = jnp.zeros((), jnp.int32)

    def cut(row_start, col_start):
        piece = lax.dynamic_slice(
            source_grid,
            (zero_index, zero_index, row_start, col_start),
            (2, source_grid.shape[1], height, height),
        )
        return piece.reshape(2, source_grid.shape[1], height * height)

    return jax.vmap(cut)(row_at, col_at)


def per_device(
    coarse, target, noise, regions, reg_conv, reg_out, conv_one, conv_two, out_proj, step_embed
):
    strips = lax.axis_size("rows")
    strip_index = lax.axis_index("rows")
    sample_count = lax.axis_size("segment") * lax.axis_size("dp")
    sample_index = lax.axis_index("segment") * lax.axis_size("dp") + lax.axis_index("dp")
    region_rows = regions[0]
    per_strip = region_rows.shape[1]
    capacity = max(2, (2 * per_strip + strips - 1) // strips)
    weights = (conv_one, conv_two, out_proj, step_embed)
    owners, pair_rank, owner_slot = owner_tables(region_rows, strip_index)
    send_slot = noise_routes(region_rows, owners, pair_rank, owner_slot, strip_index, capacity)
    outgoing = jnp.take(noise[0, 0], send_slot.reshape(-1), axis=0)
    outgoing = outgoing.reshape((strips, capacity) + outgoing.shape[1:])
    received = lax.all_to_all(outgoing, "rows", split_axis=0, concat_axis=0, tiled=True)
    count = strips
    above = lax.ppermute(coarse[:, :, -1:], "rows", [(i, i + 1) for i in range(count - 1)])
    after = lax.ppermute(coarse, "rows", [(i + 1, i) for i in range(count - 1)])
    height = coarse.shape[2]
    later = lax.ppermute(target[:, :, : height - 1], "rows", [(i + 1, i) for i in range(count - 1)])
    rimmed = jnp.concatenate([above, coarse, after], axis=2)
    mean_all = jnp.transpose(regress(rimmed[0], reg_conv, reg_out), (2, 0, 1))
    mean_strip = mean_all[:, :height]
    own_regions = lax.dynamic_index_in_dim(region_rows, strip_index, 0, keepdims=False)
    own_pairs = lax.dynamic_index_in_dim(pair_rank, strip_index, 0, keepdims=False)
    extended = jnp.stack([mean_all[:, : 2 * height - 1], jnp.concatenate([target[0], later[0]], axis=1)])
    patches = cut_patches(extended, own_regions[:, 0], own_regions[:, 1], height)
    flat_recv = received.reshape((strips * capacity,) + received.shape[2:])
    patch_noise = jnp.take(flat_recv, own_regions[:, 2] * capacity + own_pairs, axis=0)
    in_use = jnp.ones((per_strip,), jnp.float32)
    losses, gradients = kernel_blocks(
        patches[:, 0], patches[:, 1], patch_noise, own_regions[:, 3], in_use, weights
    )
    owner_hot = (own_regions[:, 2][:, None] == jnp.arange(strips, dtype=jnp.int32)[None, :])
    owner_part = jnp.sum(owner_hot.astype(jnp.float32) * losses[:, None], axis=0)
    sample_hot = (jnp.arange(sample_count, dtype=jnp.int32) == sample_index).astype(jnp.float32)
    owner_table = sample_hot[:, None] * owner_part[None, :]
    pieces = (gradients[0], gradients[1], gradients[2], gradients[3], owner_table)
    flat = jnp.concatenate([piece.reshape(-1) for piece in pieces])
    summed = exchange_sum(flat, reduce_steps())
    results = []
    offset = 0
    for piece in pieces:
        results.append(summed[offset : offset + piece.size].reshape(piece.shape))
        offset += piece.size
    table = results[4]
    owner_total = lax.dynamic_slice(table, (sample_index, strip_index), (1, 1))
    return (mean_strip[None], owner_total, results[0], results[1], results[2], results[3])


def solution(mesh):
    placed = (
        P(("segment", "dp"), None, "rows", None),
        P(("segment", "dp"), None, "rows", None),
        P(("segment", "dp"), "rows", None, None, None),
        P(("segment", "dp"), None, None, None),
        P(),
        P(),
        P(),
        P(),
        P(),
        P(),
    )
    return jax.shard_map(
        per_device,
        mesh=mesh,
        in_specs=placed,
        out_specs=(
            P(("segment", "dp"), None, "rows", None),
            P(("segment", "dp"), "rows"),
            P(),
            P(),
            P(),
            P(),
        ),
        check_vma=False,
    )
```

```python
import math

import jax
import jax.numpy as jnp
from jax import lax
from jax.experimental import pallas as pl
from jax.experimental.pallas import tpu as pltpu
from jax.sharding import PartitionSpec as P

PATCH = 12


TAPS = ((-1, -1), (-1, 0), (-1, 1), (0, -1), (0, 0), (0, 1), (1, -1), (1, 0), (1, 1))


def padded_2(cells, sides, width):
    for axis, dim in sides:
        count = lax.axis_size(axis)
        ends = count - 1
        head = lax.slice_in_dim(cells, 0, width, axis=dim)
        tail = lax.slice_in_dim(cells, cells.shape[dim] - width, cells.shape[dim], axis=dim)
        cells = jnp.concatenate(
            [
                lax.ppermute(tail, axis, [(i, (i + 1) % count) for i in range(ends)]),
                cells,
                lax.ppermute(head, axis, [((i + 1) % count, i) for i in range(ends)]),
            ],
            axis=dim,
        )
    return cells


def shifted_2(block, axis, distance):
    devices = range(lax.axis_size(axis))
    route = [(i - distance, i) for i in devices if i - distance in devices]
    return lax.ppermute(block, axis, route)


def shifted(values, row_step, col_step, stride):
    length = values.shape[-1]
    margin = stride + 1
    widths = [(0, 0)] * (values.ndim - 1) + [(margin, margin)]
    padded = jnp.pad(values, widths)
    offset = margin + row_step * stride + col_step
    moved = lax.slice_in_dim(padded, offset, offset + length, axis=values.ndim - 1)
    column = jnp.arange(length, dtype=jnp.int32) % stride + col_step
    inside = (column >= 0) & (column < stride)
    return jnp.where(inside, moved, jnp.zeros((), moved.dtype))


def columns(values, stride):
    return jnp.concatenate(
        [shifted(values, row_step, col_step, stride) for row_step, col_step in TAPS], axis=-2
    )


def fold(gradients, stride):
    width = gradients.shape[-2] // 9
    result = jnp.zeros(gradients.shape[:-2] + (width, gradients.shape[-1]), jnp.float32)
    for position, (row_step, col_step) in enumerate(TAPS):
        piece = gradients[..., position * width : (position + 1) * width, :]
        result = result + shifted(piece, -row_step, -col_step, stride)
    return result


def noise_levels(level_count):
    steps_f = jnp.arange(level_count, dtype=jnp.float32)
    return 0.1 * jnp.exp(steps_f * (math.log(100.0) / (level_count - 1)))


def silu_slope(values):
    gate = jax.nn.sigmoid(values)
    return gate * (1.0 + values * (1.0 - gate))


def product(form, left, right):
    return jnp.einsum(form, left, right, preferred_element_type=jnp.float32)


def regress(grid_rows, reg_conv, reg_out):
    channels, height, width = grid_rows.shape
    hidden_count = reg_conv.shape[0]
    kernel = reg_conv.reshape(hidden_count, 3, 3, channels).transpose(1, 2, 3, 0)
    hidden = lax.conv_general_dilated(
        grid_rows[None],
        kernel,
        window_strides=(1, 1),
        padding=((0, 0), (1, 1)),
        dimension_numbers=("NCHW", "HWIO", "NHWC"),
        preferred_element_type=jnp.float32,
    )[0]
    activated = jax.nn.silu(hidden).astype(jnp.bfloat16)
    return product("rqo,co->rqc", activated, reg_out).astype(jnp.bfloat16)


def patch_block(mean_part, target_part, noise_part, step_ids, in_use, weights):
    conv_one, conv_two, out_proj, step_embed = weights
    stride = PATCH
    level_count = step_embed.shape[0]
    sigma_table = noise_levels(level_count)
    step_hot = (step_ids[:, None] == jnp.arange(level_count, dtype=jnp.int32)[None, :]).astype(
        jnp.float32
    )
    sigma = jnp.sum(step_hot * sigma_table[None, :], axis=1)
    sigma_sq = sigma * sigma + 1.0
    scale_in = (1.0 / jnp.sqrt(sigma_sq))[:, None, None]
    scale_skip = (1.0 / sigma_sq)[:, None, None]
    scale_out = (sigma / jnp.sqrt(sigma_sq))[:, None, None]
    weight_loss = sigma_sq / (sigma * sigma)
    mean_float = mean_part.astype(jnp.float32)
    residual = target_part.astype(jnp.float32) - mean_float
    noisy = residual + sigma[:, None, None] * noise_part.astype(jnp.float32)
    inputs = jnp.concatenate([scale_in * noisy, mean_float], axis=1).astype(jnp.bfloat16)
    cols_in = columns(inputs, stride)
    embedded = jnp.sum(step_hot[:, :, None] * step_embed[None, :, :], axis=1)
    pre_one = product("ok,bkp->bop", conv_one, cols_in) + embedded[:, :, None]
    act_one = jax.nn.silu(pre_one).astype(jnp.bfloat16)
    cols_one = columns(act_one, stride)
    pre_two = product("ok,bkp->bop", conv_two, cols_one)
    act_two = jax.nn.silu(pre_two).astype(jnp.bfloat16)
    output = product("co,bop->bcp", out_proj, act_two)
    error = scale_skip * noisy + scale_out * output - residual
    losses = weight_loss * jnp.mean(error * error, axis=(1, 2)) * in_use
    factor = 2.0 * weight_loss * in_use / (error.shape[1] * error.shape[2])
    grad_output = (factor[:, None, None] * scale_out * error).astype(jnp.bfloat16)
    grad_proj = product("bcp,bop->co", grad_output, act_two)
    grad_act_two = product("co,bcp->bop", out_proj, grad_output)
    grad_pre_two = (grad_act_two * silu_slope(pre_two)).astype(jnp.bfloat16)
    grad_two = product("bop,bkp->ok", grad_pre_two, cols_one)
    grad_cols = product("ok,bop->bkp", conv_two, grad_pre_two)
    grad_act_one = fold(grad_cols, stride)
    grad_pre_one = (grad_act_one * silu_slope(pre_one)).astype(jnp.bfloat16)
    grad_one = product("bop,bkp->ok", grad_pre_one, cols_in)
    pixel_sums = jnp.sum(grad_pre_one, axis=2, dtype=jnp.float32)
    grad_table = jnp.sum(step_hot[:, :, None] * pixel_sums[:, None, :], axis=0)
    return (losses, (grad_one, grad_two, grad_proj, grad_table))


def run_blocks(mean_part, target_part, noise_part, step_ids, in_use, weights):
    patch_count = mean_part.shape[0]
    blocks = patch_count // 4

    def regroup(values):
        return values.reshape((blocks, 4) + values.shape[1:])

    def advance(running, group_block):
        losses, gradients = patch_block(
            group_block[0], group_block[1], group_block[2], group_block[3], group_block[4], weights
        )
        summed = (
            running[0] + gradients[0],
            running[1] + gradients[1],
            running[2] + gradients[2],
            running[3] + gradients[3],
        )
        return (summed, losses)

    initial = (
        jnp.zeros(weights[0].shape, jnp.float32),
        jnp.zeros(weights[1].shape, jnp.float32),
        jnp.zeros(weights[2].shape, jnp.float32),
        jnp.zeros(weights[3].shape, jnp.float32),
    )
    stacked = (
        regroup(mean_part),
        regroup(target_part),
        regroup(noise_part),
        regroup(step_ids),
        regroup(in_use),
    )
    gradients, losses = lax.scan(advance, initial, stacked)
    return (losses.reshape(patch_count), gradients)


def tap_masks(rows):
    cell = jnp.arange(rows, dtype=jnp.int32) % (PATCH * PATCH)
    line = cell // PATCH
    place = cell % PATCH
    cols = []
    for row_step, col_step in TAPS:
        inside = (line + row_step >= 0) & (line + row_step < PATCH)
        inside = inside & (place + col_step >= 0) & (place + col_step < PATCH)
        cols.append(inside.astype(jnp.float32))
    cols += [jnp.zeros((rows,), jnp.float32)] * (16 - len(cols))
    return jnp.stack(cols, axis=1)


def sig(values):
    return 1.0 / (1.0 + jnp.exp(-values))


def patch_kernel(xin_ref, skip_ref, scale_ref, emb_ref, mask_ref, w1t_ref, w2t_ref, w2_ref,
                 pt_ref, pm_ref, err_ref, sums_ref, g1_ref, g2_ref, gp_ref, cin_ref, cone_ref):
    rows = xin_ref.shape[0]
    groups = sums_ref.shape[0]
    cells = rows // groups
    channels = xin_ref.shape[1]

    @pl.when(pl.program_id(0) == 0)
    def _():
        g1_ref[...] = jnp.zeros_like(g1_ref)
        g2_ref[...] = jnp.zeros_like(g2_ref)
        gp_ref[...] = jnp.zeros_like(gp_ref)

    def stack(values, target):
        for tap, (row_step, col_step) in enumerate(TAPS):
            shift = row_step * PATCH + col_step
            moved = values if shift == 0 else pltpu.roll(values, (-shift) % rows, 0)
            moved = moved * mask_ref[:, tap : tap + 1]
            target[:, tap * channels : (tap + 1) * channels] = moved.astype(target.dtype)

    stack(xin_ref[...].astype(jnp.float32), cin_ref)
    pre_one = jnp.dot(cin_ref[...], w1t_ref[...], preferred_element_type=jnp.float32)
    pre_one = pre_one + emb_ref[...]
    gate_one = sig(pre_one)
    act_one = (pre_one * gate_one).astype(jnp.bfloat16)
    stack(act_one.astype(jnp.float32), cone_ref)
    pre_two = jnp.dot(cone_ref[...], w2t_ref[...], preferred_element_type=jnp.float32)
    gate_two = sig(pre_two)
    act_two = (pre_two * gate_two).astype(jnp.bfloat16)
    output = jnp.dot(act_two, pt_ref[...], preferred_element_type=jnp.float32)
    error = skip_ref[...] + scale_ref[:, 0:1] * output
    err_ref[...] = error
    grad_output = (scale_ref[:, 1:2] * error).astype(jnp.bfloat16)
    contract = (((0,), (0,)), ((), ()))
    gp_ref[...] += lax.dot_general(grad_output, act_two, contract, preferred_element_type=jnp.float32)
    grad_act_two = jnp.dot(grad_output, pm_ref[...], preferred_element_type=jnp.float32)
    slope_two = gate_two * (1.0 + pre_two * (1.0 - gate_two))
    grad_pre_two = (grad_act_two * slope_two).astype(jnp.bfloat16)
    g2_ref[...] += lax.dot_general(grad_pre_two, cone_ref[...], contract, preferred_element_type=jnp.float32)
    grad_act_one = jnp.zeros((rows, channels), jnp.float32)
    for tap, (row_step, col_step) in enumerate(TAPS):
        shift = row_step * PATCH + col_step
        piece = jnp.dot(grad_pre_two, w2_ref[:, tap * channels : (tap + 1) * channels],
                        preferred_element_type=jnp.float32)
        moved = piece if shift == 0 else pltpu.roll(piece, shift % rows, 0)
        grad_act_one = grad_act_one + moved * mask_ref[:, 8 - tap : 9 - tap]
    slope_one = gate_one * (1.0 + pre_one * (1.0 - gate_one))
    grad_pre_one = (grad_act_one * slope_one).astype(jnp.bfloat16)
    g1_ref[...] += lax.dot_general(grad_pre_one, cin_ref[...], contract, preferred_element_type=jnp.float32)
    wide = grad_pre_one.astype(jnp.float32)
    for group in range(groups):
        sums_ref[group : group + 1, :] = jnp.sum(wide[group * cells : (group + 1) * cells], axis=0, keepdims=True)


def patch_pass(xin, skip, scale, emb, conv_one, conv_two, out_proj, group=8, interpret=False):
    rows_all, channels = xin.shape
    cells = PATCH * PATCH
    patches = rows_all // cells
    rows = group * cells
    steps = patches // group
    width = conv_one.shape[1]
    outs = conv_one.shape[0]
    targets = out_proj.shape[0]
    masks = tap_masks(rows)
    block = lambda shape: pl.BlockSpec(shape, lambda i: (i, 0))
    whole = lambda shape: pl.BlockSpec(shape, lambda i: (0, 0))
    return pl.pallas_call(
        patch_kernel,
        grid=(steps,),
        in_specs=[
            block((rows, channels)),
            block((rows, targets)),
            block((rows, 8)),
            block((rows, outs)),
            whole((rows, 16)),
            whole((width, outs)),
            whole((width, outs)),
            whole((outs, width)),
            whole((outs, targets)),
            whole((targets, outs)),
        ],
        out_specs=[
            block((rows, targets)),
            block((group, outs)),
            whole((outs, width)),
            whole((outs, width)),
            whole((targets, outs)),
        ],
        out_shape=[
            jax.ShapeDtypeStruct((rows_all, targets), jnp.float32),
            jax.ShapeDtypeStruct((patches, outs), jnp.float32),
            jax.ShapeDtypeStruct((outs, width), jnp.float32),
            jax.ShapeDtypeStruct((outs, width), jnp.float32),
            jax.ShapeDtypeStruct((targets, outs), jnp.float32),
        ],
        scratch_shapes=[pltpu.VMEM((rows, width), jnp.bfloat16), pltpu.VMEM((rows, width), jnp.bfloat16)],
        compiler_params=pltpu.CompilerParams(dimension_semantics=("arbitrary",)),
        interpret=interpret,
    )(xin, skip, scale, emb, masks, conv_one.T, conv_two.T, conv_two, out_proj.T, out_proj)


def kernel_blocks(mean_part, target_part, noise_part, step_ids, in_use, weights, interpret=False):
    conv_one, conv_two, out_proj, step_embed = weights
    patch_count, targets, cells = mean_part.shape
    level_count = step_embed.shape[0]
    sigma_table = noise_levels(level_count)
    step_hot = (step_ids[:, None] == jnp.arange(level_count, dtype=jnp.int32)[None, :]).astype(
        jnp.float32
    )
    sigma = jnp.sum(step_hot * sigma_table[None, :], axis=1)
    sigma_sq = sigma * sigma + 1.0
    scale_in = (1.0 / jnp.sqrt(sigma_sq))[:, None, None]
    scale_skip = (1.0 / sigma_sq)[:, None, None]
    scale_out = sigma / jnp.sqrt(sigma_sq)
    weight_loss = sigma_sq / (sigma * sigma)
    mean_float = mean_part.astype(jnp.float32)
    residual = target_part.astype(jnp.float32) - mean_float
    noisy = residual + sigma[:, None, None] * noise_part.astype(jnp.float32)
    inputs = jnp.concatenate([scale_in * noisy, mean_float], axis=1).astype(jnp.bfloat16)
    xin = jnp.swapaxes(inputs, 1, 2).reshape(patch_count * cells, 2 * targets)
    skip = jnp.swapaxes(scale_skip * noisy - residual, 1, 2).reshape(patch_count * cells, targets)
    factor = 2.0 * weight_loss * in_use / (targets * cells)
    per_patch = jnp.stack([scale_out, factor * scale_out], axis=1)
    per_patch = jnp.pad(per_patch, ((0, 0), (0, 6)))
    scale = jnp.broadcast_to(per_patch[:, None, :], (patch_count, cells, 8)).reshape(-1, 8)
    embedded = jnp.sum(step_hot[:, :, None] * step_embed[None, :, :], axis=1)
    emb = jnp.broadcast_to(embedded[:, None, :], (patch_count, cells, embedded.shape[1]))
    emb = emb.reshape(patch_count * cells, embedded.shape[1])
    error, pixel_sums, grad_one, grad_two, grad_proj = patch_pass(
        xin, skip, scale, emb, conv_one, conv_two, out_proj, interpret=interpret
    )
    error = error.reshape(patch_count, cells * targets)
    losses = weight_loss * jnp.mean(error * error, axis=1) * in_use
    grad_table = jnp.sum(step_hot[:, :, None] * pixel_sums[:, None, :], axis=0)
    return (losses, (grad_one, grad_two, grad_proj, grad_table))


def owner_tables(region_rows, strip_index):
    owners = region_rows[:, :, 2]
    earlier = (
        jnp.arange(owners.shape[1], dtype=jnp.int32)[None, :, None]
        > jnp.arange(owners.shape[1], dtype=jnp.int32)[None, None, :]
    )
    same = owners[:, :, None] == owners[:, None, :]
    pair_rank = jnp.sum((same & earlier).astype(jnp.int32), axis=2)
    mine = (owners == strip_index).astype(jnp.int32)
    flat = mine.reshape(-1)
    owner_slot = (jnp.cumsum(flat) - flat).reshape(owners.shape)
    return (owners, pair_rank, owner_slot)


def noise_routes(region_rows, owners, pair_rank, owner_slot, strip_index, capacity):
    hits = (
        (owners == strip_index)[:, :, None]
        & (pair_rank[:, :, None] == jnp.arange(capacity, dtype=jnp.int32)[None, None, :])
    ).astype(jnp.int32)
    return jnp.sum(hits * owner_slot[:, :, None], axis=1)


def exchange_sum(flat, steps):
    spread = 1
    for _, distance in steps:
        spread *= 2
    size = flat.shape[0]
    unit = spread * 8
    padded = (size + unit - 1) // unit * unit
    values = jnp.pad(flat, (0, padded - size))
    places = {axis: lax.axis_index(axis) for axis, _ in steps}
    for axis, distance in steps:
        count = lax.axis_size(axis)
        half = values.shape[0] // 2
        upper = (places[axis] // distance) % 2
        route = [(i, i ^ distance) for i in range(count)]
        kept = lax.dynamic_slice_in_dim(values, upper * half, half)
        sent = lax.dynamic_slice_in_dim(values, (1 - upper) * half, half)
        values = kept + lax.ppermute(sent, axis, route)
    for axis, distance in reversed(steps):
        count = lax.axis_size(axis)
        upper = (places[axis] // distance) % 2
        route = [(i, i ^ distance) for i in range(count)]
        other = lax.ppermute(values, axis, route)
        width = values.shape[0]
        joined = jnp.zeros((2 * width,), values.dtype)
        joined = lax.dynamic_update_slice_in_dim(joined, values, upper * width, 0)
        values = lax.dynamic_update_slice_in_dim(joined, other, (1 - upper) * width, 0)
    return values[:size]


def reduce_steps():
    sizes = {axis: lax.axis_size(axis) for axis in ("segment", "rows", "dp")}
    steps = []
    distance = 1
    while distance < max(sizes.values()):
        for axis in ("segment", "rows", "dp"):
            if distance < sizes[axis]:
                steps.append((axis, distance))
        distance *= 2
    return steps


def cut_patches(source_grid, row_at, col_at, height):
    zero_index = jnp.zeros((), jnp.int32)

    def cut(row_start, col_start):
        piece = lax.dynamic_slice(
            source_grid,
            (zero_index, zero_index, row_start, col_start),
            (2, source_grid.shape[1], height, height),
        )
        return piece.reshape(2, source_grid.shape[1], height * height)

    return jax.vmap(cut)(row_at, col_at)


def per_device(
    coarse, target, noise, regions, reg_conv, reg_out, conv_one, conv_two, out_proj, step_embed
):
    strips = lax.axis_size("rows")
    strip_index = lax.axis_index("rows")
    sample_count = lax.axis_size("segment") * lax.axis_size("dp")
    sample_index = lax.axis_index("segment") * lax.axis_size("dp") + lax.axis_index("dp")
    region_rows = regions[0]
    per_strip = region_rows.shape[1]
    capacity = max(2, (2 * per_strip + strips - 1) // strips)
    weights = (conv_one, conv_two, out_proj, step_embed)
    owners, pair_rank, owner_slot = owner_tables(region_rows, strip_index)
    send_slot = noise_routes(region_rows, owners, pair_rank, owner_slot, strip_index, capacity)
    outgoing = jnp.take(noise[0, 0], send_slot.reshape(-1), axis=0)
    outgoing = outgoing.reshape((strips, capacity) + outgoing.shape[1:])
    received = lax.all_to_all(outgoing, "rows", split_axis=0, concat_axis=0, tiled=True)
    count = strips
    above = lax.ppermute(coarse[:, :, -1:], "rows", [(i, i + 1) for i in range(count - 1)])
    after = lax.ppermute(coarse, "rows", [(i + 1, i) for i in range(count - 1)])
    height = coarse.shape[2]
    later = lax.ppermute(target[:, :, : height - 1], "rows", [(i + 1, i) for i in range(count - 1)])
    rimmed = jnp.concatenate([above, coarse, after], axis=2)
    mean_all = jnp.transpose(regress(rimmed[0], reg_conv, reg_out), (2, 0, 1))
    mean_strip = mean_all[:, :height]
    own_regions = lax.dynamic_index_in_dim(region_rows, strip_index, 0, keepdims=False)
    own_pairs = lax.dynamic_index_in_dim(pair_rank, strip_index, 0, keepdims=False)
    extended = jnp.stack([mean_all[:, : 2 * height - 1], jnp.concatenate([target[0], later[0]], axis=1)])
    patches = cut_patches(extended, own_regions[:, 0], own_regions[:, 1], height)
    flat_recv = received.reshape((strips * capacity,) + received.shape[2:])
    patch_noise = jnp.take(flat_recv, own_regions[:, 2] * capacity + own_pairs, axis=0)
    in_use = jnp.ones((per_strip,), jnp.float32)
    losses, gradients = kernel_blocks(
        patches[:, 0], patches[:, 1], patch_noise, own_regions[:, 3], in_use, weights
    )
    owner_hot = (own_regions[:, 2][:, None] == jnp.arange(strips, dtype=jnp.int32)[None, :])
    owner_part = jnp.sum(owner_hot.astype(jnp.float32) * losses[:, None], axis=0)
    sample_hot = (jnp.arange(sample_count, dtype=jnp.int32) == sample_index).astype(jnp.float32)
    owner_table = sample_hot[:, None] * owner_part[None, :]
    pieces = (gradients[0], gradients[1], gradients[2], gradients[3], owner_table)
    flat = jnp.concatenate([piece.reshape(-1) for piece in pieces])
    summed = exchange_sum(flat, reduce_steps())
    results = []
    offset = 0
    for piece in pieces:
        results.append(summed[offset : offset + piece.size].reshape(piece.shape))
        offset += piece.size
    table = results[4]
    owner_total = lax.dynamic_slice(table, (sample_index, strip_index), (1, 1))
    return (mean_strip[None], owner_total, results[0], results[1], results[2], results[3])


def solution(mesh):
    placed = (
        P(("segment", "dp"), None, "rows", None),
        P(("segment", "dp"), None, "rows", None),
        P(("segment", "dp"), "rows", None, None, None),
        P(("segment", "dp"), None, None, None),
        P(),
        P(),
        P(),
        P(),
        P(),
        P(),
    )
    return jax.shard_map(
        per_device,
        mesh=mesh,
        in_specs=placed,
        out_specs=(
            P(("segment", "dp"), None, "rows", None),
            P(("segment", "dp"), "rows"),
            P(),
            P(),
            P(),
            P(),
        ),
        check_vma=False,
    )
```

```python
import math

import jax
import jax.numpy as jnp
from jax import lax
from jax.experimental import pallas as pl
from jax.experimental.pallas import tpu as pltpu
from jax.sharding import PartitionSpec as P

PATCH = 12


TAPS = ((-1, -1), (-1, 0), (-1, 1), (0, -1), (0, 0), (0, 1), (1, -1), (1, 0), (1, 1))


def padded_2(cells, sides, width):
    for axis, dim in sides:
        count = lax.axis_size(axis)
        ends = count - 1
        head = lax.slice_in_dim(cells, 0, width, axis=dim)
        tail = lax.slice_in_dim(cells, cells.shape[dim] - width, cells.shape[dim], axis=dim)
        cells = jnp.concatenate(
            [
                lax.ppermute(tail, axis, [(i, (i + 1) % count) for i in range(ends)]),
                cells,
                lax.ppermute(head, axis, [((i + 1) % count, i) for i in range(ends)]),
            ],
            axis=dim,
        )
    return cells


def shifted_2(block, axis, distance):
    devices = range(lax.axis_size(axis))
    route = [(i - distance, i) for i in devices if i - distance in devices]
    return lax.ppermute(block, axis, route)


def shifted(values, row_step, col_step, stride):
    length = values.shape[-1]
    margin = stride + 1
    widths = [(0, 0)] * (values.ndim - 1) + [(margin, margin)]
    padded = jnp.pad(values, widths)
    offset = margin + row_step * stride + col_step
    moved = lax.slice_in_dim(padded, offset, offset + length, axis=values.ndim - 1)
    column = jnp.arange(length, dtype=jnp.int32) % stride + col_step
    inside = (column >= 0) & (column < stride)
    return jnp.where(inside, moved, jnp.zeros((), moved.dtype))


def columns(values, stride):
    return jnp.concatenate(
        [shifted(values, row_step, col_step, stride) for row_step, col_step in TAPS], axis=-2
    )


def fold(gradients, stride):
    width = gradients.shape[-2] // 9
    result = jnp.zeros(gradients.shape[:-2] + (width, gradients.shape[-1]), jnp.float32)
    for position, (row_step, col_step) in enumerate(TAPS):
        piece = gradients[..., position * width : (position + 1) * width, :]
        result = result + shifted(piece, -row_step, -col_step, stride)
    return result


def noise_levels(level_count):
    steps_f = jnp.arange(level_count, dtype=jnp.float32)
    return 0.1 * jnp.exp(steps_f * (math.log(100.0) / (level_count - 1)))


def silu_slope(values):
    gate = jax.nn.sigmoid(values)
    return gate * (1.0 + values * (1.0 - gate))


def product(form, left, right):
    return jnp.einsum(form, left, right, preferred_element_type=jnp.float32)


def regress(grid_rows, reg_conv, reg_out):
    channels, height, width = grid_rows.shape
    hidden_count = reg_conv.shape[0]
    kernel = reg_conv.reshape(hidden_count, 3, 3, channels).transpose(1, 2, 3, 0)
    hidden = lax.conv_general_dilated(
        grid_rows[None],
        kernel,
        window_strides=(1, 1),
        padding=((0, 0), (1, 1)),
        dimension_numbers=("NCHW", "HWIO", "NHWC"),
        preferred_element_type=jnp.float32,
    )[0]
    activated = jax.nn.silu(hidden).astype(jnp.bfloat16)
    return product("rqo,co->rqc", activated, reg_out).astype(jnp.bfloat16)


def patch_block(mean_part, target_part, noise_part, step_ids, in_use, weights):
    conv_one, conv_two, out_proj, step_embed = weights
    stride = PATCH
    level_count = step_embed.shape[0]
    sigma_table = noise_levels(level_count)
    step_hot = (step_ids[:, None] == jnp.arange(level_count, dtype=jnp.int32)[None, :]).astype(
        jnp.float32
    )
    sigma = jnp.sum(step_hot * sigma_table[None, :], axis=1)
    sigma_sq = sigma * sigma + 1.0
    scale_in = (1.0 / jnp.sqrt(sigma_sq))[:, None, None]
    scale_skip = (1.0 / sigma_sq)[:, None, None]
    scale_out = (sigma / jnp.sqrt(sigma_sq))[:, None, None]
    weight_loss = sigma_sq / (sigma * sigma)
    mean_float = mean_part.astype(jnp.float32)
    residual = target_part.astype(jnp.float32) - mean_float
    noisy = residual + sigma[:, None, None] * noise_part.astype(jnp.float32)
    inputs = jnp.concatenate([scale_in * noisy, mean_float], axis=1).astype(jnp.bfloat16)
    cols_in = columns(inputs, stride)
    embedded = jnp.sum(step_hot[:, :, None] * step_embed[None, :, :], axis=1)
    pre_one = product("ok,bkp->bop", conv_one, cols_in) + embedded[:, :, None]
    act_one = jax.nn.silu(pre_one).astype(jnp.bfloat16)
    cols_one = columns(act_one, stride)
    pre_two = product("ok,bkp->bop", conv_two, cols_one)
    act_two = jax.nn.silu(pre_two).astype(jnp.bfloat16)
    output = product("co,bop->bcp", out_proj, act_two)
    error = scale_skip * noisy + scale_out * output - residual
    losses = weight_loss * jnp.mean(error * error, axis=(1, 2)) * in_use
    factor = 2.0 * weight_loss * in_use / (error.shape[1] * error.shape[2])
    grad_output = (factor[:, None, None] * scale_out * error).astype(jnp.bfloat16)
    grad_proj = product("bcp,bop->co", grad_output, act_two)
    grad_act_two = product("co,bcp->bop", out_proj, grad_output)
    grad_pre_two = (grad_act_two * silu_slope(pre_two)).astype(jnp.bfloat16)
    grad_two = product("bop,bkp->ok", grad_pre_two, cols_one)
    grad_cols = product("ok,bop->bkp", conv_two, grad_pre_two)
    grad_act_one = fold(grad_cols, stride)
    grad_pre_one = (grad_act_one * silu_slope(pre_one)).astype(jnp.bfloat16)
    grad_one = product("bop,bkp->ok", grad_pre_one, cols_in)
    pixel_sums = jnp.sum(grad_pre_one, axis=2, dtype=jnp.float32)
    grad_table = jnp.sum(step_hot[:, :, None] * pixel_sums[:, None, :], axis=0)
    return (losses, (grad_one, grad_two, grad_proj, grad_table))


def run_blocks(mean_part, target_part, noise_part, step_ids, in_use, weights):
    patch_count = mean_part.shape[0]
    blocks = patch_count // 4

    def regroup(values):
        return values.reshape((blocks, 4) + values.shape[1:])

    def advance(running, group_block):
        losses, gradients = patch_block(
            group_block[0], group_block[1], group_block[2], group_block[3], group_block[4], weights
        )
        summed = (
            running[0] + gradients[0],
            running[1] + gradients[1],
            running[2] + gradients[2],
            running[3] + gradients[3],
        )
        return (summed, losses)

    initial = (
        jnp.zeros(weights[0].shape, jnp.float32),
        jnp.zeros(weights[1].shape, jnp.float32),
        jnp.zeros(weights[2].shape, jnp.float32),
        jnp.zeros(weights[3].shape, jnp.float32),
    )
    stacked = (
        regroup(mean_part),
        regroup(target_part),
        regroup(noise_part),
        regroup(step_ids),
        regroup(in_use),
    )
    gradients, losses = lax.scan(advance, initial, stacked)
    return (losses.reshape(patch_count), gradients)


def tap_masks(rows):
    cell = jnp.arange(rows, dtype=jnp.int32) % (PATCH * PATCH)
    line = cell // PATCH
    place = cell % PATCH
    cols = []
    for row_step, col_step in TAPS:
        inside = (line + row_step >= 0) & (line + row_step < PATCH)
        inside = inside & (place + col_step >= 0) & (place + col_step < PATCH)
        cols.append(inside.astype(jnp.float32))
    cols += [jnp.zeros((rows,), jnp.float32)] * (16 - len(cols))
    return jnp.stack(cols, axis=1)


def sig(values):
    return 1.0 / (1.0 + jnp.exp(-values))


def patch_kernel(xin_ref, skip_ref, scale_ref, emb_ref, mask_ref, w1t_ref, w2t_ref, w2_ref,
                 pt_ref, pm_ref, err_ref, sums_ref, g1_ref, g2_ref, gp_ref, cin_ref, cone_ref):
    rows = xin_ref.shape[0]
    groups = sums_ref.shape[0]
    cells = rows // groups
    channels = xin_ref.shape[1]

    @pl.when(pl.program_id(0) == 0)
    def _():
        g1_ref[...] = jnp.zeros_like(g1_ref)
        g2_ref[...] = jnp.zeros_like(g2_ref)
        gp_ref[...] = jnp.zeros_like(gp_ref)

    def stack(values, target):
        for tap, (row_step, col_step) in enumerate(TAPS):
            shift = row_step * PATCH + col_step
            moved = values if shift == 0 else pltpu.roll(values, (-shift) % rows, 0)
            moved = moved * mask_ref[:, tap : tap + 1]
            target[:, tap * channels : (tap + 1) * channels] = moved.astype(target.dtype)

    stack(xin_ref[...].astype(jnp.float32), cin_ref)
    pre_one = jnp.dot(cin_ref[...], w1t_ref[...], preferred_element_type=jnp.float32)
    pre_one = pre_one + emb_ref[...]
    gate_one = sig(pre_one)
    act_one = (pre_one * gate_one).astype(jnp.bfloat16)
    stack(act_one.astype(jnp.float32), cone_ref)
    pre_two = jnp.dot(cone_ref[...], w2t_ref[...], preferred_element_type=jnp.float32)
    gate_two = sig(pre_two)
    act_two = (pre_two * gate_two).astype(jnp.bfloat16)
    output = jnp.dot(act_two, pt_ref[...], preferred_element_type=jnp.float32)
    error = skip_ref[...] + scale_ref[:, 0:1] * output
    err_ref[...] = error
    grad_output = (scale_ref[:, 1:2] * error).astype(jnp.bfloat16)
    contract = (((0,), (0,)), ((), ()))
    gp_ref[...] += lax.dot_general(grad_output, act_two, contract, preferred_element_type=jnp.float32)
    grad_act_two = jnp.dot(grad_output, pm_ref[...], preferred_element_type=jnp.float32)
    slope_two = gate_two * (1.0 + pre_two * (1.0 - gate_two))
    grad_pre_two = (grad_act_two * slope_two).astype(jnp.bfloat16)
    g2_ref[...] += lax.dot_general(grad_pre_two, cone_ref[...], contract, preferred_element_type=jnp.float32)
    grad_act_one = jnp.zeros((rows, channels), jnp.float32)
    for tap, (row_step, col_step) in enumerate(TAPS):
        shift = row_step * PATCH + col_step
        piece = jnp.dot(grad_pre_two, w2_ref[:, tap * channels : (tap + 1) * channels],
                        preferred_element_type=jnp.float32)
        moved = piece if shift == 0 else pltpu.roll(piece, shift % rows, 0)
        grad_act_one = grad_act_one + moved * mask_ref[:, 8 - tap : 9 - tap]
    slope_one = gate_one * (1.0 + pre_one * (1.0 - gate_one))
    grad_pre_one = (grad_act_one * slope_one).astype(jnp.bfloat16)
    g1_ref[...] += lax.dot_general(grad_pre_one, cin_ref[...], contract, preferred_element_type=jnp.float32)
    wide = grad_pre_one.astype(jnp.float32)
    for group in range(groups):
        sums_ref[group : group + 1, :] = jnp.sum(wide[group * cells : (group + 1) * cells], axis=0, keepdims=True)


def patch_pass(xin, skip, scale, emb, conv_one, conv_two, out_proj, group=8, interpret=False):
    rows_all, channels = xin.shape
    cells = PATCH * PATCH
    patches = rows_all // cells
    rows = group * cells
    steps = patches // group
    width = conv_one.shape[1]
    outs = conv_one.shape[0]
    targets = out_proj.shape[0]
    masks = tap_masks(rows)
    block = lambda shape: pl.BlockSpec(shape, lambda i: (i, 0))
    whole = lambda shape: pl.BlockSpec(shape, lambda i: (0, 0))
    return pl.pallas_call(
        patch_kernel,
        grid=(steps,),
        in_specs=[
            block((rows, channels)),
            block((rows, targets)),
            block((rows, 8)),
            block((rows, outs)),
            whole((rows, 16)),
            whole((width, outs)),
            whole((width, outs)),
            whole((outs, width)),
            whole((outs, targets)),
            whole((targets, outs)),
        ],
        out_specs=[
            block((rows, targets)),
            block((group, outs)),
            whole((outs, width)),
            whole((outs, width)),
            whole((targets, outs)),
        ],
        out_shape=[
            jax.ShapeDtypeStruct((rows_all, targets), jnp.float32),
            jax.ShapeDtypeStruct((patches, outs), jnp.float32),
            jax.ShapeDtypeStruct((outs, width), jnp.float32),
            jax.ShapeDtypeStruct((outs, width), jnp.float32),
            jax.ShapeDtypeStruct((targets, outs), jnp.float32),
        ],
        scratch_shapes=[pltpu.VMEM((rows, width), jnp.bfloat16), pltpu.VMEM((rows, width), jnp.bfloat16)],
        compiler_params=pltpu.CompilerParams(dimension_semantics=("arbitrary",)),
        interpret=interpret,
    )(xin, skip, scale, emb, masks, conv_one.T, conv_two.T, conv_two, out_proj.T, out_proj)


def kernel_blocks(mean_part, target_part, noise_part, step_ids, in_use, weights, interpret=False):
    conv_one, conv_two, out_proj, step_embed = weights
    patch_count, targets, cells = mean_part.shape
    level_count = step_embed.shape[0]
    sigma_table = noise_levels(level_count)
    step_hot = (step_ids[:, None] == jnp.arange(level_count, dtype=jnp.int32)[None, :]).astype(
        jnp.float32
    )
    sigma = jnp.sum(step_hot * sigma_table[None, :], axis=1)
    sigma_sq = sigma * sigma + 1.0
    scale_in = (1.0 / jnp.sqrt(sigma_sq))[:, None, None]
    scale_skip = (1.0 / sigma_sq)[:, None, None]
    scale_out = sigma / jnp.sqrt(sigma_sq)
    weight_loss = sigma_sq / (sigma * sigma)
    mean_float = mean_part.astype(jnp.float32)
    residual = target_part.astype(jnp.float32) - mean_float
    noisy = residual + sigma[:, None, None] * noise_part.astype(jnp.float32)
    inputs = jnp.concatenate([scale_in * noisy, mean_float], axis=1).astype(jnp.bfloat16)
    xin = jnp.swapaxes(inputs, 1, 2).reshape(patch_count * cells, 2 * targets)
    skip = jnp.swapaxes(scale_skip * noisy - residual, 1, 2).reshape(patch_count * cells, targets)
    factor = 2.0 * weight_loss * in_use / (targets * cells)
    per_patch = jnp.stack([scale_out, factor * scale_out], axis=1)
    per_patch = jnp.pad(per_patch, ((0, 0), (0, 6)))
    scale = jnp.broadcast_to(per_patch[:, None, :], (patch_count, cells, 8)).reshape(-1, 8)
    embedded = jnp.sum(step_hot[:, :, None] * step_embed[None, :, :], axis=1)
    emb = jnp.broadcast_to(embedded[:, None, :], (patch_count, cells, embedded.shape[1]))
    emb = emb.reshape(patch_count * cells, embedded.shape[1])
    error, pixel_sums, grad_one, grad_two, grad_proj = patch_pass(
        xin, skip, scale, emb, conv_one, conv_two, out_proj, interpret=interpret
    )
    error = error.reshape(patch_count, cells * targets)
    losses = weight_loss * jnp.mean(error * error, axis=1) * in_use
    grad_table = jnp.sum(step_hot[:, :, None] * pixel_sums[:, None, :], axis=0)
    return (losses, (grad_one, grad_two, grad_proj, grad_table))


def owner_tables(region_rows, strip_index):
    owners = region_rows[:, :, 2]
    earlier = (
        jnp.arange(owners.shape[1], dtype=jnp.int32)[None, :, None]
        > jnp.arange(owners.shape[1], dtype=jnp.int32)[None, None, :]
    )
    same = owners[:, :, None] == owners[:, None, :]
    pair_rank = jnp.sum((same & earlier).astype(jnp.int32), axis=2)
    mine = (owners == strip_index).astype(jnp.int32)
    flat = mine.reshape(-1)
    owner_slot = (jnp.cumsum(flat) - flat).reshape(owners.shape)
    return (owners, pair_rank, owner_slot)


def noise_routes(region_rows, owners, pair_rank, owner_slot, strip_index, capacity):
    hits = (
        (owners == strip_index)[:, :, None]
        & (pair_rank[:, :, None] == jnp.arange(capacity, dtype=jnp.int32)[None, None, :])
    ).astype(jnp.int32)
    return jnp.sum(hits * owner_slot[:, :, None], axis=1)


def exchange_sum(flat, steps):
    spread = 1
    for _, distance in steps:
        spread *= 2
    size = flat.shape[0]
    unit = spread * 8
    padded = (size + unit - 1) // unit * unit
    values = jnp.pad(flat, (0, padded - size))
    places = {axis: lax.axis_index(axis) for axis, _ in steps}
    for axis, distance in steps:
        count = lax.axis_size(axis)
        half = values.shape[0] // 2
        low, high = values[:half], values[half:]
        upper = (places[axis] // distance) % 2 == 1
        route = [(i, i ^ distance) for i in range(count)]
        kept = jnp.where(upper, high, low)
        sent = jnp.where(upper, low, high)
        values = kept + lax.ppermute(sent, axis, route)
    for axis, distance in reversed(steps):
        count = lax.axis_size(axis)
        upper = (places[axis] // distance) % 2 == 1
        route = [(i, i ^ distance) for i in range(count)]
        other = lax.ppermute(values, axis, route)
        values = jnp.where(
            upper, jnp.concatenate([other, values]), jnp.concatenate([values, other])
        )
    return values[:size]


def reduce_steps():
    sizes = {axis: lax.axis_size(axis) for axis in ("segment", "rows", "dp")}
    steps = []
    distance = 1
    while distance < max(sizes.values()):
        for axis in ("segment", "rows", "dp"):
            if distance < sizes[axis]:
                steps.append((axis, distance))
        distance *= 2
    return steps


def cut_patches(source_grid, row_at, col_at, height):
    zero_index = jnp.zeros((), jnp.int32)

    def cut(row_start, col_start):
        piece = lax.dynamic_slice(
            source_grid,
            (zero_index, zero_index, row_start, col_start),
            (2, source_grid.shape[1], height, height),
        )
        return piece.reshape(2, source_grid.shape[1], height * height)

    return jax.vmap(cut)(row_at, col_at)


def per_device(
    coarse, target, noise, regions, reg_conv, reg_out, conv_one, conv_two, out_proj, step_embed
):
    strips = lax.axis_size("rows")
    strip_index = lax.axis_index("rows")
    sample_count = lax.axis_size("segment") * lax.axis_size("dp")
    sample_index = lax.axis_index("segment") * lax.axis_size("dp") + lax.axis_index("dp")
    region_rows = regions[0]
    per_strip = region_rows.shape[1]
    capacity = max(2, (2 * per_strip + strips - 1) // strips)
    weights = (conv_one, conv_two, out_proj, step_embed)
    owners, pair_rank, owner_slot = owner_tables(region_rows, strip_index)
    send_slot = noise_routes(region_rows, owners, pair_rank, owner_slot, strip_index, capacity)
    outgoing = jnp.take(noise[0, 0], send_slot.reshape(-1), axis=0)
    outgoing = outgoing.reshape((strips, capacity) + outgoing.shape[1:])
    received = lax.all_to_all(outgoing, "rows", split_axis=0, concat_axis=0, tiled=True)
    count = strips
    above = lax.ppermute(coarse[:, :, -1:], "rows", [(i, i + 1) for i in range(count - 1)])
    height = coarse.shape[2]
    both = jnp.concatenate([coarse, target], axis=1)
    both = lax.ppermute(both, "rows", [(i + 1, i) for i in range(count - 1)])
    after = both[:, : coarse.shape[1]]
    later = both[:, coarse.shape[1] :, : height - 1]
    rimmed = jnp.concatenate([above, coarse, after], axis=2)
    mean_all = jnp.transpose(regress(rimmed[0], reg_conv, reg_out), (2, 0, 1))
    mean_strip = mean_all[:, :height]
    own_regions = lax.dynamic_index_in_dim(region_rows, strip_index, 0, keepdims=False)
    own_pairs = lax.dynamic_index_in_dim(pair_rank, strip_index, 0, keepdims=False)
    extended = jnp.stack([mean_all[:, : 2 * height - 1], jnp.concatenate([target[0], later[0]], axis=1)])
    patches = cut_patches(extended, own_regions[:, 0], own_regions[:, 1], height)
    flat_recv = received.reshape((strips * capacity,) + received.shape[2:])
    patch_noise = jnp.take(flat_recv, own_regions[:, 2] * capacity + own_pairs, axis=0)
    in_use = jnp.ones((per_strip,), jnp.float32)
    losses, gradients = kernel_blocks(
        patches[:, 0], patches[:, 1], patch_noise, own_regions[:, 3], in_use, weights
    )
    owner_hot = (own_regions[:, 2][:, None] == jnp.arange(strips, dtype=jnp.int32)[None, :])
    owner_part = jnp.sum(owner_hot.astype(jnp.float32) * losses[:, None], axis=0)
    sample_hot = (jnp.arange(sample_count, dtype=jnp.int32) == sample_index).astype(jnp.float32)
    owner_table = sample_hot[:, None] * owner_part[None, :]
    pieces = (gradients[0], gradients[1], gradients[2], gradients[3], owner_table)
    flat = jnp.concatenate([piece.reshape(-1) for piece in pieces])
    summed = exchange_sum(flat, reduce_steps())
    results = []
    offset = 0
    for piece in pieces:
        results.append(summed[offset : offset + piece.size].reshape(piece.shape))
        offset += piece.size
    table = results[4]
    owner_total = lax.dynamic_slice(table, (sample_index, strip_index), (1, 1))
    return (mean_strip[None], owner_total, results[0], results[1], results[2], results[3])


def solution(mesh):
    placed = (
        P(("segment", "dp"), None, "rows", None),
        P(("segment", "dp"), None, "rows", None),
        P(("segment", "dp"), "rows", None, None, None),
        P(("segment", "dp"), None, None, None),
        P(),
        P(),
        P(),
        P(),
        P(),
        P(),
    )
    return jax.shard_map(
        per_device,
        mesh=mesh,
        in_specs=placed,
        out_specs=(
            P(("segment", "dp"), None, "rows", None),
            P(("segment", "dp"), "rows"),
            P(),
            P(),
            P(),
            P(),
        ),
        check_vma=False,
    )
```
